32 devices in a mesh: ctx: 8 (over z, x), fsdp: 4 (over y, core).
Axes of the slice: x: 2, y: 2, z: 4, core: 2. Of those that a mesh axis runs over, the one named last changes fastest.
Arguments:
- block_in: bfloat16 [4, 2048, 1024], P('fsdp', 'ctx'), may hold values from -6 to 6
- out_grad: bfloat16 [4, 2048, 1024], P('fsdp', 'ctx'), may hold values from -6 to 6
- w_query: bfloat16 [1024, 1024], P('fsdp'), may hold values from -0.1875 to 0.1875
- w_key: bfloat16 [1024, 1024], P('fsdp'), may hold values from -0.1875 to 0.1875
- w_value: bfloat16 [1024, 1024], P('fsdp'), may hold values from -0.1875 to 0.1875
- w_out: bfloat16 [1024, 1024], P('fsdp'), may hold values from -0.1875 to 0.1875
- norm_one: float32 [1024], replicated, may hold values from 0.25 to 1.75
- norm_two: float32 [1024], replicated, may hold values from 0.25 to 1.75
- w_gate: bfloat16 [1024, 2816], P('fsdp'), may hold values from -0.1875 to 0.1875
- w_up: bfloat16 [1024, 2816], P('fsdp'), may hold values from -0.1875 to 0.1875
- w_down: bfloat16 [2816, 1024], P('fsdp'), may hold values from -0.109375 to 0.109375
- norm_three: float32 [1024], replicated, may hold values from 0.25 to 1.75
- norm_four: float32 [1024], replicated, may hold values from 0.25 to 1.75
- prompt_len: int32 [4], replicated, may hold values from 512 to 1024, as said below
- cont_len: int32 [4, 2], replicated, may hold values from 257 to 512, as said below
- group_ids: int32 [4], replicated, may hold values from 0 to 3, each once
- cont_ids: int32 [4, 2], replicated, may hold values from 0 to 1, each once within a row
Outputs:
- block_out: bfloat16 [4, 2048, 1024], P('fsdp', 'ctx')
- in_grad: float32 [4, 2048, 1024], P('fsdp', 'ctx')
- grad_query: float32 [1024, 1024], P('fsdp')
- grad_key: float32 [1024, 1024], P('fsdp')
- grad_value: float32 [1024, 1024], P('fsdp')
- grad_out: float32 [1024, 1024], P('fsdp')
- grad_norm_one: float32 [1024], replicated
- grad_norm_two: float32 [1024], replicated
- grad_gate: float32 [1024, 2816], P('fsdp')
- grad_up: float32 [1024, 2816], P('fsdp')
- grad_down: float32 [2816, 1024], P('fsdp')
- grad_norm_three: float32 [1024], replicated
- grad_norm_four: float32 [1024], replicated
The draws below stay inside these ranges and needn't reach their ends.
Inputs may be any that keep to these rules, and one draw needn't show every extreme that they name: `prompt_len`: in every draw some group's prompt has exactly 1024 tokens. `cont_len`: every group has a continuation of exactly 512 tokens. `group_ids`: A permutation of the groups. `cont_ids`: each row is a permutation of the continuation numbers.
All inputs are finite; a program needn't handle non-finite values.
Results may differ from the reference program's by a relative error of at most 0.023.
Values may be sent and summed in bfloat16 or wider, within the bound.
No kernel may reach another device: no remote copies, remote signals or barrier semaphores. Data moves between devices by JAX's collectives and lax.ppermute only.
A program may use at most 192 MiB of HBM per device.

```python
import math
import jax
import jax.numpy as jnp
from jax import lax

D = 1024
HEADS = 8
HEAD = 128
FF = 2816
CONT = 512
KC = 2
PROMPT = 1024
GTOK = 2048
GROUPS = 4


def draw_prompt_len(key, part):
    len_key, full_key = jax.random.split(key)
    lengths = jax.random.randint(len_key, (GROUPS,), PROMPT // 2, PROMPT + 1)
    full_slot = jax.random.randint(full_key, (), 0, GROUPS)
    return jnp.where(jnp.arange(GROUPS) == full_slot, PROMPT, lengths).astype(jnp.int32)


def draw_cont_len(key, part):
    len_key, full_key = jax.random.split(key)
    lengths = jax.random.randint(len_key, (GROUPS, KC), CONT // 2 + 1, CONT + 1)
    full_slot = jax.random.randint(full_key, (GROUPS, 1), 0, KC)
    return jnp.where(jnp.arange(KC)[None, :] == full_slot, CONT, lengths).astype(jnp.int32)


def raised(drawn, own_key, source, target, blocks, factor):
    owner, partner = [(jnp.arange(drawn.shape[dim]) // (drawn.shape[dim] // blocks)).reshape([-1 if axis == dim else 1 for axis in range(drawn.ndim)]) for dim in (source, target)]
    chosen = jax.random.permutation(own_key, blocks)[partner]
    strong = (owner == chosen) | (owner == (partner + blocks // 2) % blocks)
    return jnp.where(strong, factor * drawn, drawn)


def block_scale(rng, shape, shards, smallest, largest):
    factor_of = 1.0
    for dim, blocks in shards:
        draws = jax.random.uniform(jax.random.fold_in(jax.random.fold_in(rng, 6), dim), (blocks,), jnp.float32, smallest / len(shards), largest / len(shards))
        factor_of = factor_of * jnp.repeat(jnp.exp(draws), shape[dim] // blocks).reshape((-1,) + (1,) * (len(shape) - 1 - dim))
    return factor_of


def bell_draw(own_key, shape, deviation, limit, shards=(), kind=jnp.bfloat16):
    drawn = jax.random.normal(own_key, shape, jnp.float32) * deviation
    if len(shards) > 0:
        drawn = block_scale(own_key, shape, shards, -0.22, 0.18) * drawn
    return jnp.clip(drawn, min=-limit, max=limit).astype(kind)


def gaussian_with(stream_key, shape, deviation, reach, pieces, heavy, kind=jnp.bfloat16):
    entries = deviation * jax.random.normal(stream_key, shape, jnp.float32)
    if pieces:
        entries = entries * block_scale(stream_key, shape, pieces, -0.22, 0.18)
    return jnp.clip(raised(entries, jax.random.fold_in(stream_key, 3), *heavy), -reach, reach).astype(kind)


def setup_inputs(seed: int = 0) -> dict:
    key_of = jax.random.split(jax.random.key(seed), 18)
    block_in = gaussian_with(key_of[0], (GROUPS, GTOK, D), 1.0, 6.0, ((0, 4), (1, 8)), (0, 2, 4, 2.0))
    out_grad = bell_draw(key_of[1], (GROUPS, GTOK, D), 1.0, 6.0, ((0, 4), (1, 8)))
    w_query = bell_draw(key_of[2], (D, D), D ** -0.5, 0.1875, ((0, 4),))
    w_key = bell_draw(key_of[3], (D, D), D ** -0.5, 0.1875, ((0, 4),))
    w_value = bell_draw(key_of[4], (D, D), D ** -0.5, 0.1875, ((0, 4),))
    w_out = bell_draw(key_of[5], (D, D), D ** -0.5, 0.1875, ((0, 4),))
    norm_one = jnp.clip(1.0 + 0.15 * jax.random.normal(key_of[6], (D,), jnp.float32), 0.25, 1.75)
    norm_two = jnp.clip(1.0 + 0.15 * jax.random.normal(key_of[7], (D,), jnp.float32), 0.25, 1.75)
    w_gate = bell_draw(key_of[8], (D, FF), D ** -0.5, 0.1875, ((0, 4),))
    w_up = bell_draw(key_of[9], (D, FF), D ** -0.5, 0.1875, ((0, 4),))
    w_down = bell_draw(key_of[10], (FF, D), FF ** -0.5, 0.109375, ((0, 4),))
    norm_three = jnp.clip(1.0 + 0.15 * jax.random.normal(key_of[11], (D,), jnp.float32), 0.25, 1.75)
    norm_four = jnp.clip(1.0 + 0.15 * jax.random.normal(key_of[12], (D,), jnp.float32), 0.25, 1.75)
    prompt_len = draw_prompt_len(jax.random.fold_in(key_of[17], 71), 0)
    cont_len = draw_cont_len(jax.random.fold_in(key_of[17], 71), 0)
    group_ids = jax.random.permutation(key_of[15], GROUPS).astype(jnp.int32)
    cont_ids = jax.vmap(lambda own: jax.random.permutation(own, KC))(jax.random.split(key_of[16], GROUPS)).reshape((GROUPS, KC)).astype(jnp.int32)
    return {"block_in": block_in, "out_grad": out_grad, "w_query": w_query, "w_key": w_key, "w_value": w_value, "w_out": w_out, "norm_one": norm_one, "norm_two": norm_two, "w_gate": w_gate, "w_up": w_up, "w_down": w_down, "norm_three": norm_three, "norm_four": norm_four, "prompt_len": prompt_len, "cont_len": cont_len, "group_ids": group_ids, "cont_ids": cont_ids}


@jax.custom_vjp
def low(v):
    return lax.optimization_barrier(v.astype(jnp.bfloat16)).astype(jnp.float32)

@jax.custom_vjp
def low_back(v):
    return v

def low_keep(v):
    return (low(v), None)

def low_pass(kept, grad):
    return (grad,)

def back_keep(v):
    return (v, None)

def back_low(kept, grad):
    return (low(grad),)
low.defvjp(low_keep, low_pass)
low_back.defvjp(back_keep, back_low)
highest = lax.Precision.HIGHEST
eps_norm = 1e-06
rope_base = 50000.0
masked_out = -1e+30

def rms_norm(values, gain_vec):
    return values * lax.rsqrt(lax.optimization_barrier(jnp.mean(values * values, axis=-1, keepdims=True)) + eps_norm) * gain_vec

def rotate(values, position, turn_sign):
    seq_len = values.shape[0]
    half_size = HEAD // 2
    split_heads = values.reshape(seq_len, -1, HEAD)
    frequencies = rope_base ** (-2.0 * jnp.arange(half_size, dtype=jnp.float32) / HEAD)
    angles = position.astype(jnp.float32)[:, None] * frequencies[None, :]
    cosine = jnp.concatenate([jnp.cos(angles), jnp.cos(angles)], axis=-1)[:, None, :]
    sine_part = turn_sign * jnp.concatenate([jnp.sin(angles), jnp.sin(angles)], axis=-1)[:, None, :]
    turned = jnp.concatenate([-split_heads[..., half_size:], split_heads[..., :half_size]], axis=-1)
    return (split_heads * cosine + turned * sine_part).reshape(seq_len, -1)

def token_info(slot_index, prompt, prompt_size, slot_lens):
    in_cont = slot_index >= prompt
    rel_index = jnp.maximum(slot_index - prompt, 0)
    slot_of = jnp.where(in_cont, rel_index // CONT, -1)
    offset = rel_index % CONT
    slot_range = jnp.arange(slot_lens.shape[0], dtype=jnp.int32)
    slot_len = lax.optimization_barrier(jnp.sum(jnp.where(slot_of[:, None] == slot_range[None, :], slot_lens[None, :], 0), axis=1))
    token_valid = jnp.where(in_cont, offset < slot_len, slot_index < prompt_size)
    position = jnp.where(in_cont, prompt_size + offset, slot_index)
    return (token_valid, slot_of, position)

def group_layer(params, tokens, prompt_size, slot_lens):
    w_query, w_key, w_value, w_out, norm_one, norm_two, w_gate, w_up, w_down, norm_three, norm_four = params
    slot_index = jnp.arange(GTOK, dtype=jnp.int32)
    token_valid, slot_of, position = token_info(slot_index, PROMPT, prompt_size, slot_lens)
    normed = low(rms_norm(tokens, norm_one))
    queries = low(rotate(low_back(jnp.dot(normed, w_query, precision=highest)), position, 1.0))
    keys = low(rotate(low_back(jnp.dot(normed, w_key, precision=highest)), position, 1.0))
    values = low(low_back(jnp.dot(normed, w_value, precision=highest)))
    key_heads = keys.reshape(GTOK, HEADS, HEAD)
    value_heads = values.reshape(GTOK, HEADS, HEAD)
    query_block = math.gcd(GTOK, 512)
    score_scale = 1.0 / math.sqrt(HEAD)

    def attend(first_row):
        query_rows = lax.dynamic_slice_in_dim(queries, first_row, query_block, 0).reshape(query_block, HEADS, HEAD)
        query_index = first_row + jnp.arange(query_block, dtype=jnp.int32)
        query_valid = lax.dynamic_slice_in_dim(token_valid, first_row, query_block, 0)
        query_slot = lax.dynamic_slice_in_dim(slot_of, first_row, query_block, 0)
        allowed = query_valid[:, None] & token_valid[None, :] & (slot_index[None, :] <= query_index[:, None]) & ((slot_index[None, :] < PROMPT) | (slot_of[None, :] == query_slot[:, None]))
        scores = low_back(jnp.einsum('qhd,khd->hqk', query_rows, key_heads, precision=highest) * score_scale)
        scores = jnp.where(allowed[None], scores, masked_out)
        row_top = lax.optimization_barrier(jnp.max(scores, axis=-1, keepdims=True))
        exp_scores = jnp.exp(scores - row_top)
        attn_probs = low(exp_scores / lax.optimization_barrier(jnp.sum(exp_scores, axis=-1, keepdims=True)))
        mixture = jnp.einsum('hqk,khd->qhd', attn_probs, value_heads, precision=highest).reshape(query_block, HEADS * HEAD)
        return mixture * query_valid[:, None].astype(jnp.float32)
    starts = jnp.arange(GTOK // query_block, dtype=jnp.int32) * query_block
    attended = lax.map(jax.checkpoint(attend), starts).reshape(GTOK, HEADS * HEAD)
    attended = low(low_back(attended))
    branch = low_back(jnp.dot(attended, w_out, precision=highest))
    middle = tokens + rms_norm(branch, norm_two)
    ff_input = low(rms_norm(middle, norm_three))
    gate_pre = low_back(jnp.dot(ff_input, w_gate, precision=highest))
    upward = low_back(jnp.dot(ff_input, w_up, precision=highest))
    hidden = low(jax.nn.silu(gate_pre) * upward)
    ff_out = low_back(jnp.dot(hidden, w_down, precision=highest))
    return middle + rms_norm(ff_out, norm_four)

def reference(block_in, out_grad, w_query, w_key, w_value, w_out, norm_one, norm_two, w_gate, w_up, w_down, norm_three, norm_four, prompt_len, cont_len, group_ids, cont_ids):
    group_range = jnp.arange(GROUPS, dtype=jnp.int32)
    own_group = group_ids[:, None] == group_range[None, :]
    prompt_lens = lax.optimization_barrier(jnp.sum(jnp.where(own_group, prompt_len[None, :], 0), axis=1))
    group_lens = lax.optimization_barrier(jnp.sum(jnp.where(own_group[:, :, None], cont_len[None, :, :], 0), axis=1))
    slot_lens = jnp.take_along_axis(group_lens, cont_ids, axis=1)
    weights = tuple((weight.astype(jnp.float32) for weight in (w_query, w_key, w_value, w_out, norm_one, norm_two, w_gate, w_up, w_down, norm_three, norm_four)))

    def forward(tokens, *params):

        def one_group(inputs):
            return group_layer(params, inputs[0], inputs[1], inputs[2])
        return lax.map(jax.checkpoint(one_group), (tokens, prompt_lens, slot_lens))
    result, pullback = jax.vjp(forward, block_in.astype(jnp.float32), *weights)
    gradients = pullback(out_grad.astype(jnp.float32))
    return (result.astype(jnp.bfloat16), gradients[0], gradients[1], gradients[2], gradients[3], gradients[4], gradients[5], gradients[6], gradients[7], gradients[8], gradients[9], gradients[10], gradients[11])
```

```python
import functools
import math

import jax
import jax.numpy as jnp
from jax import lax
from jax.experimental import pallas as pl
from jax.experimental.pallas import tpu as pltpu
from jax.sharding import PartitionSpec as P

HEAD = 128
P_DEV = 128
CONT = 512
LOG2E = 1.4426950408889634

eps_norm = 1e-06
rope_base = 50000.0
masked_out = -1e30

bf16 = jnp.bfloat16
f32 = jnp.float32

def rms_norm(values, gain_vec):
    inverse = lax.rsqrt(jnp.mean(values * values, axis=-1, keepdims=True) + eps_norm)
    return (values * inverse * gain_vec, inverse)


def norm_back(values, inverse, gain_vec, upstream):
    weighted = upstream * gain_vec
    inner_mean = jnp.mean(values * weighted, axis=-1, keepdims=True)
    value_grad = inverse * weighted - values * inverse * inverse * inverse * inner_mean
    return (value_grad, jnp.sum(upstream * values * inverse, axis=0))


def rotate(values, position, turn_sign):
    seq_len = values.shape[0]
    half_size = HEAD // 2
    split_heads = values.reshape(seq_len, -1, HEAD)
    frequencies = rope_base ** (-2.0 * jnp.arange(half_size, dtype=jnp.float32) / HEAD)
    angles = position.astype(jnp.float32)[:, None] * frequencies[None, :]
    cosine = jnp.concatenate([jnp.cos(angles), jnp.cos(angles)], axis=-1)[:, None, :]
    sine_part = turn_sign * jnp.concatenate([jnp.sin(angles), jnp.sin(angles)], axis=-1)[:, None, :]
    turned = jnp.concatenate([-split_heads[..., half_size:], split_heads[..., :half_size]], axis=-1)
    return (split_heads * cosine + turned * sine_part).reshape(seq_len, -1)


def token_info(slot_index, prompt, prompt_size, slot_lens):
    in_cont = slot_index >= prompt
    rel_index = jnp.maximum(slot_index - prompt, 0)
    slot_of = jnp.where(in_cont, rel_index // CONT, -1)
    offset = rel_index % CONT
    slot_range = jnp.arange(slot_lens.shape[0], dtype=jnp.int32)
    slot_len = jnp.sum(
        jnp.where(slot_of[:, None] == slot_range[None, :], slot_lens[None, :], 0), axis=1
    )
    token_valid = jnp.where(in_cont, offset < slot_len, slot_index < prompt_size)
    position = jnp.where(in_cont, prompt_size + offset, slot_index)
    return (token_valid, slot_of, position)


def cross_dot(operand, partner):
    return lax.dot_general(
        operand, partner, (((0,), (0,)), ((), ())), preferred_element_type=jnp.float32
    )


def back_dot(operand, partner):
    return lax.dot_general(
        operand, partner, (((1,), (1,)), ((), ())), preferred_element_type=jnp.float32
    )


def keep_same(state):
    return state


def shards(
    block_in,
    out_grad,
    w_query,
    w_key,
    w_value,
    w_out,
    norm_one,
    norm_two,
    w_gate,
    w_up,
    w_down,
    norm_three,
    norm_four,
    prompt_len,
    cont_len,
    group_ids,
    cont_ids,
):
    local_rows = block_in.shape[1]
    model_width = block_in.shape[2]
    ff_width = w_gate.shape[1]
    ctx_size = lax.axis_size("ctx")
    group_rows = local_rows * ctx_size
    prompt = P_DEV * ctx_size
    head_count = model_width // HEAD
    score_scale = 1.0 / math.sqrt(HEAD)
    row_index = lax.axis_index("fsdp")
    groups = group_ids.shape[0]
    slot_count = cont_ids.shape[1]
    group_range = jnp.arange(groups, dtype=jnp.int32)
    own_group = jnp.sum(jnp.where(group_range == row_index, group_ids, 0))
    own_prompt = jnp.sum(jnp.where(group_range == own_group, prompt_len, 0))
    own_lens = jnp.sum(jnp.where((group_range == own_group)[:, None], cont_len, 0), axis=0)
    own_ids = jnp.sum(jnp.where((group_range == row_index)[:, None], cont_ids, 0), axis=0)
    slot_range = jnp.arange(slot_count, dtype=jnp.int32)
    slot_lens = jnp.sum(
        jnp.where(own_ids[:, None] == slot_range[None, :], own_lens[None, :], 0), axis=1
    )
    query_index = lax.axis_index("ctx") * local_rows + jnp.arange(local_rows, dtype=jnp.int32)
    key_index = jnp.arange(group_rows, dtype=jnp.int32)
    query_valid, query_slot, position = token_info(query_index, prompt, own_prompt, slot_lens)
    key_valid, key_slot, unused_pos = token_info(key_index, prompt, own_prompt, slot_lens)
    tokens = block_in[0].astype(jnp.float32)
    full_query, full_key, full_value, full_out = (
        lax.all_gather(w_query, "fsdp", axis=0, tiled=True),
        lax.all_gather(w_key, "fsdp", axis=0, tiled=True),
        lax.all_gather(w_value, "fsdp", axis=0, tiled=True),
        lax.all_gather(w_out, "fsdp", axis=0, tiled=True),
    )
    normed_full, inverse_one = rms_norm(tokens, norm_one)
    normed = normed_full.astype(jnp.bfloat16)
    queries = rotate(
        jnp.dot(normed, full_query, preferred_element_type=jnp.float32), position, 1.0
    ).astype(jnp.bfloat16)
    keys_local = rotate(
        jnp.dot(normed, full_key, preferred_element_type=jnp.float32), position, 1.0
    ).astype(jnp.bfloat16)
    values_local = jnp.dot(normed, full_value, preferred_element_type=jnp.float32).astype(
        jnp.bfloat16
    )
    all_keys, all_values = (
        lax.all_gather(keys_local, "ctx", axis=0, tiled=True),
        lax.all_gather(values_local, "ctx", axis=0, tiled=True),
    )
    key_block = math.gcd(group_rows, 512)
    block_count = group_rows // key_block
    blocks_in = (
        all_keys.reshape(block_count, key_block, head_count, HEAD),
        all_values.reshape(block_count, key_block, head_count, HEAD),
        key_valid.reshape(block_count, key_block),
        key_slot.reshape(block_count, key_block),
        key_index.reshape(block_count, key_block),
    )
    query_heads = queries.reshape(local_rows, head_count, HEAD)

    def mask_of(inputs):
        key_ids = inputs[4]
        return (
            query_valid[:, None]
            & inputs[2][None, :]
            & (key_ids[None, :] <= query_index[:, None])
            & ((key_ids[None, :] < prompt) | (inputs[3][None, :] == query_slot[:, None]))
        )

    def raw_scores(inputs):
        return (
            jnp.einsum("qhd,khd->hqk", query_heads, inputs[0], preferred_element_type=jnp.float32)
            * score_scale
        )

    def running(state_in, inputs):
        allowed = mask_of(inputs)

        def running_visit(state):
            row_top, exp_total = state
            scores = jnp.where(allowed[None], raw_scores(inputs), masked_out)
            new_top = jnp.maximum(row_top, jnp.max(scores, axis=-1, keepdims=True))
            exp_total = exp_total * jnp.exp(row_top - new_top) + jnp.sum(
                jnp.where(allowed[None], jnp.exp(scores - new_top), 0.0), axis=-1, keepdims=True
            )
            return (new_top, exp_total)

        return (lax.cond(jnp.any(allowed), running_visit, keep_same, state_in), None)

    start_top = jnp.full((head_count, local_rows, 1), -jnp.inf, jnp.float32)
    start_total = jnp.zeros((head_count, local_rows, 1), jnp.float32)
    (row_top, exp_total), unused = lax.scan(running, (start_top, start_total), blocks_in)
    has_keys = exp_total > 0.0
    log_total = jnp.where(has_keys, row_top + jnp.log(jnp.where(has_keys, exp_total, 1.0)), 0.0)

    def probs_of(inputs, allowed):
        return jnp.where(allowed[None], jnp.exp(raw_scores(inputs) - log_total), 0.0)

    def mix_step(accumulated, inputs):
        allowed = mask_of(inputs)

        def mix_visit(total):
            attn_probs = probs_of(inputs, allowed).astype(jnp.bfloat16)
            return total + jnp.einsum(
                "hqk,khd->qhd", attn_probs, inputs[1], preferred_element_type=jnp.float32
            )

        return (lax.cond(jnp.any(allowed), mix_visit, keep_same, accumulated), None)

    mixture, unused = lax.scan(
        mix_step, jnp.zeros((local_rows, head_count, HEAD), jnp.float32), blocks_in
    )
    valid_col = query_valid[:, None].astype(jnp.float32)
    attended = (mixture.reshape(local_rows, model_width) * valid_col).astype(jnp.bfloat16)
    branch = jnp.dot(attended, full_out, preferred_element_type=jnp.float32)
    branch_normed, inverse_two = rms_norm(branch, norm_two)
    middle = tokens + branch_normed
    full_gate, full_up, full_down = (
        lax.all_gather(w_gate, "fsdp", axis=0, tiled=True),
        lax.all_gather(w_up, "fsdp", axis=0, tiled=True),
        lax.all_gather(w_down, "fsdp", axis=0, tiled=True),
    )
    ff_normed, inverse_three = rms_norm(middle, norm_three)
    ff_input = ff_normed.astype(jnp.bfloat16)
    gate_pre = jnp.dot(ff_input, full_gate, preferred_element_type=jnp.float32)
    upward = jnp.dot(ff_input, full_up, preferred_element_type=jnp.float32)
    gate_sig = jax.nn.sigmoid(gate_pre)
    swish_out = gate_pre * gate_sig
    hidden = (swish_out * upward).astype(jnp.bfloat16)
    ff_out = jnp.dot(hidden, full_down, preferred_element_type=jnp.float32)
    out_normed, inverse_four = rms_norm(ff_out, norm_four)
    result = middle + out_normed
    upstream = out_grad[0].astype(jnp.float32)
    ff_out_full, grad_norm_four = norm_back(ff_out, inverse_four, norm_four, upstream)
    ff_out_grad = ff_out_full.astype(jnp.bfloat16)
    hidden_grad = back_dot(ff_out_grad, full_down)
    up_grad = (hidden_grad * swish_out).astype(jnp.bfloat16)
    gate_grad = (hidden_grad * upward * gate_sig * (1.0 + gate_pre * (1.0 - gate_sig))).astype(
        jnp.bfloat16
    )
    ff_in_grad = back_dot(gate_grad, full_gate) + back_dot(up_grad, full_up)
    middle_part, grad_norm_three = norm_back(middle, inverse_three, norm_three, ff_in_grad)
    middle_grad = upstream + middle_part
    branch_full, grad_norm_two = norm_back(branch, inverse_two, norm_two, middle_grad)
    branch_grad = branch_full.astype(jnp.bfloat16)
    attended_grad = back_dot(branch_grad, full_out).astype(jnp.bfloat16) * valid_col.astype(
        jnp.bfloat16
    )
    grad_heads = attended_grad.reshape(local_rows, head_count, HEAD)

    def delta_step(accumulated, inputs):
        allowed = mask_of(inputs)

        def delta_visit(total):
            attn_probs = probs_of(inputs, allowed)
            prob_grad = jnp.einsum(
                "qhd,khd->hqk", grad_heads, inputs[1], preferred_element_type=jnp.float32
            )
            return total + jnp.sum(attn_probs * prob_grad, axis=-1, keepdims=True)

        return (lax.cond(jnp.any(allowed), delta_visit, keep_same, accumulated), None)

    row_delta, unused = lax.scan(
        delta_step, jnp.zeros((head_count, local_rows, 1), jnp.float32), blocks_in
    )
    zero_part = jnp.zeros((key_block, head_count, HEAD), jnp.float32)

    def grad_step(accumulated, inputs):
        allowed = mask_of(inputs)

        def grad_visit(total):
            attn_probs = probs_of(inputs, allowed)
            prob_grad = jnp.einsum(
                "qhd,khd->hqk", grad_heads, inputs[1], preferred_element_type=jnp.float32
            )
            score_grad = (attn_probs * (prob_grad - row_delta)).astype(jnp.bfloat16)
            total = total + jnp.einsum(
                "hqk,khd->qhd", score_grad, inputs[0], preferred_element_type=jnp.float32
            )
            key_part = jnp.einsum(
                "hqk,qhd->khd", score_grad, query_heads, preferred_element_type=jnp.float32
            )
            value_part = jnp.einsum(
                "hqk,qhd->khd",
                attn_probs.astype(jnp.bfloat16),
                grad_heads,
                preferred_element_type=jnp.float32,
            )
            return (total, (key_part, value_part))

        def skip(total):
            return (total, (zero_part, zero_part))

        return lax.cond(jnp.any(allowed), grad_visit, skip, accumulated)

    query_acc, (key_parts, value_parts) = lax.scan(
        grad_step, jnp.zeros((local_rows, head_count, HEAD), jnp.float32), blocks_in
    )
    key_terms = key_parts.reshape(group_rows, model_width) * score_scale
    value_terms = value_parts.reshape(group_rows, model_width)
    key_sum, value_sum = (
        lax.psum_scatter(
            key_terms.astype(jnp.bfloat16), "ctx", scatter_dimension=0, tiled=True
        ).astype(jnp.float32),
        lax.psum_scatter(
            value_terms.astype(jnp.bfloat16), "ctx", scatter_dimension=0, tiled=True
        ).astype(jnp.float32),
    )
    query_grad = rotate(
        query_acc.reshape(local_rows, model_width) * score_scale, position, -1.0
    ).astype(jnp.bfloat16)
    key_grad = rotate(key_sum, position, -1.0).astype(jnp.bfloat16)
    value_grad = value_sum.astype(jnp.bfloat16)
    normed_grad = (
        back_dot(query_grad, full_query)
        + back_dot(key_grad, full_key)
        + back_dot(value_grad, full_value)
    )
    input_part, grad_norm_one = norm_back(tokens, inverse_one, norm_one, normed_grad)
    input_grad = middle_grad + input_part
    wide_pairs = (
        (normed, query_grad),
        (normed, key_grad),
        (normed, value_grad),
        (attended, branch_grad),
        (ff_input, gate_grad),
        (ff_input, up_grad),
    )

    def wide_term(selector):
        return jnp.concatenate(
            [cross_dot(selector(operand), partner) for operand, partner in wide_pairs], axis=1
        )

    wide_local = lax.psum_scatter(
        wide_term(lambda operand: operand).astype(jnp.bfloat16),
        "fsdp",
        scatter_dimension=0,
        tiled=True,
    )
    ff_local = lax.psum_scatter(
        cross_dot((lambda operand: operand)(hidden), ff_out_grad).astype(jnp.bfloat16),
        "fsdp",
        scatter_dimension=0,
        tiled=True,
    )
    wide_sum, ff_sum = (
        lax.psum(wide_local, "ctx").astype(jnp.float32),
        lax.psum(ff_local, "ctx").astype(jnp.float32),
    )
    gain_sums = lax.psum(
        jnp.stack([grad_norm_one, grad_norm_two, grad_norm_three, grad_norm_four]), ("ctx", "fsdp")
    )
    edge_two = 2 * model_width
    edge_three = 3 * model_width
    edge_four = 4 * model_width
    edge_five = 4 * model_width + ff_width
    return (
        result.astype(jnp.bfloat16)[None],
        input_grad[None],
        wide_sum[:, :model_width],
        wide_sum[:, model_width:edge_two],
        wide_sum[:, edge_two:edge_three],
        wide_sum[:, edge_three:edge_four],
        gain_sums[0],
        gain_sums[1],
        wide_sum[:, edge_four:edge_five],
        wide_sum[:, edge_five:],
        ff_sum,
        gain_sums[2],
        gain_sums[3],
    )


IN_SPECS = (
    (P("fsdp", "ctx", None),) * 2
    + (P("fsdp", None),) * 4
    + (P(), P())
    + (P("fsdp", None),) * 3
    + (P(),) * 6
)
OUT_SPECS = (
    (P("fsdp", "ctx", None),) * 2
    + (P("fsdp", None),) * 4
    + (P(), P())
    + (P("fsdp", None),) * 3
    + (P(), P())
)


REL = (0, 2, 1, 3)
MIB = 1 << 20


def core_swap(values):
    return lax.ppermute(values, "fsdp", [(i, i ^ 1) for i in range(4)])


def y_swap(values):
    return lax.ppermute(values, "fsdp", [(i, i ^ 2) for i in range(4)])


def gather_rows(own):
    across = y_swap(own)
    beside = core_swap(own)
    corner = core_swap(across)
    return jnp.stack([own, across, beside, corner])


def exchange_sums(keep, send):
    received = core_swap(send)
    onward = (keep[1].astype(f32) + received[1].astype(f32)).astype(bf16)
    return keep, received, y_swap(onward)


def params(limit_mib, *semantics):
    return pltpu.CompilerParams(
        dimension_semantics=semantics or None, vmem_limit_bytes=limit_mib * MIB
    )


def whole(shape):
    return pl.BlockSpec(shape, lambda *_: (0,) * len(shape))


def place(shape):
    return pl.BlockSpec((1,) + shape, lambda t: (t,) + (0,) * len(shape))


def first_place(shape):
    return pl.BlockSpec((1,) + shape, lambda *_: (0,) * (1 + len(shape)))


def kept(shape):
    return pl.BlockSpec((1,) + shape, lambda t: (jnp.minimum(t, 1),) + (0,) * len(shape))


def sent(shape):
    return pl.BlockSpec((1,) + shape, lambda t: (jnp.maximum(t - 2, 0),) + (0,) * len(shape))


def put_partial(step, partial, keep_ref, send_ref):
    rounded = partial.astype(bf16)

    @pl.when(step < 2)
    def _():
        keep_ref[0] = rounded

    @pl.when(step >= 2)
    def _():
        send_ref[0] = rounded


def dot_nn(a, b):
    return lax.dot_general(a, b, (((1,), (0,)), ((), ())), preferred_element_type=f32)


def dot_nt(a, b):
    return lax.dot_general(a, b, (((1,), (1,)), ((), ())), preferred_element_type=f32)


def dot_tn(a, b):
    return lax.dot_general(a, b, (((0,), (0,)), ((), ())), preferred_element_type=f32)


def inverse_rms(values):
    return lax.rsqrt(jnp.mean(values * values, axis=-1, keepdims=True) + eps_norm)


def turn(values, cosine, sine):
    return values * cosine + pltpu.roll(values, HEAD // 2, 1) * sine


def project_kernel(x_ref, gain_ref, w_ref, cos_ref, sin_ref, out_ref):
    x = x_ref[0].astype(f32)
    normed = (x * inverse_rms(x) * gain_ref[...]).astype(bf16)
    product = dot_nn(normed, w_ref[...])
    heads = out_ref.shape[0]
    for kind in range(3):
        for head in range(heads):
            start = (kind * heads + head) * HEAD
            part = product[:, start : start + HEAD]
            if kind < 2:
                part = turn(part, cos_ref[0], sin_ref[0])
            out_ref[head, kind] = part.astype(bf16)


def key_span(chunk, prompt_chunks, cont_chunks):
    in_cont = chunk >= prompt_chunks
    first = jnp.where(
        in_cont, prompt_chunks + (chunk - prompt_chunks) // cont_chunks * cont_chunks, 0
    )
    return first, jnp.where(in_cont, prompt_chunks, 0)


def attend_kernel(
    prompt_chunks, cont_chunks, info_ref, qkv_ref, out_ref, exact_ref, lse_ref
):
    chunk = pl.program_id(0)
    rows = qkv_ref.shape[2]
    scale = LOG2E / math.sqrt(HEAD)
    query = qkv_ref[chunk, 0]
    prompt_size = info_ref[0]
    first, ahead = key_span(chunk, prompt_chunks, cont_chunks)
    key_place = lax.broadcasted_iota(jnp.int32, (rows, rows), 0)
    query_place = lax.broadcasted_iota(jnp.int32, (rows, rows), 1)

    def visit(key_chunk, bias, state):
        top, total, mixed = state
        scores = dot_nt(qkv_ref[key_chunk, 1], query) * scale + bias
        new_top = jnp.maximum(top, jnp.max(scores, axis=0, keepdims=True))
        weights = jnp.exp2(scores - new_top)
        shrink = jnp.exp2(top - new_top)
        total = total * shrink + jnp.sum(weights, axis=0, keepdims=True)
        mixed = mixed * shrink + dot_tn(qkv_ref[key_chunk, 2], weights.astype(bf16))
        return new_top, total, mixed

    def prompt_visit(key_chunk, state):
        bias = jnp.where(key_chunk * rows + key_place < prompt_size, 0.0, masked_out)
        return visit(key_chunk, bias, state)

    def own_visit(key_chunk, state):
        return visit(key_chunk, 0.0, state)

    state = (
        jnp.full((1, rows), -1e38, f32),
        jnp.zeros((1, rows), f32),
        jnp.zeros((HEAD, rows), f32),
    )
    state = visit(chunk, jnp.where(key_place <= query_place, 0.0, masked_out), state)
    state = lax.fori_loop(0, ahead, prompt_visit, state)
    top, total, mixed = lax.fori_loop(first, chunk, own_visit, state)
    slot = jnp.maximum(chunk - prompt_chunks, 0) // cont_chunks
    start = jnp.where(
        chunk < prompt_chunks,
        chunk,
        jnp.maximum(chunk - prompt_chunks, 0) % cont_chunks,
    )
    limit = jnp.where(chunk < prompt_chunks, prompt_size, info_ref[1 + slot])
    valid = start * rows + lax.broadcasted_iota(jnp.int32, (1, rows), 1) < limit
    mixed = jnp.where(valid, mixed / total, 0.0)
    settled = mixed.T
    out_ref[chunk] = settled.astype(bf16)
    exact_ref[chunk] = settled
    lse_ref[chunk] = top + jnp.log2(total)


def attend_back_kernel(
    prompt_chunks,
    cont_chunks,
    info_ref,
    qkv_ref,
    grad_ref,
    exact_ref,
    lse_ref,
    cos_ref,
    sin_ref,
    out_ref,
    key_sum,
    value_sum,
):
    chunk = pl.program_id(0)
    chunks = pl.num_programs(0)
    rows = qkv_ref.shape[2]
    scale = LOG2E / math.sqrt(HEAD)
    query = qkv_ref[chunk, 0]
    prompt_size = info_ref[0]
    first, ahead = key_span(chunk, prompt_chunks, cont_chunks)
    key_place = lax.broadcasted_iota(jnp.int32, (rows, rows), 0)
    query_place = lax.broadcasted_iota(jnp.int32, (rows, rows), 1)
    slot = jnp.maximum(chunk - prompt_chunks, 0) // cont_chunks
    start = jnp.where(
        chunk < prompt_chunks,
        chunk,
        jnp.maximum(chunk - prompt_chunks, 0) % cont_chunks,
    )
    limit = jnp.where(chunk < prompt_chunks, prompt_size, info_ref[1 + slot])
    valid = start * rows + lax.broadcasted_iota(jnp.int32, (rows, 1), 0) < limit
    grad_full = jnp.where(valid, grad_ref[chunk].astype(f32), 0.0)
    grad = grad_full.astype(bf16)
    delta = jnp.sum((grad_full * exact_ref[chunk]).T, axis=0, keepdims=True)
    log_total = lse_ref[chunk]

    @pl.when(chunk == 0)
    def _():
        key_sum[...] = jnp.zeros_like(key_sum)
        value_sum[...] = jnp.zeros_like(value_sum)

    def visit(key_chunk, bias, query_sum):
        key = qkv_ref[key_chunk, 1]
        scores = dot_nt(key, query) * scale + bias
        weights = jnp.exp2(scores - log_total)
        weight_grad = dot_nt(qkv_ref[key_chunk, 2], grad)
        score_grad = (weights * (weight_grad - delta)).astype(bf16)
        value_sum[key_chunk] += dot_nn(weights.astype(bf16), grad)
        key_sum[key_chunk] += dot_nn(score_grad, query)
        return query_sum + dot_tn(key, score_grad)

    def prompt_visit(key_chunk, query_sum):
        bias = jnp.where(key_chunk * rows + key_place < prompt_size, 0.0, masked_out)
        return visit(key_chunk, bias, query_sum)

    def own_visit(key_chunk, query_sum):
        return visit(key_chunk, 0.0, query_sum)

    query_sum = visit(
        chunk,
        jnp.where(key_place <= query_place, 0.0, masked_out),
        jnp.zeros((HEAD, rows), f32),
    )
    query_sum = lax.fori_loop(0, ahead, prompt_visit, query_sum)
    query_sum = lax.fori_loop(first, chunk, own_visit, query_sum)
    back = 1.0 / math.sqrt(HEAD)
    out_ref[chunk, 0] = turn(query_sum.T * back, cos_ref[chunk], -sin_ref[chunk]).astype(bf16)

    @pl.when(chunk == chunks - 1)
    def _():
        @pl.loop(0, chunks)
        def _(key_chunk):
            out_ref[key_chunk, 1] = turn(
                key_sum[key_chunk] * back, cos_ref[key_chunk], -sin_ref[key_chunk]
            ).astype(bf16)
            out_ref[key_chunk, 2] = value_sum[key_chunk].astype(bf16)


def mix_out_kernel(heads_ref, w_ref, keep_ref, send_ref):
    step = pl.program_id(0)
    both = jnp.concatenate([heads_ref[j] for j in range(heads_ref.shape[0])], axis=1)
    put_partial(step, dot_nn(both, w_ref[...]), keep_ref, send_ref)


def middle_kernel(
    keep_ref, received_ref, across_ref, x_ref, two_ref, three_ref, branch_ref, middle_ref, input_ref
):
    branch = (
        keep_ref[0].astype(f32) + received_ref[0].astype(f32) + across_ref[...].astype(f32)
    )
    middle = x_ref[...].astype(f32) + branch * inverse_rms(branch) * two_ref[...]
    branch_ref[...] = branch
    middle_ref[...] = middle
    input_ref[...] = (middle * inverse_rms(middle) * three_ref[...]).astype(bf16)


def ff_kernel(x_ref, gate_ref, up_ref, down_ref, keep_ref, send_ref, slope_ref, swish_ref, hidden_ref):
    step = pl.program_id(0)
    x = x_ref[0]
    gate = dot_nn(x, gate_ref[...])
    upward = dot_nn(x, up_ref[...])
    sigma = 1.0 / (1.0 + jnp.exp(-gate))
    swish = gate * sigma
    hidden = (swish * upward).astype(bf16)
    slope_ref[0] = (upward * sigma * (1.0 + gate * (1.0 - sigma))).astype(bf16)
    swish_ref[0] = swish.astype(bf16)
    hidden_ref[0] = hidden
    put_partial(step, dot_nn(hidden, down_ref[...]), keep_ref, send_ref)


def norm_back_parts(values, gain, upstream):
    inverse = inverse_rms(values)
    weighted = upstream * gain
    inner = jnp.mean(values * weighted, axis=-1, keepdims=True)
    value_grad = inverse * weighted - values * (inverse * inverse * inverse * inner)
    return value_grad, jnp.sum(upstream * values * inverse, axis=0, keepdims=True)


def turnaround_kernel(
    keep_ref, received_ref, across_ref, middle_ref, grad_ref, four_ref, out_ref, back_ref, gain_ref
):
    ff_out = keep_ref[0].astype(f32) + received_ref[0].astype(f32) + across_ref[...].astype(f32)
    out_ref[...] = (middle_ref[...] + ff_out * inverse_rms(ff_out) * four_ref[...]).astype(bf16)
    value_grad, gain = norm_back_parts(ff_out, four_ref[...], grad_ref[...].astype(f32))
    back_ref[...] = value_grad.astype(bf16)
    gain_ref[...] = gain


def ff_back_kernel(
    grad_ref, gate_ref, up_ref, down_ref, slope_ref, swish_ref, keep_ref, send_ref, gate_grad_ref, up_grad_ref
):
    step = pl.program_id(0)
    hidden_grad = dot_nt(grad_ref[0], down_ref[...])
    gate_grad = (hidden_grad * slope_ref[0].astype(f32)).astype(bf16)
    up_grad = (hidden_grad * swish_ref[0].astype(f32)).astype(bf16)
    gate_grad_ref[0] = gate_grad
    up_grad_ref[0] = up_grad
    partial = dot_nt(gate_grad, gate_ref[...]) + dot_nt(up_grad, up_ref[...])
    put_partial(step, partial, keep_ref, send_ref)


def branch_back_kernel(
    keep_ref,
    received_ref,
    across_ref,
    middle_ref,
    branch_ref,
    grad_ref,
    two_ref,
    three_ref,
    middle_grad_ref,
    branch_grad_ref,
    gain_two_ref,
    gain_three_ref,
):
    input_grad = keep_ref[0].astype(f32) + received_ref[0].astype(f32) + across_ref[...].astype(f32)
    middle_part, gain_three_ref[...] = norm_back_parts(middle_ref[...], three_ref[...], input_grad)
    middle_grad = grad_ref[...].astype(f32) + middle_part
    middle_grad_ref[...] = middle_grad
    branch_grad, gain_two_ref[...] = norm_back_parts(branch_ref[...], two_ref[...], middle_grad)
    branch_grad_ref[...] = branch_grad.astype(bf16)


def heads_back_kernel(grad_ref, w_ref, out_ref):
    both = dot_nt(grad_ref[0], w_ref[...]).astype(bf16)
    for head in range(out_ref.shape[0]):
        out_ref[head] = both[:, head * HEAD : (head + 1) * HEAD]


def project_back_kernel(
    pieces_ref, x_ref, gain_ref, w_ref, keep_ref, send_ref, grad_ref, total
):
    step = pl.program_id(0)
    heads = pieces_ref.shape[0]
    pieces = jnp.concatenate(
        [pieces_ref[head, kind] for kind in range(3) for head in range(heads)], axis=1
    )
    put_partial(step, dot_nt(pieces, w_ref[...]), keep_ref, send_ref)
    x = x_ref[0].astype(f32)
    normed = (x * inverse_rms(x) * gain_ref[...]).astype(bf16)
    term = dot_tn(normed, pieces)

    @pl.when(step == 0)
    def _():
        total[...] = term

    @pl.when(step > 0)
    def _():
        total[...] += term

    @pl.when(step == pl.num_programs(0) - 1)
    def _():
        grad_ref[...] = total[...].astype(bf16)


def input_back_kernel(
    keep_ref, received_ref, across_ref, x_ref, middle_grad_ref, one_ref, out_ref, gain_ref
):
    normed_grad = keep_ref[0].astype(f32) + received_ref[0].astype(f32) + across_ref[...].astype(f32)
    part, gain_ref[...] = norm_back_parts(x_ref[...].astype(f32), one_ref[...], normed_grad)
    out_ref[...] = middle_grad_ref[...] + part


def shaped(*shape, kind=bf16):
    return jax.ShapeDtypeStruct(shape, kind)


def rope_tables(position):
    half = HEAD // 2
    frequencies = rope_base ** (-2.0 * jnp.arange(half, dtype=f32) / HEAD)
    angles = position.astype(f32)[..., None] * frequencies
    cosine, sine = jnp.cos(angles), jnp.sin(angles)
    return (
        jnp.concatenate([cosine, cosine], axis=-1),
        jnp.concatenate([-sine, sine], axis=-1),
    )


def cross_dot_low(operand, partner):
    return lax.dot_general(
        operand, partner, (((0,), (0,)), ((), ())), preferred_element_type=f32
    ).astype(bf16)


def pair_shards(
    block_in,
    out_grad,
    w_query,
    w_key,
    w_value,
    w_out,
    norm_one,
    norm_two,
    w_gate,
    w_up,
    w_down,
    norm_three,
    norm_four,
    prompt_len,
    cont_len,
    group_ids,
    cont_ids,
):
    rows, width = block_in.shape[1:]
    ctx_size = lax.axis_size("ctx")
    heads = width // HEAD // 4
    prompt = P_DEV * ctx_size
    prompt_chunks, cont_chunks = prompt // rows, CONT // rows
    ff_part = w_down.shape[0]
    ff_width = w_gate.shape[1]
    my_row = lax.axis_index("fsdp")
    my_chunk = lax.axis_index("ctx")
    groups, slots = cont_ids.shape

    row_of = my_row ^ jnp.array(REL, jnp.int32)
    group_range = jnp.arange(groups, dtype=jnp.int32)
    slot_range = jnp.arange(slots, dtype=jnp.int32)
    pick_row = row_of[:, None] == group_range[None, :]
    group_of = jnp.sum(jnp.where(pick_row, group_ids[None, :], 0), axis=1)
    pick_group = group_of[:, None] == group_range[None, :]
    prompt_of = jnp.sum(jnp.where(pick_group, prompt_len[None, :], 0), axis=1)
    lens_of = jnp.sum(jnp.where(pick_group[:, :, None], cont_len[None], 0), axis=1)
    ids_of = jnp.sum(jnp.where(pick_row[:, :, None], cont_ids[None], 0), axis=1)
    slot_lens = jnp.sum(
        jnp.where(ids_of[:, :, None] == slot_range, lens_of[:, None, :], 0), axis=2
    )
    pick_pair = jnp.arange(4, dtype=jnp.int32) == my_chunk // heads
    pair_prompt = jnp.sum(jnp.where(pick_pair, prompt_of, 0))
    pair_lens = jnp.sum(jnp.where(pick_pair[:, None], slot_lens, 0), axis=0)
    info = jnp.concatenate([pair_prompt[None], pair_lens])

    def positions(slot, prompt_size):
        return jnp.where(slot >= prompt, prompt_size + (slot - prompt) % CONT, slot)

    own_slots = my_chunk * rows + jnp.arange(rows, dtype=jnp.int32)
    cos_own, sin_own = rope_tables(positions(own_slots[None, :], prompt_of[:, None]))
    all_slots = jnp.arange(rows * ctx_size, dtype=jnp.int32).reshape(ctx_size, rows)
    cos_all, sin_all = rope_tables(positions(all_slots, pair_prompt))

    gain_one, gain_two, gain_three, gain_four = (
        gain[None, :] for gain in (norm_one, norm_two, norm_three, norm_four)
    )
    x_own, grad_own = block_in[0], out_grad[0]

    x_all = gather_rows(x_own)
    part = heads * HEAD
    wide = jnp.stack(
        [w.reshape(rows, 4, part) for w in (w_query, w_key, w_value)], axis=2
    ).transpose(1, 0, 2, 3)
    w_qkv = lax.all_to_all(
        wide.reshape(4, rows, 3 * part), "fsdp", 0, 0, tiled=True
    ).reshape(width, 3 * part)
    w_pair = lax.all_to_all(
        jnp.stack([w.reshape(w.shape[0], 4, ff_part).transpose(1, 0, 2) for w in (w_gate, w_up)], axis=1),
        "fsdp",
        0,
        0,
        tiled=True,
    )
    gate_part = w_pair[:, 0].reshape(width, ff_part)
    up_part = w_pair[:, 1].reshape(width, ff_part)

    piece = (heads, 3, rows, HEAD)
    qkv = pl.pallas_call(
        project_kernel,
        name="project",
        grid=(4,),
        in_specs=[
            place((rows, width)),
            whole((1, width)),
            whole((width, 3 * part)),
            place((rows, HEAD)),
            place((rows, HEAD)),
        ],
        out_specs=pl.BlockSpec(piece, lambda t: (t, 0, 0, 0)),
        out_shape=shaped(4 * heads, 3, rows, HEAD),
        compiler_params=params(24, "arbitrary"),
    )(x_all, gain_one, w_qkv, cos_own, sin_own)
    qkv = lax.all_to_all(qkv, "ctx", 0, 0, tiled=True)

    smem = pl.BlockSpec(memory_space=pltpu.SMEM)
    qkv_shape, head_shape = (ctx_size, 3, rows, HEAD), (ctx_size, rows, HEAD)
    mixed, exact, log_total = pl.pallas_call(
        functools.partial(attend_kernel, prompt_chunks, cont_chunks),
        name="attend",
        grid=(ctx_size,),
        in_specs=[smem, whole(qkv_shape)],
        out_specs=[whole(head_shape), whole(head_shape), whole((ctx_size, 1, rows))],
        out_shape=[
            shaped(*head_shape),
            shaped(*head_shape, kind=f32),
            shaped(ctx_size, 1, rows, kind=f32),
        ],
        compiler_params=params(32, "arbitrary"),
    )(info, qkv)
    attended = lax.all_to_all(mixed, "ctx", 0, 0, tiled=True)

    pair_spec = pl.BlockSpec((heads, rows, HEAD), lambda t: (t, 0, 0))
    two = shaped(2, rows, width)
    keep, send = pl.pallas_call(
        mix_out_kernel,
        name="mix_out",
        grid=(4,),
        in_specs=[pair_spec, whole((part, width))],
        out_specs=[kept((rows, width)), sent((rows, width))],
        out_shape=[two, two],
        compiler_params=params(16, "arbitrary"),
    )(attended, w_out)

    row_spec, gain_spec = whole((rows, width)), whole((1, width))
    sum_specs = [first_place((rows, width)), first_place((rows, width)), row_spec]
    full_row, low_row, gain_row = (
        shaped(rows, width, kind=f32),
        shaped(rows, width),
        shaped(1, width, kind=f32),
    )
    branch, middle, ff_input = pl.pallas_call(
        middle_kernel,
        name="middle",
        grid=(1,),
        in_specs=sum_specs + [row_spec, gain_spec, gain_spec],
        out_specs=[row_spec] * 3,
        out_shape=[full_row, full_row, low_row],
        compiler_params=params(24),
    )(*exchange_sums(keep, send), x_own, gain_two, gain_three)
    ff_all = gather_rows(ff_input)

    ff_rows = shaped(4, rows, ff_part)
    keep, send, slope, swish, hidden = pl.pallas_call(
        ff_kernel,
        name="ff",
        grid=(4,),
        in_specs=[
            place((rows, width)),
            whole((width, ff_part)),
            whole((width, ff_part)),
            whole((ff_part, width)),
        ],
        out_specs=[kept((rows, width)), sent((rows, width))] + [place((rows, ff_part))] * 3,
        out_shape=[two, two, ff_rows, ff_rows, ff_rows],
        compiler_params=params(40, "arbitrary"),
    )(ff_all, gate_part, up_part, w_down)

    block_out, ff_grad, part_four = pl.pallas_call(
        turnaround_kernel,
        name="turnaround",
        grid=(1,),
        in_specs=sum_specs + [row_spec, row_spec, gain_spec],
        out_specs=[row_spec, row_spec, gain_spec],
        out_shape=[low_row, low_row, gain_row],
        compiler_params=params(24),
    )(*exchange_sums(keep, send), middle, grad_own, gain_four)

    ff_grad_all = gather_rows(ff_grad)
    keep, send, gate_grad, up_grad = pl.pallas_call(
        ff_back_kernel,
        name="ff_back",
        grid=(4,),
        in_specs=[
            place((rows, width)),
            whole((width, ff_part)),
            whole((width, ff_part)),
            whole((ff_part, width)),
            place((rows, ff_part)),
            place((rows, ff_part)),
        ],
        out_specs=[kept((rows, width)), sent((rows, width))] + [place((rows, ff_part))] * 2,
        out_shape=[two, two, ff_rows, ff_rows],
        compiler_params=params(40, "arbitrary"),
    )(ff_grad_all, gate_part, up_part, w_down, slope, swish)

    tokens = 4 * rows
    flat_input = ff_all.reshape(tokens, width)
    down_term = cross_dot_low(
        hidden.reshape(tokens, ff_part), ff_grad_all.reshape(tokens, width)
    )
    pair_term = jnp.stack(
        [
            cross_dot_low(flat_input, grad.reshape(tokens, ff_part)).reshape(4, rows, ff_part)
            for grad in (gate_grad, up_grad)
        ],
        axis=1,
    )
    pair_term = lax.all_to_all(pair_term, "fsdp", 0, 0, tiled=True)
    pair_term = pair_term.transpose(1, 2, 0, 3).reshape(2, rows, ff_width)

    middle_grad, branch_grad, part_two, part_three = pl.pallas_call(
        branch_back_kernel,
        name="branch_back",
        grid=(1,),
        in_specs=sum_specs + [row_spec, row_spec, row_spec, gain_spec, gain_spec],
        out_specs=[row_spec, row_spec, gain_spec, gain_spec],
        out_shape=[full_row, low_row, gain_row, gain_row],
        compiler_params=params(24),
    )(*exchange_sums(keep, send), middle, branch, grad_own, gain_two, gain_three)
    branch_grad_all = gather_rows(branch_grad)

    attended_grad = pl.pallas_call(
        heads_back_kernel,
        name="heads_back",
        grid=(4,),
        in_specs=[place((rows, width)), whole((part, width))],
        out_specs=pair_spec,
        out_shape=shaped(4 * heads, rows, HEAD),
        compiler_params=params(16, "arbitrary"),
    )(branch_grad_all, w_out)
    attended_grad = lax.all_to_all(attended_grad, "ctx", 0, 0, tiled=True)
    out_term = cross_dot_low(
        attended.reshape(4, heads, rows, HEAD).transpose(0, 2, 1, 3).reshape(tokens, part),
        branch_grad_all.reshape(tokens, width),
    )

    pieces = pl.pallas_call(
        functools.partial(attend_back_kernel, prompt_chunks, cont_chunks),
        name="attend_back",
        grid=(ctx_size,),
        in_specs=[
            smem,
            whole(qkv_shape),
            whole(head_shape),
            whole(head_shape),
            whole((ctx_size, 1, rows)),
            whole(head_shape),
            whole(head_shape),
        ],
        out_specs=whole(qkv_shape),
        out_shape=shaped(*qkv_shape),
        scratch_shapes=[pltpu.VMEM(head_shape, f32), pltpu.VMEM(head_shape, f32)],
        compiler_params=params(40, "arbitrary"),
    )(info, qkv, attended_grad, exact, log_total, cos_all, sin_all)
    pieces = lax.all_to_all(pieces, "ctx", 0, 0, tiled=True)

    keep, send, qkv_term = pl.pallas_call(
        project_back_kernel,
        name="project_back",
        grid=(4,),
        in_specs=[
            pl.BlockSpec(piece, lambda t: (t, 0, 0, 0)),
            place((rows, width)),
            gain_spec,
            whole((width, 3 * part)),
        ],
        out_specs=[kept((rows, width)), sent((rows, width)), whole((width, 3 * part))],
        out_shape=[two, two, shaped(width, 3 * part)],
        scratch_shapes=[pltpu.VMEM((width, 3 * part), f32)],
        compiler_params=params(32, "arbitrary"),
    )(pieces, x_all, gain_one, w_qkv)

    in_grad, part_one = pl.pallas_call(
        input_back_kernel,
        name="input_back",
        grid=(1,),
        in_specs=sum_specs + [row_spec, row_spec, gain_spec],
        out_specs=[row_spec, gain_spec],
        out_shape=[full_row, gain_row],
        compiler_params=params(24),
    )(*exchange_sums(keep, send), x_own, middle_grad, gain_one)

    qkv_term = lax.all_to_all(qkv_term.reshape(4, rows, 3 * part), "fsdp", 0, 0, tiled=True)
    ff_sums = lax.psum((pair_term, down_term, out_term), "ctx")
    qkv_sum = lax.psum(qkv_term, "ctx")
    qkv_sum = (
        qkv_sum.reshape(4, rows, 3, part).transpose(2, 1, 0, 3).reshape(3, rows, width).astype(f32)
    )
    gain_sums = lax.psum(
        jnp.concatenate([part_one, part_two, part_three, part_four]), ("ctx", "fsdp")
    )
    return (
        block_out[None],
        in_grad[None],
        qkv_sum[0],
        qkv_sum[1],
        qkv_sum[2],
        ff_sums[2].astype(f32),
        gain_sums[0],
        gain_sums[1],
        ff_sums[0][0].astype(f32),
        ff_sums[0][1].astype(f32),
        ff_sums[1].astype(f32),
        gain_sums[2],
        gain_sums[3],
    )


def solution(mesh):
    fsdp, ctx = mesh.shape["fsdp"], mesh.shape["ctx"]

    def step(*args):
        width, groups = args[0].shape[2], args[0].shape[0]
        heads = width // HEAD
        rows = args[0].shape[1] // ctx
        paired = (
            fsdp == 4
            and groups == fsdp
            and heads == ctx
            and CONT % rows == 0
            and (P_DEV * ctx) % rows == 0
            and width // fsdp == rows
        )
        return jax.shard_map(
            pair_shards if paired else shards,
            mesh=mesh,
            in_specs=IN_SPECS,
            out_specs=OUT_SPECS,
            check_vma=False,
        )(*args)

    return step
```

```python
import functools
import math

import jax
import jax.numpy as jnp
from jax import lax
from jax.experimental import pallas as pl
from jax.experimental.pallas import tpu as pltpu
from jax.sharding import PartitionSpec as P

HEAD = 128
P_DEV = 128
CONT = 512
LOG2E = 1.4426950408889634

eps_norm = 1e-06
rope_base = 50000.0
masked_out = -1e30

bf16 = jnp.bfloat16
f32 = jnp.float32

def rms_norm(values, gain_vec):
    inverse = lax.rsqrt(jnp.mean(values * values, axis=-1, keepdims=True) + eps_norm)
    return (values * inverse * gain_vec, inverse)


def norm_back(values, inverse, gain_vec, upstream):
    weighted = upstream * gain_vec
    inner_mean = jnp.mean(values * weighted, axis=-1, keepdims=True)
    value_grad = inverse * weighted - values * inverse * inverse * inverse * inner_mean
    return (value_grad, jnp.sum(upstream * values * inverse, axis=0))


def rotate(values, position, turn_sign):
    seq_len = values.shape[0]
    half_size = HEAD // 2
    split_heads = values.reshape(seq_len, -1, HEAD)
    frequencies = rope_base ** (-2.0 * jnp.arange(half_size, dtype=jnp.float32) / HEAD)
    angles = position.astype(jnp.float32)[:, None] * frequencies[None, :]
    cosine = jnp.concatenate([jnp.cos(angles), jnp.cos(angles)], axis=-1)[:, None, :]
    sine_part = turn_sign * jnp.concatenate([jnp.sin(angles), jnp.sin(angles)], axis=-1)[:, None, :]
    turned = jnp.concatenate([-split_heads[..., half_size:], split_heads[..., :half_size]], axis=-1)
    return (split_heads * cosine + turned * sine_part).reshape(seq_len, -1)


def token_info(slot_index, prompt, prompt_size, slot_lens):
    in_cont = slot_index >= prompt
    rel_index = jnp.maximum(slot_index - prompt, 0)
    slot_of = jnp.where(in_cont, rel_index // CONT, -1)
    offset = rel_index % CONT
    slot_range = jnp.arange(slot_lens.shape[0], dtype=jnp.int32)
    slot_len = jnp.sum(
        jnp.where(slot_of[:, None] == slot_range[None, :], slot_lens[None, :], 0), axis=1
    )
    token_valid = jnp.where(in_cont, offset < slot_len, slot_index < prompt_size)
    position = jnp.where(in_cont, prompt_size + offset, slot_index)
    return (token_valid, slot_of, position)


def cross_dot(operand, partner):
    return lax.dot_general(
        operand, partner, (((0,), (0,)), ((), ())), preferred_element_type=jnp.float32
    )


def back_dot(operand, partner):
    return lax.dot_general(
        operand, partner, (((1,), (1,)), ((), ())), preferred_element_type=jnp.float32
    )


def keep_same(state):
    return state


def shards(
    block_in,
    out_grad,
    w_query,
    w_key,
    w_value,
    w_out,
    norm_one,
    norm_two,
    w_gate,
    w_up,
    w_down,
    norm_three,
    norm_four,
    prompt_len,
    cont_len,
    group_ids,
    cont_ids,
):
    local_rows = block_in.shape[1]
    model_width = block_in.shape[2]
    ff_width = w_gate.shape[1]
    ctx_size = lax.axis_size("ctx")
    group_rows = local_rows * ctx_size
    prompt = P_DEV * ctx_size
    head_count = model_width // HEAD
    score_scale = 1.0 / math.sqrt(HEAD)
    row_index = lax.axis_index("fsdp")
    groups = group_ids.shape[0]
    slot_count = cont_ids.shape[1]
    group_range = jnp.arange(groups, dtype=jnp.int32)
    own_group = jnp.sum(jnp.where(group_range == row_index, group_ids, 0))
    own_prompt = jnp.sum(jnp.where(group_range == own_group, prompt_len, 0))
    own_lens = jnp.sum(jnp.where((group_range == own_group)[:, None], cont_len, 0), axis=0)
    own_ids = jnp.sum(jnp.where((group_range == row_index)[:, None], cont_ids, 0), axis=0)
    slot_range = jnp.arange(slot_count, dtype=jnp.int32)
    slot_lens = jnp.sum(
        jnp.where(own_ids[:, None] == slot_range[None, :], own_lens[None, :], 0), axis=1
    )
    query_index = lax.axis_index("ctx") * local_rows + jnp.arange(local_rows, dtype=jnp.int32)
    key_index = jnp.arange(group_rows, dtype=jnp.int32)
    query_valid, query_slot, position = token_info(query_index, prompt, own_prompt, slot_lens)
    key_valid, key_slot, unused_pos = token_info(key_index, prompt, own_prompt, slot_lens)
    tokens = block_in[0].astype(jnp.float32)
    full_query, full_key, full_value, full_out = (
        lax.all_gather(w_query, "fsdp", axis=0, tiled=True),
        lax.all_gather(w_key, "fsdp", axis=0, tiled=True),
        lax.all_gather(w_value, "fsdp", axis=0, tiled=True),
        lax.all_gather(w_out, "fsdp", axis=0, tiled=True),
    )
    normed_full, inverse_one = rms_norm(tokens, norm_one)
    normed = normed_full.astype(jnp.bfloat16)
    queries = rotate(
        jnp.dot(normed, full_query, preferred_element_type=jnp.float32), position, 1.0
    ).astype(jnp.bfloat16)
    keys_local = rotate(
        jnp.dot(normed, full_key, preferred_element_type=jnp.float32), position, 1.0
    ).astype(jnp.bfloat16)
    values_local = jnp.dot(normed, full_value, preferred_element_type=jnp.float32).astype(
        jnp.bfloat16
    )
    all_keys, all_values = (
        lax.all_gather(keys_local, "ctx", axis=0, tiled=True),
        lax.all_gather(values_local, "ctx", axis=0, tiled=True),
    )
    key_block = math.gcd(group_rows, 512)
    block_count = group_rows // key_block
    blocks_in = (
        all_keys.reshape(block_count, key_block, head_count, HEAD),
        all_values.reshape(block_count, key_block, head_count, HEAD),
        key_valid.reshape(block_count, key_block),
        key_slot.reshape(block_count, key_block),
        key_index.reshape(block_count, key_block),
    )
    query_heads = queries.reshape(local_rows, head_count, HEAD)

    def mask_of(inputs):
        key_ids = inputs[4]
        return (
            query_valid[:, None]
            & inputs[2][None, :]
            & (key_ids[None, :] <= query_index[:, None])
            & ((key_ids[None, :] < prompt) | (inputs[3][None, :] == query_slot[:, None]))
        )

    def raw_scores(inputs):
        return (
            jnp.einsum("qhd,khd->hqk", query_heads, inputs[0], preferred_element_type=jnp.float32)
            * score_scale
        )

    def running(state_in, inputs):
        allowed = mask_of(inputs)

        def running_visit(state):
            row_top, exp_total = state
            scores = jnp.where(allowed[None], raw_scores(inputs), masked_out)
            new_top = jnp.maximum(row_top, jnp.max(scores, axis=-1, keepdims=True))
            exp_total = exp_total * jnp.exp(row_top - new_top) + jnp.sum(
                jnp.where(allowed[None], jnp.exp(scores - new_top), 0.0), axis=-1, keepdims=True
            )
            return (new_top, exp_total)

        return (lax.cond(jnp.any(allowed), running_visit, keep_same, state_in), None)

    start_top = jnp.full((head_count, local_rows, 1), -jnp.inf, jnp.float32)
    start_total = jnp.zeros((head_count, local_rows, 1), jnp.float32)
    (row_top, exp_total), unused = lax.scan(running, (start_top, start_total), blocks_in)
    has_keys = exp_total > 0.0
    log_total = jnp.where(has_keys, row_top + jnp.log(jnp.where(has_keys, exp_total, 1.0)), 0.0)

    def probs_of(inputs, allowed):
        return jnp.where(allowed[None], jnp.exp(raw_scores(inputs) - log_total), 0.0)

    def mix_step(accumulated, inputs):
        allowed = mask_of(inputs)

        def mix_visit(total):
            attn_probs = probs_of(inputs, allowed).astype(jnp.bfloat16)
            return total + jnp.einsum(
                "hqk,khd->qhd", attn_probs, inputs[1], preferred_element_type=jnp.float32
            )

        return (lax.cond(jnp.any(allowed), mix_visit, keep_same, accumulated), None)

    mixture, unused = lax.scan(
        mix_step, jnp.zeros((local_rows, head_count, HEAD), jnp.float32), blocks_in
    )
    valid_col = query_valid[:, None].astype(jnp.float32)
    attended = (mixture.reshape(local_rows, model_width) * valid_col).astype(jnp.bfloat16)
    branch = jnp.dot(attended, full_out, preferred_element_type=jnp.float32)
    branch_normed, inverse_two = rms_norm(branch, norm_two)
    middle = tokens + branch_normed
    full_gate, full_up, full_down = (
        lax.all_gather(w_gate, "fsdp", axis=0, tiled=True),
        lax.all_gather(w_up, "fsdp", axis=0, tiled=True),
        lax.all_gather(w_down, "fsdp", axis=0, tiled=True),
    )
    ff_normed, inverse_three = rms_norm(middle, norm_three)
    ff_input = ff_normed.astype(jnp.bfloat16)
    gate_pre = jnp.dot(ff_input, full_gate, preferred_element_type=jnp.float32)
    upward = jnp.dot(ff_input, full_up, preferred_element_type=jnp.float32)
    gate_sig = jax.nn.sigmoid(gate_pre)
    swish_out = gate_pre * gate_sig
    hidden = (swish_out * upward).astype(jnp.bfloat16)
    ff_out = jnp.dot(hidden, full_down, preferred_element_type=jnp.float32)
    out_normed, inverse_four = rms_norm(ff_out, norm_four)
    result = middle + out_normed
    upstream = out_grad[0].astype(jnp.float32)
    ff_out_full, grad_norm_four = norm_back(ff_out, inverse_four, norm_four, upstream)
    ff_out_grad = ff_out_full.astype(jnp.bfloat16)
    hidden_grad = back_dot(ff_out_grad, full_down)
    up_grad = (hidden_grad * swish_out).astype(jnp.bfloat16)
    gate_grad = (hidden_grad * upward * gate_sig * (1.0 + gate_pre * (1.0 - gate_sig))).astype(
        jnp.bfloat16
    )
    ff_in_grad = back_dot(gate_grad, full_gate) + back_dot(up_grad, full_up)
    middle_part, grad_norm_three = norm_back(middle, inverse_three, norm_three, ff_in_grad)
    middle_grad = upstream + middle_part
    branch_full, grad_norm_two = norm_back(branch, inverse_two, norm_two, middle_grad)
    branch_grad = branch_full.astype(jnp.bfloat16)
    attended_grad = back_dot(branch_grad, full_out).astype(jnp.bfloat16) * valid_col.astype(
        jnp.bfloat16
    )
    grad_heads = attended_grad.reshape(local_rows, head_count, HEAD)

    def delta_step(accumulated, inputs):
        allowed = mask_of(inputs)

        def delta_visit(total):
            attn_probs = probs_of(inputs, allowed)
            prob_grad = jnp.einsum(
                "qhd,khd->hqk", grad_heads, inputs[1], preferred_element_type=jnp.float32
            )
            return total + jnp.sum(attn_probs * prob_grad, axis=-1, keepdims=True)

        return (lax.cond(jnp.any(allowed), delta_visit, keep_same, accumulated), None)

    row_delta, unused = lax.scan(
        delta_step, jnp.zeros((head_count, local_rows, 1), jnp.float32), blocks_in
    )
    zero_part = jnp.zeros((key_block, head_count, HEAD), jnp.float32)

    def grad_step(accumulated, inputs):
        allowed = mask_of(inputs)

        def grad_visit(total):
            attn_probs = probs_of(inputs, allowed)
            prob_grad = jnp.einsum(
                "qhd,khd->hqk", grad_heads, inputs[1], preferred_element_type=jnp.float32
            )
            score_grad = (attn_probs * (prob_grad - row_delta)).astype(jnp.bfloat16)
            total = total + jnp.einsum(
                "hqk,khd->qhd", score_grad, inputs[0], preferred_element_type=jnp.float32
            )
            key_part = jnp.einsum(
                "hqk,qhd->khd", score_grad, query_heads, preferred_element_type=jnp.float32
            )
            value_part = jnp.einsum(
                "hqk,qhd->khd",
                attn_probs.astype(jnp.bfloat16),
                grad_heads,
                preferred_element_type=jnp.float32,
            )
            return (total, (key_part, value_part))

        def skip(total):
            return (total, (zero_part, zero_part))

        return lax.cond(jnp.any(allowed), grad_visit, skip, accumulated)

    query_acc, (key_parts, value_parts) = lax.scan(
        grad_step, jnp.zeros((local_rows, head_count, HEAD), jnp.float32), blocks_in
    )
    key_terms = key_parts.reshape(group_rows, model_width) * score_scale
    value_terms = value_parts.reshape(group_rows, model_width)
    key_sum, value_sum = (
        lax.psum_scatter(
            key_terms.astype(jnp.bfloat16), "ctx", scatter_dimension=0, tiled=True
        ).astype(jnp.float32),
        lax.psum_scatter(
            value_terms.astype(jnp.bfloat16), "ctx", scatter_dimension=0, tiled=True
        ).astype(jnp.float32),
    )
    query_grad = rotate(
        query_acc.reshape(local_rows, model_width) * score_scale, position, -1.0
    ).astype(jnp.bfloat16)
    key_grad = rotate(key_sum, position, -1.0).astype(jnp.bfloat16)
    value_grad = value_sum.astype(jnp.bfloat16)
    normed_grad = (
        back_dot(query_grad, full_query)
        + back_dot(key_grad, full_key)
        + back_dot(value_grad, full_value)
    )
    input_part, grad_norm_one = norm_back(tokens, inverse_one, norm_one, normed_grad)
    input_grad = middle_grad + input_part
    wide_pairs = (
        (normed, query_grad),
        (normed, key_grad),
        (normed, value_grad),
        (attended, branch_grad),
        (ff_input, gate_grad),
        (ff_input, up_grad),
    )

    def wide_term(selector):
        return jnp.concatenate(
            [cross_dot(selector(operand), partner) for operand, partner in wide_pairs], axis=1
        )

    wide_local = lax.psum_scatter(
        wide_term(lambda operand: operand).astype(jnp.bfloat16),
        "fsdp",
        scatter_dimension=0,
        tiled=True,
    )
    ff_local = lax.psum_scatter(
        cross_dot((lambda operand: operand)(hidden), ff_out_grad).astype(jnp.bfloat16),
        "fsdp",
        scatter_dimension=0,
        tiled=True,
    )
    wide_sum, ff_sum = (
        lax.psum(wide_local, "ctx").astype(jnp.float32),
        lax.psum(ff_local, "ctx").astype(jnp.float32),
    )
    gain_sums = lax.psum(
        jnp.stack([grad_norm_one, grad_norm_two, grad_norm_three, grad_norm_four]), ("ctx", "fsdp")
    )
    edge_two = 2 * model_width
    edge_three = 3 * model_width
    edge_four = 4 * model_width
    edge_five = 4 * model_width + ff_width
    return (
        result.astype(jnp.bfloat16)[None],
        input_grad[None],
        wide_sum[:, :model_width],
        wide_sum[:, model_width:edge_two],
        wide_sum[:, edge_two:edge_three],
        wide_sum[:, edge_three:edge_four],
        gain_sums[0],
        gain_sums[1],
        wide_sum[:, edge_four:edge_five],
        wide_sum[:, edge_five:],
        ff_sum,
        gain_sums[2],
        gain_sums[3],
    )


IN_SPECS = (
    (P("fsdp", "ctx", None),) * 2
    + (P("fsdp", None),) * 4
    + (P(), P())
    + (P("fsdp", None),) * 3
    + (P(),) * 6
)
OUT_SPECS = (
    (P("fsdp", "ctx", None),) * 2
    + (P("fsdp", None),) * 4
    + (P(), P())
    + (P("fsdp", None),) * 3
    + (P(), P())
)


MIB = 1 << 20
PLACES = 4


def core_swap(values):
    return lax.ppermute(values, "fsdp", [(i, i ^ 1) for i in range(4)])


def y_swap(values):
    return lax.ppermute(values, "fsdp", [(i, i ^ 2) for i in range(4)])


def ctx_swap(values, bit):
    size = lax.axis_size("ctx")
    return lax.ppermute(values, "ctx", [(i, i ^ bit) for i in range(size)])


def z_shift(values):
    size = lax.axis_size("ctx")
    return lax.ppermute(values, "ctx", [(i, (i + 2) % size) for i in range(size)])


def tie(*values):
    return lax.optimization_barrier(values)


def after(value, *others):
    return lax.optimization_barrier((value, others))[0]


def far_rows(own):
    across = y_swap(own)
    return across, core_swap(across)


def params(limit_mib, *semantics):
    return pltpu.CompilerParams(
        dimension_semantics=semantics or None, vmem_limit_bytes=limit_mib * MIB
    )


def cost(microseconds):
    return pl.CostEstimate(flops=int(microseconds * 3e8), bytes_accessed=0, transcendentals=0)


def whole(shape):
    return pl.BlockSpec(shape, lambda *_: (0,) * len(shape))


SMEM = pl.BlockSpec(memory_space=pltpu.SMEM)


def dot_nn(a, b):
    return lax.dot_general(a, b, (((1,), (0,)), ((), ())), preferred_element_type=f32)


def dot_nt(a, b):
    return lax.dot_general(a, b, (((1,), (1,)), ((), ())), preferred_element_type=f32)


def dot_tn(a, b):
    return lax.dot_general(a, b, (((0,), (0,)), ((), ())), preferred_element_type=f32)


def inverse_rms(values):
    return lax.rsqrt(jnp.mean(values * values, axis=-1, keepdims=True) + eps_norm)


def turn(values, cosine, sine):
    return values * cosine + pltpu.roll(values, HEAD // 2, 1) * sine


def choose(step, refs, target):
    for index, ref in enumerate(refs):

        @pl.when(step == index)
        def _(ref=ref):
            target[...] = ref[...]


def columns_of(me_ref, place, rows):
    return pl.ds(pl.multiple_of((me_ref[0] ^ place) * rows, rows), rows)


def split_qkv_kernel(me_ref, q_ref, k_ref, v_ref, *out_refs):
    part = out_refs[0].shape[1] // 3
    for place, out_ref in enumerate(out_refs):
        for kind, ref in enumerate((q_ref, k_ref, v_ref)):
            out_ref[:, kind * part : (kind + 1) * part] = ref[:, columns_of(me_ref, place, part)]


def pair_columns(half):
    main = half // HEAD * HEAD
    rest = half - main
    return (
        (0, 0, 0, main),
        (1, 0, main, main),
        (0, main, 2 * main, rest),
        (1, main, 2 * main + rest, rest),
    )


def split_ff_kernel(
    me_ref, gate_ref, up_ref, down_ref, own_ref, own_sent, beside_ref, beside_sent, down_sent
):
    half = own_ref.shape[-1] // 2
    for me in range(PLACES):

        @pl.when(me_ref[0] == me)
        def _(me=me):
            for place in range(PLACES):
                target = own_ref if place % 2 == 0 else beside_ref
                for kind, start, where, size in pair_columns(half):
                    first = (me ^ place) * half + start
                    target[place // 2, :, where : where + size] = (gate_ref, up_ref)[kind][
                        :, first : first + size
                    ]

    side = me_ref[1] % 2
    own_sent[...] = own_ref[1 - side]
    beside_sent[...] = beside_ref[1 - side]
    columns = down_sent.shape[1]
    down_sent[...] = down_ref[:, pl.ds(pl.multiple_of(side * columns, columns), columns)]


def project_kernel(
    me_ref, x0, x1, x2, x3, gain_ref, w0, w1, w2, w3, cos_ref, sin_ref, out_ref, x_scr, normed_scr
):
    choose(pl.program_id(0), (x0, x1, x2, x3), x_scr)
    x = x_scr[...].astype(f32)
    normed_scr[...] = (x * inverse_rms(x) * gain_ref[...]).astype(bf16)
    rows = w0.shape[0]
    product = sum(
        dot_nn(normed_scr[:, columns_of(me_ref, place, rows)], w[...])
        for place, w in enumerate((w0, w1, w2, w3))
    )
    heads = out_ref.shape[0]
    for kind in range(3):
        for head in range(heads):
            start = (kind * heads + head) * HEAD
            part = product[:, start : start + HEAD]
            if kind < 2:
                part = turn(part, cos_ref[0], sin_ref[0])
            out_ref[head, kind] = part.astype(bf16)


def chunk_facts(chunk, rows, prompt_chunks, cont_chunks, info_ref):
    beyond = jnp.maximum(chunk - prompt_chunks, 0)
    in_cont = chunk >= prompt_chunks
    slot = beyond // cont_chunks
    first = jnp.where(in_cont, prompt_chunks + slot * cont_chunks, 0)
    ahead = jnp.where(in_cont, prompt_chunks, 0)
    start = jnp.where(in_cont, beyond % cont_chunks, chunk) * rows
    limit = jnp.where(in_cont, info_ref[1 + slot], info_ref[0])
    return first, ahead, start, limit


def attend_kernel(
    prompt_chunks, cont_chunks, info_ref, qkv_ref, out_ref, exact_ref, lse_ref
):
    chunk = pl.program_id(0)
    rows = qkv_ref.shape[2]
    scale = LOG2E / math.sqrt(HEAD)
    query = qkv_ref[chunk, 0]
    first, ahead, start, limit = chunk_facts(chunk, rows, prompt_chunks, cont_chunks, info_ref)
    key_place = lax.broadcasted_iota(jnp.int32, (rows, rows), 0)
    query_place = lax.broadcasted_iota(jnp.int32, (rows, rows), 1)

    def visit(key_chunk, bias, state):
        top, total, mixed = state
        scores = dot_nt(qkv_ref[key_chunk, 1], query) * scale + bias
        new_top = jnp.maximum(top, jnp.max(scores, axis=0, keepdims=True))
        weights = jnp.exp2(scores - new_top)
        shrink = jnp.exp2(top - new_top)
        total = total * shrink + jnp.sum(weights, axis=0, keepdims=True)
        mixed = mixed * shrink + dot_tn(qkv_ref[key_chunk, 2], weights.astype(bf16))
        return new_top, total, mixed

    def prompt_visit(key_chunk, state):
        bias = jnp.where(key_chunk * rows + key_place < info_ref[0], 0.0, masked_out)
        return visit(key_chunk, bias, state)

    def own_visit(key_chunk, state):
        return visit(key_chunk, 0.0, state)

    state = (
        jnp.full((1, rows), -1e38, f32),
        jnp.zeros((1, rows), f32),
        jnp.zeros((HEAD, rows), f32),
    )
    state = visit(chunk, jnp.where(key_place <= query_place, 0.0, masked_out), state)
    state = lax.fori_loop(0, ahead, prompt_visit, state)
    top, total, mixed = lax.fori_loop(first, chunk, own_visit, state)
    valid = start + lax.broadcasted_iota(jnp.int32, (1, rows), 1) < limit
    settled = jnp.where(valid, mixed / total, 0.0).T
    out_ref[chunk] = settled.astype(bf16)
    exact_ref[chunk] = settled
    lse_ref[chunk] = top + jnp.log2(total)


def attend_back_kernel(
    prompt_chunks,
    cont_chunks,
    info_ref,
    qkv_ref,
    grad_ref,
    exact_ref,
    lse_ref,
    cos_ref,
    sin_ref,
    out_ref,
    key_sum,
    value_sum,
):
    chunk = pl.program_id(0)
    chunks = pl.num_programs(0)
    rows = qkv_ref.shape[2]
    scale = LOG2E / math.sqrt(HEAD)
    query = qkv_ref[chunk, 0]
    first, ahead, start, limit = chunk_facts(chunk, rows, prompt_chunks, cont_chunks, info_ref)
    key_place = lax.broadcasted_iota(jnp.int32, (rows, rows), 0)
    query_place = lax.broadcasted_iota(jnp.int32, (rows, rows), 1)
    valid = start + lax.broadcasted_iota(jnp.int32, (rows, 1), 0) < limit
    grad_full = jnp.where(valid, grad_ref[chunk].astype(f32), 0.0)
    grad = grad_full.astype(bf16)
    delta = jnp.sum((grad_full * exact_ref[chunk]).T, axis=0, keepdims=True)
    log_total = lse_ref[chunk]

    @pl.when(chunk == 0)
    def _():
        key_sum[...] = jnp.zeros_like(key_sum)
        value_sum[...] = jnp.zeros_like(value_sum)

    def visit(key_chunk, bias, query_sum):
        key = qkv_ref[key_chunk, 1]
        scores = dot_nt(key, query) * scale + bias
        weights = jnp.exp2(scores - log_total)
        weight_grad = dot_nt(qkv_ref[key_chunk, 2], grad)
        score_grad = (weights * (weight_grad - delta)).astype(bf16)
        value_sum[key_chunk] += dot_nn(weights.astype(bf16), grad)
        key_sum[key_chunk] += dot_nn(score_grad, query)
        return query_sum + dot_tn(key, score_grad)

    def prompt_visit(key_chunk, query_sum):
        bias = jnp.where(key_chunk * rows + key_place < info_ref[0], 0.0, masked_out)
        return visit(key_chunk, bias, query_sum)

    def own_visit(key_chunk, query_sum):
        return visit(key_chunk, 0.0, query_sum)

    query_sum = visit(
        chunk,
        jnp.where(key_place <= query_place, 0.0, masked_out),
        jnp.zeros((HEAD, rows), f32),
    )
    query_sum = lax.fori_loop(0, ahead, prompt_visit, query_sum)
    query_sum = lax.fori_loop(first, chunk, own_visit, query_sum)
    back = 1.0 / math.sqrt(HEAD)
    out_ref[chunk, 0] = turn(query_sum.T * back, cos_ref[chunk], -sin_ref[chunk]).astype(bf16)

    @pl.when(chunk == chunks - 1)
    def _():
        @pl.loop(0, chunks)
        def _(key_chunk):
            out_ref[key_chunk, 1] = turn(
                key_sum[key_chunk] * back, cos_ref[key_chunk], -sin_ref[key_chunk]
            ).astype(bf16)
            out_ref[key_chunk, 2] = value_sum[key_chunk].astype(bf16)


def mix_out_kernel(near_ref, far_ref, w_near_ref, w_far_ref, keep_ref, send_ref):
    heads = near_ref.shape[0] // PLACES
    part = heads * HEAD
    for step in range(2):
        total = 0.0
        for ref, w_ref in ((near_ref, w_near_ref), (far_ref, w_far_ref)):
            both = jnp.concatenate([ref[step * heads + j] for j in range(heads)], axis=1)
            total = total + dot_nn(both, w_ref[...])
        if step == 0:
            keep_ref[...] = total
        else:
            send_ref[...] = total.astype(bf16)


def heads_back_kernel(own_ref, beside_ref, w_near_ref, w_far_ref, near_ref, far_ref):
    heads = near_ref.shape[0] // 2
    for step, ref in enumerate((own_ref, beside_ref)):
        for w_ref, out_ref in ((w_near_ref, near_ref), (w_far_ref, far_ref)):
            both = dot_nt(ref[...], w_ref[...]).astype(bf16)
            for head in range(heads):
                out_ref[step * heads + head] = both[:, head * HEAD : (head + 1) * HEAD]


def project_back_kernel(me_ref, pieces_ref, w0, w1, w2, w3, keep_ref, send_ref):
    step = pl.program_id(0)
    heads = pieces_ref.shape[0]
    pieces = jnp.concatenate(
        [pieces_ref[head, kind] for kind in range(3) for head in range(heads)], axis=1
    )
    rows = w0.shape[0]
    for target, parity in ((keep_ref, 0), (send_ref, 1)):

        @pl.when(step % 2 == parity)
        def _(target=target):
            for place, w in enumerate((w0, w1, w2, w3)):
                target[0, :, columns_of(me_ref, place, rows)] = dot_nt(pieces, w[...]).astype(bf16)


def project_grad_kernel(me_ref, pieces_ref, own_ref, other_ref, gain_ref, out_ref, total):
    step = pl.program_id(0)
    side = me_ref[1] % 2

    def add(ref, chunk):
        x = ref[...].astype(f32)
        normed = (x * inverse_rms(x) * gain_ref[...]).astype(bf16)
        pieces = jnp.concatenate([pieces_ref[chunk, kind] for kind in range(3)], axis=1)
        return dot_tn(normed, pieces)

    term = add(own_ref.at[step], 2 * step + side) + add(other_ref.at[step], 2 * step + 1 - side)

    @pl.when(step == 0)
    def _():
        total[...] = term

    @pl.when(step > 0)
    def _():
        total[...] += term

    @pl.when(step == pl.num_programs(0) - 1)
    def _():
        spread_rows(me_ref, total, [out_ref])


def middle_kernel(keep_ref, received_ref, x_ref, two_ref, three_ref, branch_ref, middle_ref, input_ref):
    branch = keep_ref[...] + received_ref[...].astype(f32)
    middle = x_ref[...].astype(f32) + branch * inverse_rms(branch) * two_ref[...]
    branch_ref[...] = branch
    middle_ref[...] = middle
    input_ref[...] = (middle * inverse_rms(middle) * three_ref[...]).astype(bf16)


def norm_back_parts(values, gain, upstream):
    inverse = inverse_rms(values)
    weighted = upstream * gain
    inner = jnp.mean(values * weighted, axis=-1, keepdims=True)
    value_grad = inverse * weighted - values * (inverse * inverse * inverse * inner)
    return value_grad, jnp.sum(upstream * values * inverse, axis=0, keepdims=True)


def turnaround_kernel(
    keep_ref, received_ref, middle_ref, grad_ref, four_ref, out_ref, back_ref, gain_ref
):
    ff_out = keep_ref[...] + received_ref[...].astype(f32)
    out_ref[...] = (middle_ref[...] + ff_out * inverse_rms(ff_out) * four_ref[...]).astype(bf16)
    value_grad, gain = norm_back_parts(ff_out, four_ref[...], grad_ref[...].astype(f32))
    back_ref[...] = value_grad.astype(bf16)
    gain_ref[...] = gain


def branch_back_kernel(
    keep_ref,
    received_ref,
    middle_ref,
    branch_ref,
    grad_ref,
    two_ref,
    three_ref,
    middle_grad_ref,
    branch_grad_ref,
    gain_two_ref,
    gain_three_ref,
):
    input_grad = keep_ref[...] + received_ref[...].astype(f32)
    middle_part, gain_three_ref[...] = norm_back_parts(middle_ref[...], three_ref[...], input_grad)
    middle_grad = grad_ref[...].astype(f32) + middle_part
    middle_grad_ref[...] = middle_grad
    branch_grad, gain_two_ref[...] = norm_back_parts(branch_ref[...], two_ref[...], middle_grad)
    branch_grad_ref[...] = branch_grad.astype(bf16)


def input_back_kernel(
    keep_ref, received_ref, across_ref, x_ref, middle_grad_ref, one_ref, out_ref, gain_ref
):
    normed_grad = keep_ref[0].astype(f32) + received_ref[0].astype(f32) + across_ref[...].astype(f32)
    part, gain_ref[...] = norm_back_parts(x_ref[...].astype(f32), one_ref[...], normed_grad)
    out_ref[...] = middle_grad_ref[...] + part


def far_columns(side, width, first, second):
    half = width // 2
    for place, ref in ((side, first), (1 - side, second)):
        yield pl.ds(pl.multiple_of(place * half, half), half), ref


def put_rows(scr, place_major, me_ref, *refs):
    rows, width = refs[0].shape
    size = width // PLACES
    for index, ref in enumerate(refs):
        where = slice(index * rows, (index + 1) * rows)
        if place_major:
            for place in range(PLACES):
                scr[where, place * size : (place + 1) * size] = ref[:, columns_of(me_ref, place, size)]
        else:
            scr[where, :] = ref[...]


def pair_product(x_scr, weights):
    size = x_scr.shape[1] // PLACES
    return sum(
        dot_nn(x_scr[:, place * size : (place + 1) * size], w)
        for place, w in enumerate(weights)
    )


def gate_parts(pair, half):
    def parts(gate, upward):
        sigma = 1.0 / (1.0 + jnp.exp(-gate))
        swish = gate * sigma
        slope = upward * sigma * (1.0 + gate * (1.0 - sigma))
        return swish, slope, (swish * upward).astype(bf16)

    main = half // HEAD * HEAD
    rest = half - main
    body = parts(pair[:, :main], pair[:, main : 2 * main])
    edge = pair[:, 2 * main :]
    edge_swish, edge_slope, edge_hidden = parts(edge, pltpu.roll(edge, rest, 1))
    lane = lax.broadcasted_iota(jnp.int32, edge.shape, 1)
    edge_factor = jnp.where(lane < rest, edge_slope, pltpu.roll(edge_swish, rest, 1))
    return body, edge_factor, edge_hidden


def put_hidden(ref, body, edge, main):
    rows = ref.shape[1]
    for row in range(2):
        where = slice(row * rows, (row + 1) * rows)
        ref[row, :, :main] = body[where]
        ref[row, :, main:] = edge[where]


def ff_kernel(
    me_ref,
    own_ref,
    beside_ref,
    w0,
    w1,
    w2y,
    w2x,
    w3y,
    w3x,
    down_near,
    down_y,
    down_x,
    keep_ref,
    send_ref,
    saved_ref,
    hidden_ref,
    x_scr,
    pair_scr,
    hidden_scr,
    total,
):
    turn_index = pl.program_id(0)
    side = me_ref[1] % 2
    block = turn_index ^ side
    width = x_scr.shape[1]
    half = down_near.shape[0]
    main = half // HEAD * HEAD

    @pl.when(turn_index == 0)
    def _():
        put_rows(x_scr, True, me_ref, own_ref, beside_ref)
        pair_scr[...] = pair_product(x_scr, (w0[0], w1[0], w2y[...], w3y[...]))

    @pl.when(turn_index == 1)
    def _():
        pair_scr[...] = pair_product(x_scr, (w0[0], w1[0], w2x[...], w3x[...]))

    (swish, slope, hidden), edge_factor, edge_hidden = gate_parts(pair_scr[...], half)
    saved_ref[0, :, :main] = slope.astype(bf16)
    saved_ref[0, :, main : 2 * main] = swish.astype(bf16)
    saved_ref[0, :, 2 * main :] = edge_factor.astype(bf16)
    hidden_scr[:, :main] = hidden
    hidden_scr[:, main:] = edge_hidden

    def add_term(columns, term):
        @pl.when(turn_index == 0)
        def _():
            total[:, columns] = term

        @pl.when(turn_index == 1)
        def _():
            total[:, columns] += term

    @pl.when(block == 0)
    def _():
        put_hidden(hidden_ref, hidden, edge_hidden, main)
        add_term(slice(None), dot_nn(hidden_scr[:, :half], down_near[...]))

    @pl.when(block == 1)
    def _():
        for columns, down in far_columns(side, width, down_y, down_x):
            add_term(columns, dot_nn(hidden_scr[:, :half], down[...]))

    @pl.when(turn_index == 1)
    def _():
        rows = keep_ref.shape[0]
        keep_ref[...] = total[:rows]
        send_ref[...] = total[rows:].astype(bf16)


def put_pair_grad(target, hidden_grad, factors, half):
    main = half // HEAD * HEAD
    edge = hidden_grad[:, main:]
    edge = jnp.concatenate([edge, edge], axis=1)
    for values, start in ((hidden_grad[:, :main], 0), (hidden_grad[:, :main], main), (edge, 2 * main)):
        columns = slice(start, start + values.shape[1])
        target[:, columns] = (values * factors[:, columns].astype(f32)).astype(bf16)


def ff_back_kernel(
    me_ref,
    own_ref,
    beside_ref,
    w0,
    w1,
    w2y,
    w2x,
    w3y,
    w3x,
    down_near,
    down_y,
    down_x,
    saved_ref,
    keep_ref,
    send_ref,
    pair_ref,
    grad_scr,
    hidden_scr,
    pair_scr,
    total,
):
    turn_index = pl.program_id(0)
    side = me_ref[1] % 2
    block = turn_index ^ side
    width = grad_scr.shape[1]
    half = down_near.shape[0]
    rows = keep_ref.shape[0]

    @pl.when(turn_index == 0)
    def _():
        put_rows(grad_scr, False, me_ref, own_ref, beside_ref)

    @pl.when(block == 0)
    def _():
        hidden_scr[...] = dot_nt(grad_scr[...], down_near[...])

    @pl.when(block == 1)
    def _():
        hidden_scr[...] = sum(
            dot_nt(grad_scr[:, columns], down[...])
            for columns, down in far_columns(side, width, down_y, down_x)
        )

    put_pair_grad(pair_scr, hidden_scr[...], saved_ref.at[0], half)

    @pl.when(block == 0)
    def _():
        for row in range(2):
            pair_ref[row] = pair_scr[row * rows : (row + 1) * rows]

    size = width // PLACES
    for index, far in enumerate(((w2y, w3y), (w2x, w3x))):

        @pl.when(turn_index == index)
        def _(index=index, far=far):
            for place, w in enumerate((w0[0], w1[0], far[0][...], far[1][...])):
                term = dot_nt(pair_scr[...], w)
                columns = columns_of(me_ref, place, size)
                if index == 0:
                    total[:, place * size : (place + 1) * size] = term
                else:
                    term = term + total[:, place * size : (place + 1) * size]
                    keep_ref[:, columns] = term[:rows]
                    send_ref[:, columns] = term[rows:].astype(bf16)


def ff_far_kernel(
    me_ref,
    x2_ref,
    x3_ref,
    grad2_ref,
    grad3_ref,
    w0,
    w1,
    w2y,
    w2x,
    w3y,
    w3x,
    down_near,
    hidden_ref,
    pair_ref,
    x_scr,
    pair_scr,
    factor_scr,
):
    side = me_ref[1] % 2
    half = down_near.shape[0]
    main = half // HEAD * HEAD
    rows = x2_ref.shape[0]
    put_rows(x_scr, True, me_ref, x2_ref, x3_ref)
    for index, far in enumerate(((w2y, w3y), (w2x, w3x))):

        @pl.when(side == index)
        def _(far=far):
            pair_scr[...] = pair_product(x_scr, (w0[0], w1[0], far[0][...], far[1][...]))

    (swish, slope, hidden), edge_factor, edge_hidden = gate_parts(pair_scr[...], half)
    put_hidden(hidden_ref, hidden, edge_hidden, main)
    factor_scr[:, :main] = slope.astype(bf16)
    factor_scr[:, main : 2 * main] = swish.astype(bf16)
    factor_scr[:, 2 * main :] = edge_factor.astype(bf16)
    put_rows(x_scr, False, me_ref, grad2_ref, grad3_ref)
    hidden_grad = dot_nt(x_scr[...], down_near[...])
    for row in range(2):
        where = slice(row * rows, (row + 1) * rows)
        put_pair_grad(pair_ref.at[row], hidden_grad[where], factor_scr.at[where], half)


def piece_height(me_ref, ahead):
    size = 4
    return (me_ref[1] // 2 + ahead) % size


def piece_owner(me_ref, other_x, ahead):
    return (me_ref[1] % 2 ^ other_x) + 2 * piece_height(me_ref, ahead)


def spread_rows(me_ref, total, refs, columns=slice(None), contiguous=False):
    across = len(refs)
    for other_x, ref in enumerate(refs):
        shards, piece_rows = ref.shape[1:3]
        for ahead in range(4):
            owner = (
                piece_owner(me_ref, other_x, ahead) if across == 2 else piece_height(me_ref, ahead)
            )
            for shard in range(shards):
                block = owner * shards + shard if contiguous else shard * 4 * across + owner
                start = pl.multiple_of(block * piece_rows, 8)
                ref[ahead, shard, :, columns] = total[pl.ds(start, piece_rows), :].astype(bf16)


def weight_grads_kernel(sources, me_ref, *refs):
    lefts, rights = [], []
    for heads_layout, _ in sources:
        lefts.append(refs[:4])
        count = 1 if heads_layout else 2
        rights.append(refs[4 : 4 + count])
        refs = refs[4 + count :]
    outs, (left_scr, head_scr), totals = refs[:2], refs[2:4], refs[4:]
    step = pl.program_id(0)
    for (heads_layout, _), left, right, total in zip(sources, lefts, rights, totals, strict=True):
        choose(step, left, left_scr)
        columns = total.shape[1]
        if heads_layout:
            heads = right[0].shape[0] // PLACES
            for head in range(heads):
                head_scr[:, head * HEAD : (head + 1) * HEAD] = right[0][step * heads + head]
        for index in range(PLACES):

            @pl.when(step == index)
            def _(index=index, right=right, total=total, columns=columns, heads_layout=heads_layout):
                if heads_layout:
                    operand = head_scr[...]
                else:
                    operand = right[index // 2][index % 2, :, :columns]
                term = dot_tn(left_scr[...], operand)
                if index == 0:
                    total[...] = term
                else:
                    total[...] += term

    @pl.when(step == PLACES - 1)
    def _():
        first = 0
        for (_, contiguous), total in zip(sources, totals, strict=True):
            columns = slice(first, first + total.shape[1])
            spread_rows(me_ref, total, outs, columns, contiguous)
            first += total.shape[1]


def weight_grads(me, name, expected, sources):
    rows, width = sources[0][0][0].shape
    specs, operands, kinds, columns = [SMEM], [me], [], []
    for lefts, rights, count, contiguous in sources:
        operands += [*lefts, *rights]
        specs += [whole(value.shape) for value in (*lefts, *rights)]
        kinds.append((len(rights) == 1, contiguous))
        columns.append(count)
    piece = (4, PLACES, width // PLACES // 8, sum(columns))
    return pl.pallas_call(
        functools.partial(weight_grads_kernel, tuple(kinds)),
        name=name,
        cost_estimate=cost(expected),
        grid=(PLACES,),
        in_specs=specs,
        out_specs=[whole(piece)] * 2,
        out_shape=[shaped(*piece)] * 2,
        scratch_shapes=[pltpu.VMEM((rows, width), bf16), pltpu.VMEM((rows, 2 * HEAD), bf16)]
        + [pltpu.VMEM((width, count), f32) for count in columns],
        compiler_params=params(48, "arbitrary"),
    )(*operands)


def low_sum(*terms):
    return sum(term.astype(f32) for term in terms).astype(bf16)


def over_z(terms):
    running = low_sum(*terms[3])
    for ahead in (2, 1, 0):
        running = low_sum(*terms[ahead], z_shift(running))
    return running


def spread_piece(piece):
    near, far = [piece], []
    for step in range(3):
        ready = near[-1] if step == 0 else after(near[-1], far[-1])
        far.append(ctx_swap(near[-1], 1))
        near.append(z_shift(ready))
    return near + far + [ctx_swap(after(near[-1], far[-1]), 1)]


def settle_qkv_kernel(me_ref, *refs):
    pieces, outs = refs[:8], refs[8:]
    shards, rows = pieces[0].shape[:2]
    part = outs[0].shape[1] // shards
    for index, ref in enumerate(pieces):
        height = piece_height(me_ref, -(index % 4))
        head = me_ref[1] % 2 ^ (index // 4)
        where = pl.ds(pl.multiple_of(height * rows, rows), rows)
        for shard in range(shards):
            columns = pl.ds(pl.multiple_of(shard * part + head * HEAD, HEAD), HEAD)
            for kind, out in enumerate(outs):
                out[where, columns] = ref[shard, :, kind * HEAD : (kind + 1) * HEAD].astype(f32)


def settle_pair_kernel(me_ref, *refs):
    pieces, outs = refs[:8], refs[8:]
    shards, rows, columns = pieces[0].shape
    half = columns // 2
    for index, ref in enumerate(pieces):
        owner = piece_owner(me_ref, index // 4, -(index % 4))
        where = pl.ds(pl.multiple_of(owner * rows, rows), rows)
        for kind, start, source, size in pair_columns(half):
            for shard in range(shards):
                first = shard * half + start
                outs[kind][where, first : first + size] = ref[
                    shard, :, source : source + size
                ].astype(f32)


def settle_turned_kernel(me_ref, *refs):
    pieces, (down_ref, out_ref) = refs[:8], refs[8:]
    shards, rows = pieces[0].shape[:2]
    half = down_ref.shape[0]
    for index, ref in enumerate(pieces):
        owner = piece_owner(me_ref, index // 4, -(index % 4))
        stretch = jnp.concatenate([ref[shard].astype(f32) for shard in range(shards)], axis=0)
        columns = pl.ds(pl.multiple_of(owner * shards * rows, shards * rows), shards * rows)
        down_ref[:, columns] = stretch[:, :half].T
        out_ref[:, columns] = stretch[:, half:].T


def settle(kernel, name, me, pieces, outs):
    return pl.pallas_call(
        kernel,
        name=name,
        grid=(1,),
        in_specs=[SMEM] + [whole(pieces[0].shape)] * 8,
        out_specs=[whole(out) for out in outs],
        out_shape=[shaped(*out, kind=f32) for out in outs],
        cost_estimate=cost(4),
        compiler_params=params(40),
    )(me, *pieces)


def shaped(*shape, kind=bf16):
    return jax.ShapeDtypeStruct(shape, kind)


def rope_tables(position):
    half = HEAD // 2
    frequencies = rope_base ** (-2.0 * jnp.arange(half, dtype=f32) / HEAD)
    angles = position.astype(f32)[..., None] * frequencies
    cosine, sine = jnp.cos(angles), jnp.sin(angles)
    return (
        jnp.concatenate([cosine, cosine], axis=-1),
        jnp.concatenate([-sine, sine], axis=-1),
    )


def pair_shards(
    block_in,
    out_grad,
    w_query,
    w_key,
    w_value,
    w_out,
    norm_one,
    norm_two,
    w_gate,
    w_up,
    w_down,
    norm_three,
    norm_four,
    prompt_len,
    cont_len,
    group_ids,
    cont_ids,
):
    rows, width = block_in.shape[1:]
    ctx_size = lax.axis_size("ctx")
    heads = width // HEAD // PLACES
    part = heads * HEAD
    prompt = P_DEV * ctx_size
    prompt_chunks, cont_chunks = prompt // rows, CONT // rows
    ff_part = w_down.shape[0]
    my_row = lax.axis_index("fsdp")
    my_chunk = lax.axis_index("ctx")
    me = jnp.stack([my_row, my_chunk]).astype(jnp.int32)
    groups, slots = cont_ids.shape
    gain_one, gain_two, gain_three, gain_four = (
        gain[None, :] for gain in (norm_one, norm_two, norm_three, norm_four)
    )
    x_own, grad_own = block_in[0], out_grad[0]
    row_spec, gain_spec = whole((rows, width)), whole((1, width))
    full_row, low_row, gain_row = (
        shaped(rows, width, kind=f32),
        shaped(rows, width),
        shaped(1, width, kind=f32),
    )

    x_across = y_swap(x_own)
    qkv_split = pl.pallas_call(
        split_qkv_kernel,
        name="split_qkv",
        cost_estimate=cost(2),
        grid=(1,),
        in_specs=[SMEM] + [whole((rows, width))] * 3,
        out_specs=[whole((rows, 3 * part))] * 4,
        out_shape=[shaped(rows, 3 * part)] * 4,
        compiler_params=params(16),
    )(me, w_query, w_key, w_value)
    w_qkv = [
        qkv_split[0],
        core_swap(qkv_split[1]),
        y_swap(qkv_split[2]),
        y_swap(core_swap(qkv_split[3])),
    ]
    x_beside = core_swap(x_own)
    x_all = [x_own, x_beside, x_across, core_swap(x_across)]

    row_of = my_row ^ jnp.arange(PLACES, dtype=jnp.int32)
    group_range = jnp.arange(groups, dtype=jnp.int32)
    slot_range = jnp.arange(slots, dtype=jnp.int32)
    pick_row = row_of[:, None] == group_range[None, :]
    group_of = jnp.sum(jnp.where(pick_row, group_ids[None, :], 0), axis=1)
    pick_group = group_of[:, None] == group_range[None, :]
    prompt_of = jnp.sum(jnp.where(pick_group, prompt_len[None, :], 0), axis=1)
    lens_of = jnp.sum(jnp.where(pick_group[:, :, None], cont_len[None], 0), axis=1)
    ids_of = jnp.sum(jnp.where(pick_row[:, :, None], cont_ids[None], 0), axis=1)
    slot_lens = jnp.sum(
        jnp.where(ids_of[:, :, None] == slot_range, lens_of[:, None, :], 0), axis=2
    )
    pick_pair = jnp.arange(PLACES, dtype=jnp.int32) == my_chunk // heads
    pair_prompt = jnp.sum(jnp.where(pick_pair, prompt_of, 0))
    pair_lens = jnp.sum(jnp.where(pick_pair[:, None], slot_lens, 0), axis=0)
    info = jnp.concatenate([pair_prompt[None], pair_lens])

    def positions(slot, prompt_size):
        return jnp.where(slot >= prompt, prompt_size + (slot - prompt) % CONT, slot)

    own_slots = my_chunk * rows + jnp.arange(rows, dtype=jnp.int32)
    cos_own, sin_own = rope_tables(positions(own_slots[None, :], prompt_of[:, None]))
    all_slots = jnp.arange(rows * ctx_size, dtype=jnp.int32).reshape(ctx_size, rows)
    cos_all, sin_all = rope_tables(positions(all_slots, pair_prompt))

    w_qkv = after(w_qkv, cos_own, sin_own, cos_all, sin_all)

    ff_blocks, ff_block = (2, rows, 2 * ff_part), (rows, 2 * ff_part)
    split_shapes = [ff_blocks, ff_block, ff_blocks, ff_block, (ff_part, width // 2)]
    ff_own, ff_own_sent, ff_beside, ff_beside_sent, down_sent = pl.pallas_call(
        split_ff_kernel,
        name="split_ff",
        cost_estimate=cost(3),
        grid=(1,),
        in_specs=[SMEM] + [whole(w_gate.shape)] * 2 + [whole((ff_part, width))],
        out_specs=[whole(shape) for shape in split_shapes],
        out_shape=[shaped(*shape) for shape in split_shapes],
        compiler_params=params(32),
    )(me, w_gate, w_up, w_down)
    w_qkv, x_all, ff_own_sent, ff_beside_sent = tie(w_qkv, x_all, ff_own_sent, ff_beside_sent)
    w_ff_beside = core_swap(ff_beside)
    ff_beside_sent = core_swap(ff_beside_sent)
    far_y = y_swap(ff_own_sent)
    far_x = ctx_swap(far_y, 1)
    corner_y = y_swap(after(ff_beside_sent, far_y))
    corner_x = ctx_swap(corner_y, 1)
    down_y = y_swap(after(down_sent, corner_y))
    down_x = ctx_swap(down_y, 1)
    w_out_far = y_swap(after(w_out, down_y))

    piece = (heads, 3, rows, HEAD)
    qkv = pl.pallas_call(
        project_kernel,
        name="project",
        cost_estimate=cost(4),
        grid=(PLACES,),
        in_specs=[SMEM]
        + [row_spec] * 4
        + [gain_spec]
        + [whole((rows, 3 * part))] * 4
        + [pl.BlockSpec((1, rows, HEAD), lambda t: (t, 0, 0))] * 2,
        out_specs=pl.BlockSpec(piece, lambda t: (t, 0, 0, 0)),
        out_shape=shaped(PLACES * heads, 3, rows, HEAD),
        scratch_shapes=[pltpu.VMEM((rows, width), bf16)] * 2,
        compiler_params=params(24, "arbitrary"),
    )(me, *x_all, gain_one, *w_qkv, cos_own, sin_own)
    qkv = lax.all_to_all(qkv, "ctx", 0, 0, tiled=True)
    x_stack = jnp.stack(x_all)
    qkv = after(qkv, far_y, x_stack)

    qkv_shape, head_shape = (ctx_size, 3, rows, HEAD), (ctx_size, rows, HEAD)
    mixed, exact, log_total = pl.pallas_call(
        functools.partial(attend_kernel, prompt_chunks, cont_chunks),
        name="attend",
        cost_estimate=cost(15),
        grid=(ctx_size,),
        in_specs=[SMEM, whole(qkv_shape)],
        out_specs=[whole(head_shape), whole(head_shape), whole((ctx_size, 1, rows))],
        out_shape=[
            shaped(*head_shape),
            shaped(*head_shape, kind=f32),
            shaped(ctx_size, 1, rows, kind=f32),
        ],
        compiler_params=params(32, "arbitrary"),
    )(info, qkv)
    mixed = after(mixed, far_x, corner_x, down_y)
    attended = lax.all_to_all(mixed, "ctx", 0, 0, tiled=True)
    attended = after(attended, down_x, w_out_far)
    attended_far = y_swap(attended[2 * heads :])

    two_heads = (2 * heads, rows, HEAD)
    keep, send = pl.pallas_call(
        mix_out_kernel,
        name="mix_out",
        cost_estimate=cost(2),
        grid=(1,),
        in_specs=[whole((PLACES * heads, rows, HEAD)), whole(two_heads)] + [whole((part, width))] * 2,
        out_specs=[row_spec] * 2,
        out_shape=[full_row, low_row],
        compiler_params=params(16),
    )(attended, attended_far, w_out, w_out_far)

    branch, middle, ff_input = pl.pallas_call(
        middle_kernel,
        name="middle",
        cost_estimate=cost(2),
        grid=(1,),
        in_specs=[row_spec] * 3 + [gain_spec] * 2,
        out_specs=[row_spec] * 3,
        out_shape=[full_row, full_row, low_row],
        compiler_params=params(24),
    )(keep, core_swap(send), x_own, gain_two, gain_three)
    ff_input_beside = core_swap(ff_input)
    ff_input_far = far_rows(ff_input)
    x_pair = lax.all_to_all(
        after(x_stack, attended),
        "ctx",
        0,
        0,
        tiled=True,
        axis_index_groups=[[x + 2 * z for z in range(ctx_size // 2)] for x in range(2)],
    )

    padded = pl.cdiv(ff_part, HEAD) * HEAD
    far_pairs = [far_y, far_x, corner_y, corner_x]
    far_weights = far_pairs + [w_down, down_y, down_x]

    def turned(index, me_ref):
        return index ^ (me_ref[1] % 2)

    def grid_whole(shape):
        return pl.BlockSpec(shape, lambda b, me_ref: (0,) * len(shape))

    def ff_call(kernel, name, expected, more_in, outs, scratch):
        specs = (
            [grid_whole((rows, width))] * 2
            + [pl.BlockSpec((1,) + ff_block, lambda b, me_ref: (turned(b, me_ref), 0, 0))] * 2
            + [grid_whole(weight.shape) for weight in far_weights]
            + more_in
        )
        return pl.pallas_call(
            kernel,
            name=name,
            cost_estimate=cost(expected),
            grid_spec=pltpu.PrefetchScalarGridSpec(
                num_scalar_prefetch=1,
                grid=(2,),
                in_specs=specs,
                out_specs=[spec for spec, _ in outs],
                scratch_shapes=scratch,
            ),
            out_shape=[shape for _, shape in outs],
            compiler_params=params(56, "arbitrary"),
        )

    both = 2 * rows
    padded = pl.cdiv(ff_part, HEAD) * HEAD
    saved = pl.BlockSpec((1, both, 2 * ff_part), lambda b, me_ref: (b, 0, 0))
    grid_row = grid_whole((rows, width))
    hidden_shape, pair_shape = (2, rows, padded), (2, rows, 2 * ff_part)
    keep, send, ff_saved, hidden = ff_call(
        ff_kernel,
        "ff",
        9,
        [],
        [
            (grid_row, full_row),
            (grid_row, low_row),
            (saved, shaped(2, both, 2 * ff_part)),
            (grid_whole(hidden_shape), shaped(*hidden_shape)),
        ],
        [
            pltpu.VMEM((both, width), bf16),
            pltpu.VMEM((both, 2 * ff_part), f32),
            pltpu.VMEM((both, padded), bf16),
            pltpu.VMEM((both, width), f32),
        ],
    )(me, ff_input, ff_input_beside, ff_own, w_ff_beside, *far_weights)

    send = after(send, ff_input_far[0])
    block_out, ff_grad, part_four = pl.pallas_call(
        turnaround_kernel,
        name="turnaround",
        cost_estimate=cost(2),
        grid=(1,),
        in_specs=[row_spec] * 4 + [gain_spec],
        out_specs=[row_spec, row_spec, gain_spec],
        out_shape=[low_row, low_row, gain_row],
        compiler_params=params(24),
    )(keep, core_swap(send), middle, grad_own, gain_four)

    ff_grad_beside = core_swap(ff_grad)
    ff_grad_far = far_rows(ff_grad)
    keep, send, pair_grad = ff_call(
        ff_back_kernel,
        "ff_back",
        9,
        [saved],
        [
            (grid_row, full_row),
            (grid_row, low_row),
            (grid_whole(pair_shape), shaped(*pair_shape)),
        ],
        [
            pltpu.VMEM((both, width), bf16),
            pltpu.VMEM((both, ff_part), f32),
            pltpu.VMEM((both, 2 * ff_part), bf16),
            pltpu.VMEM((both, width), f32),
        ],
    )(me, ff_grad, ff_grad_beside, ff_own, w_ff_beside, *far_weights, ff_saved)
    x_pair_other = ctx_swap(x_pair, 1)
    send = after(send, ff_grad_far[0])

    middle_grad, branch_grad, part_two, part_three = pl.pallas_call(
        branch_back_kernel,
        name="branch_back",
        cost_estimate=cost(2),
        grid=(1,),
        in_specs=[row_spec] * 5 + [gain_spec] * 2,
        out_specs=[row_spec, row_spec, gain_spec, gain_spec],
        out_shape=[full_row, low_row, gain_row, gain_row],
        compiler_params=params(24),
    )(keep, core_swap(send), middle, branch, grad_own, gain_two, gain_three)
    branch_grad_beside = core_swap(branch_grad)

    heads_near, heads_far = pl.pallas_call(
        heads_back_kernel,
        name="heads_back",
        cost_estimate=cost(2),
        grid=(1,),
        in_specs=[row_spec] * 2 + [whole((part, width))] * 2,
        out_specs=[whole(two_heads)] * 2,
        out_shape=[shaped(*two_heads)] * 2,
        compiler_params=params(16),
    )(branch_grad, branch_grad_beside, w_out, w_out_far)
    heads_far = y_swap(heads_far)
    ff_input_far, ff_grad_far = after((ff_input_far, ff_grad_far), heads_near)
    branch_grad_across = y_swap(branch_grad)

    near_share = pl.BlockSpec((1,) + ff_block, lambda *_: (0, 0, 0))
    hidden_far, pair_far = pl.pallas_call(
        ff_far_kernel,
        name="ff_far",
        cost_estimate=cost(6),
        grid=(1,),
        in_specs=[SMEM]
        + [row_spec] * 4
        + [near_share] * 2
        + [whole(ff_block)] * 4
        + [whole((ff_part, width))],
        out_specs=[whole(hidden_shape), whole(pair_shape)],
        out_shape=[shaped(*hidden_shape), shaped(*pair_shape)],
        scratch_shapes=[
            pltpu.VMEM((both, width), bf16),
            pltpu.VMEM((both, 2 * ff_part), f32),
            pltpu.VMEM((both, 2 * ff_part), bf16),
        ],
        compiler_params=params(40),
    )(me, *ff_input_far, *ff_grad_far, ff_own, w_ff_beside, *far_pairs, w_down)
    pair_keep, pair_send = weight_grads(
        me,
        "pair_grads",
        7,
        [
            (
                [ff_input, ff_input_beside, *ff_input_far],
                [pair_grad, pair_far],
                2 * ff_part,
                False,
            )
        ],
    )
    pair_over = ctx_swap(pair_send, 1)
    heads_far = after(heads_far, x_pair, pair_send)
    attended_grad = lax.all_to_all(
        jnp.concatenate([heads_near, heads_far]), "ctx", 0, 0, tiled=True
    )
    branch_grad_far = [branch_grad_across, core_swap(branch_grad_across)]
    down_keep, down_send = weight_grads(
        me,
        "down_grads",
        8,
        [
            ([ff_grad, ff_grad_beside, *ff_grad_far], [hidden, hidden_far], ff_part, True),
            ([branch_grad, branch_grad_beside, *branch_grad_far], [attended], part, True),
        ],
    )
    down_over = ctx_swap(down_send, 1)
    attended_grad = after(attended_grad, down_send, x_pair_other)

    pieces = pl.pallas_call(
        functools.partial(attend_back_kernel, prompt_chunks, cont_chunks),
        name="attend_back",
        cost_estimate=cost(18),
        grid=(ctx_size,),
        in_specs=[
            SMEM,
            whole(qkv_shape),
            whole(head_shape),
            whole(head_shape),
            whole((ctx_size, 1, rows)),
            whole(head_shape),
            whole(head_shape),
        ],
        out_specs=whole(qkv_shape),
        out_shape=shaped(*qkv_shape),
        scratch_shapes=[pltpu.VMEM(head_shape, f32), pltpu.VMEM(head_shape, f32)],
        compiler_params=params(40, "arbitrary"),
    )(info, qkv, attended_grad, exact, log_total, cos_all, sin_all)
    qkv_piece = (4, PLACES, rows // 4, 3 * HEAD)
    qkv_keep = pl.pallas_call(
        project_grad_kernel,
        name="project_grad",
        cost_estimate=cost(6),
        grid=(4,),
        in_specs=[SMEM, whole(qkv_shape)] + [whole((4, rows, width))] * 2 + [gain_spec],
        out_specs=whole(qkv_piece),
        out_shape=shaped(*qkv_piece),
        scratch_shapes=[pltpu.VMEM((width, 3 * HEAD), f32)],
        compiler_params=params(32, "arbitrary"),
    )(me, pieces, x_pair, x_pair_other, gain_one)
    pair_over, down_over = after((pair_over, down_over), pieces)
    pair_came = z_shift(low_sum(pair_keep[3], pair_over[3]))
    pair_came = z_shift(low_sum(pair_keep[2], pair_over[2], pair_came))
    qkv_came = z_shift(qkv_keep[3])
    pieces = lax.all_to_all(pieces, "ctx", 0, 0, tiled=True)
    pieces = after(pieces, qkv_keep)

    piece_spec = pl.BlockSpec(piece, lambda t: (t, 0, 0, 0))
    pair_rows = pl.BlockSpec((1, rows, width), lambda t: (t // 2, 0, 0))
    keep, send = pl.pallas_call(
        project_back_kernel,
        name="project_back",
        cost_estimate=cost(5),
        grid=(PLACES,),
        in_specs=[SMEM, piece_spec] + [whole((rows, 3 * part))] * 4,
        out_specs=[pair_rows, pair_rows],
        out_shape=[shaped(2, rows, width)] * 2,
        compiler_params=params(24, "arbitrary"),
    )(me, pieces, *w_qkv)

    received = core_swap(send)
    onward = (keep[1].astype(f32) + received[1].astype(f32)).astype(bf16)
    in_grad, part_one = pl.pallas_call(
        input_back_kernel,
        name="input_back",
        cost_estimate=cost(2),
        grid=(1,),
        in_specs=[pl.BlockSpec((1, rows, width), lambda *_: (0, 0, 0))] * 2
        + [row_spec] * 3
        + [gain_spec],
        out_specs=[row_spec, gain_spec],
        out_shape=[full_row, gain_row],
        compiler_params=params(24),
    )(keep, received, y_swap(onward), x_own, middle_grad, gain_one)

    def shared_rows(piece):
        return lax.all_to_all(piece, "fsdp", 0, 0, tiled=True)

    pair_came, qkv_came, down_over = after((pair_came, qkv_came, down_over), send)
    qkv_came = z_shift(low_sum(qkv_keep[2], qkv_came))
    pair_came = z_shift(low_sum(pair_keep[1], pair_over[1], pair_came))
    qkv_came = z_shift(low_sum(qkv_keep[1], qkv_came))
    pair_piece = shared_rows(low_sum(pair_keep[0], pair_over[0], pair_came))
    qkv_piece = shared_rows(low_sum(qkv_keep[0], qkv_came))
    down_piece = over_z([[down_keep[ahead], down_over[ahead]] for ahead in range(4)])
    query_sum, key_sum, value_sum = settle(
        settle_qkv_kernel, "settle_qkv", me, spread_piece(qkv_piece), [(rows, width)] * 3
    )
    gate_sum, up_sum = settle(
        settle_pair_kernel, "settle_pair", me, spread_piece(pair_piece), [w_gate.shape] * 2
    )
    down_sum, out_sum = settle(
        settle_turned_kernel,
        "settle_turned",
        me,
        spread_piece(down_piece),
        [(ff_part, width), (part, width)],
    )

    gains = jnp.concatenate([part_one, part_two, part_three, part_four])
    for swap in (
        core_swap,
        y_swap,
        functools.partial(ctx_swap, bit=1),
        functools.partial(ctx_swap, bit=2),
        functools.partial(ctx_swap, bit=4),
    ):
        gains = gains + swap(gains)
    return (
        block_out[None],
        in_grad[None],
        query_sum,
        key_sum,
        value_sum,
        out_sum,
        gains[0],
        gains[1],
        gate_sum,
        up_sum,
        down_sum,
        gains[2],
        gains[3],
    )


def solution(mesh):
    fsdp, ctx = mesh.shape["fsdp"], mesh.shape["ctx"]

    def step(*args):
        width, groups = args[0].shape[2], args[0].shape[0]
        heads = width // HEAD
        rows = args[0].shape[1] // ctx
        paired = (
            fsdp == 4
            and groups == fsdp
            and heads == ctx
            and CONT % rows == 0
            and (P_DEV * ctx) % rows == 0
            and width // fsdp == rows
        )
        return jax.shard_map(
            pair_shards if paired else shards,
            mesh=mesh,
            in_specs=IN_SPECS,
            out_specs=OUT_SPECS,
            check_vma=False,
        )(*args)

    return step
```

```python
import functools
import math

import jax
import jax.numpy as jnp
from jax import lax
from jax.experimental import pallas as pl
from jax.experimental.pallas import tpu as pltpu
from jax.sharding import PartitionSpec as P

HEAD = 128
P_DEV = 128
CONT = 512
LOG2E = 1.4426950408889634

eps_norm = 1e-06
rope_base = 50000.0
masked_out = -1e30

bf16 = jnp.bfloat16
f32 = jnp.float32

def rms_norm(values, gain_vec):
    inverse = lax.rsqrt(jnp.mean(values * values, axis=-1, keepdims=True) + eps_norm)
    return (values * inverse * gain_vec, inverse)


def norm_back(values, inverse, gain_vec, upstream):
    weighted = upstream * gain_vec
    inner_mean = jnp.mean(values * weighted, axis=-1, keepdims=True)
    value_grad = inverse * weighted - values * inverse * inverse * inverse * inner_mean
    return (value_grad, jnp.sum(upstream * values * inverse, axis=0))


def rotate(values, position, turn_sign):
    seq_len = values.shape[0]
    half_size = HEAD // 2
    split_heads = values.reshape(seq_len, -1, HEAD)
    frequencies = rope_base ** (-2.0 * jnp.arange(half_size, dtype=jnp.float32) / HEAD)
    angles = position.astype(jnp.float32)[:, None] * frequencies[None, :]
    cosine = jnp.concatenate([jnp.cos(angles), jnp.cos(angles)], axis=-1)[:, None, :]
    sine_part = turn_sign * jnp.concatenate([jnp.sin(angles), jnp.sin(angles)], axis=-1)[:, None, :]
    turned = jnp.concatenate([-split_heads[..., half_size:], split_heads[..., :half_size]], axis=-1)
    return (split_heads * cosine + turned * sine_part).reshape(seq_len, -1)


def token_info(slot_index, prompt, prompt_size, slot_lens):
    in_cont = slot_index >= prompt
    rel_index = jnp.maximum(slot_index - prompt, 0)
    slot_of = jnp.where(in_cont, rel_index // CONT, -1)
    offset = rel_index % CONT
    slot_range = jnp.arange(slot_lens.shape[0], dtype=jnp.int32)
    slot_len = jnp.sum(
        jnp.where(slot_of[:, None] == slot_range[None, :], slot_lens[None, :], 0), axis=1
    )
    token_valid = jnp.where(in_cont, offset < slot_len, slot_index < prompt_size)
    position = jnp.where(in_cont, prompt_size + offset, slot_index)
    return (token_valid, slot_of, position)


def cross_dot(operand, partner):
    return lax.dot_general(
        operand, partner, (((0,), (0,)), ((), ())), preferred_element_type=jnp.float32
    )


def back_dot(operand, partner):
    return lax.dot_general(
        operand, partner, (((1,), (1,)), ((), ())), preferred_element_type=jnp.float32
    )


def keep_same(state):
    return state


def shards(
    block_in,
    out_grad,
    w_query,
    w_key,
    w_value,
    w_out,
    norm_one,
    norm_two,
    w_gate,
    w_up,
    w_down,
    norm_three,
    norm_four,
    prompt_len,
    cont_len,
    group_ids,
    cont_ids,
):
    local_rows = block_in.shape[1]
    model_width = block_in.shape[2]
    ff_width = w_gate.shape[1]
    ctx_size = lax.axis_size("ctx")
    group_rows = local_rows * ctx_size
    prompt = P_DEV * ctx_size
    head_count = model_width // HEAD
    score_scale = 1.0 / math.sqrt(HEAD)
    row_index = lax.axis_index("fsdp")
    groups = group_ids.shape[0]
    slot_count = cont_ids.shape[1]
    group_range = jnp.arange(groups, dtype=jnp.int32)
    own_group = jnp.sum(jnp.where(group_range == row_index, group_ids, 0))
    own_prompt = jnp.sum(jnp.where(group_range == own_group, prompt_len, 0))
    own_lens = jnp.sum(jnp.where((group_range == own_group)[:, None], cont_len, 0), axis=0)
    own_ids = jnp.sum(jnp.where((group_range == row_index)[:, None], cont_ids, 0), axis=0)
    slot_range = jnp.arange(slot_count, dtype=jnp.int32)
    slot_lens = jnp.sum(
        jnp.where(own_ids[:, None] == slot_range[None, :], own_lens[None, :], 0), axis=1
    )
    query_index = lax.axis_index("ctx") * local_rows + jnp.arange(local_rows, dtype=jnp.int32)
    key_index = jnp.arange(group_rows, dtype=jnp.int32)
    query_valid, query_slot, position = token_info(query_index, prompt, own_prompt, slot_lens)
    key_valid, key_slot, unused_pos = token_info(key_index, prompt, own_prompt, slot_lens)
    tokens = block_in[0].astype(jnp.float32)
    full_query, full_key, full_value, full_out = (
        lax.all_gather(w_query, "fsdp", axis=0, tiled=True),
        lax.all_gather(w_key, "fsdp", axis=0, tiled=True),
        lax.all_gather(w_value, "fsdp", axis=0, tiled=True),
        lax.all_gather(w_out, "fsdp", axis=0, tiled=True),
    )
    normed_full, inverse_one = rms_norm(tokens, norm_one)
    normed = normed_full.astype(jnp.bfloat16)
    queries = rotate(
        jnp.dot(normed, full_query, preferred_element_type=jnp.float32), position, 1.0
    ).astype(jnp.bfloat16)
    keys_local = rotate(
        jnp.dot(normed, full_key, preferred_element_type=jnp.float32), position, 1.0
    ).astype(jnp.bfloat16)
    values_local = jnp.dot(normed, full_value, preferred_element_type=jnp.float32).astype(
        jnp.bfloat16
    )
    all_keys, all_values = (
        lax.all_gather(keys_local, "ctx", axis=0, tiled=True),
        lax.all_gather(values_local, "ctx", axis=0, tiled=True),
    )
    key_block = math.gcd(group_rows, 512)
    block_count = group_rows // key_block
    blocks_in = (
        all_keys.reshape(block_count, key_block, head_count, HEAD),
        all_values.reshape(block_count, key_block, head_count, HEAD),
        key_valid.reshape(block_count, key_block),
        key_slot.reshape(block_count, key_block),
        key_index.reshape(block_count, key_block),
    )
    query_heads = queries.reshape(local_rows, head_count, HEAD)

    def mask_of(inputs):
        key_ids = inputs[4]
        return (
            query_valid[:, None]
            & inputs[2][None, :]
            & (key_ids[None, :] <= query_index[:, None])
            & ((key_ids[None, :] < prompt) | (inputs[3][None, :] == query_slot[:, None]))
        )

    def raw_scores(inputs):
        return (
            jnp.einsum("qhd,khd->hqk", query_heads, inputs[0], preferred_element_type=jnp.float32)
            * score_scale
        )

    def running(state_in, inputs):
        allowed = mask_of(inputs)

        def running_visit(state):
            row_top, exp_total = state
            scores = jnp.where(allowed[None], raw_scores(inputs), masked_out)
            new_top = jnp.maximum(row_top, jnp.max(scores, axis=-1, keepdims=True))
            exp_total = exp_total * jnp.exp(row_top - new_top) + jnp.sum(
                jnp.where(allowed[None], jnp.exp(scores - new_top), 0.0), axis=-1, keepdims=True
            )
            return (new_top, exp_total)

        return (lax.cond(jnp.any(allowed), running_visit, keep_same, state_in), None)

    start_top = jnp.full((head_count, local_rows, 1), -jnp.inf, jnp.float32)
    start_total = jnp.zeros((head_count, local_rows, 1), jnp.float32)
    (row_top, exp_total), unused = lax.scan(running, (start_top, start_total), blocks_in)
    has_keys = exp_total > 0.0
    log_total = jnp.where(has_keys, row_top + jnp.log(jnp.where(has_keys, exp_total, 1.0)), 0.0)

    def probs_of(inputs, allowed):
        return jnp.where(allowed[None], jnp.exp(raw_scores(inputs) - log_total), 0.0)

    def mix_step(accumulated, inputs):
        allowed = mask_of(inputs)

        def mix_visit(total):
            attn_probs = probs_of(inputs, allowed).astype(jnp.bfloat16)
            return total + jnp.einsum(
                "hqk,khd->qhd", attn_probs, inputs[1], preferred_element_type=jnp.float32
            )

        return (lax.cond(jnp.any(allowed), mix_visit, keep_same, accumulated), None)

    mixture, unused = lax.scan(
        mix_step, jnp.zeros((local_rows, head_count, HEAD), jnp.float32), blocks_in
    )
    valid_col = query_valid[:, None].astype(jnp.float32)
    attended = (mixture.reshape(local_rows, model_width) * valid_col).astype(jnp.bfloat16)
    branch = jnp.dot(attended, full_out, preferred_element_type=jnp.float32)
    branch_normed, inverse_two = rms_norm(branch, norm_two)
    middle = tokens + branch_normed
    full_gate, full_up, full_down = (
        lax.all_gather(w_gate, "fsdp", axis=0, tiled=True),
        lax.all_gather(w_up, "fsdp", axis=0, tiled=True),
        lax.all_gather(w_down, "fsdp", axis=0, tiled=True),
    )
    ff_normed, inverse_three = rms_norm(middle, norm_three)
    ff_input = ff_normed.astype(jnp.bfloat16)
    gate_pre = jnp.dot(ff_input, full_gate, preferred_element_type=jnp.float32)
    upward = jnp.dot(ff_input, full_up, preferred_element_type=jnp.float32)
    gate_sig = jax.nn.sigmoid(gate_pre)
    swish_out = gate_pre * gate_sig
    hidden = (swish_out * upward).astype(jnp.bfloat16)
    ff_out = jnp.dot(hidden, full_down, preferred_element_type=jnp.float32)
    out_normed, inverse_four = rms_norm(ff_out, norm_four)
    result = middle + out_normed
    upstream = out_grad[0].astype(jnp.float32)
    ff_out_full, grad_norm_four = norm_back(ff_out, inverse_four, norm_four, upstream)
    ff_out_grad = ff_out_full.astype(jnp.bfloat16)
    hidden_grad = back_dot(ff_out_grad, full_down)
    up_grad = (hidden_grad * swish_out).astype(jnp.bfloat16)
    gate_grad = (hidden_grad * upward * gate_sig * (1.0 + gate_pre * (1.0 - gate_sig))).astype(
        jnp.bfloat16
    )
    ff_in_grad = back_dot(gate_grad, full_gate) + back_dot(up_grad, full_up)
    middle_part, grad_norm_three = norm_back(middle, inverse_three, norm_three, ff_in_grad)
    middle_grad = upstream + middle_part
    branch_full, grad_norm_two = norm_back(branch, inverse_two, norm_two, middle_grad)
    branch_grad = branch_full.astype(jnp.bfloat16)
    attended_grad = back_dot(branch_grad, full_out).astype(jnp.bfloat16) * valid_col.astype(
        jnp.bfloat16
    )
    grad_heads = attended_grad.reshape(local_rows, head_count, HEAD)

    def delta_step(accumulated, inputs):
        allowed = mask_of(inputs)

        def delta_visit(total):
            attn_probs = probs_of(inputs, allowed)
            prob_grad = jnp.einsum(
                "qhd,khd->hqk", grad_heads, inputs[1], preferred_element_type=jnp.float32
            )
            return total + jnp.sum(attn_probs * prob_grad, axis=-1, keepdims=True)

        return (lax.cond(jnp.any(allowed), delta_visit, keep_same, accumulated), None)

    row_delta, unused = lax.scan(
        delta_step, jnp.zeros((head_count, local_rows, 1), jnp.float32), blocks_in
    )
    zero_part = jnp.zeros((key_block, head_count, HEAD), jnp.float32)

    def grad_step(accumulated, inputs):
        allowed = mask_of(inputs)

        def grad_visit(total):
            attn_probs = probs_of(inputs, allowed)
            prob_grad = jnp.einsum(
                "qhd,khd->hqk", grad_heads, inputs[1], preferred_element_type=jnp.float32
            )
            score_grad = (attn_probs * (prob_grad - row_delta)).astype(jnp.bfloat16)
            total = total + jnp.einsum(
                "hqk,khd->qhd", score_grad, inputs[0], preferred_element_type=jnp.float32
            )
            key_part = jnp.einsum(
                "hqk,qhd->khd", score_grad, query_heads, preferred_element_type=jnp.float32
            )
            value_part = jnp.einsum(
                "hqk,qhd->khd",
                attn_probs.astype(jnp.bfloat16),
                grad_heads,
                preferred_element_type=jnp.float32,
            )
            return (total, (key_part, value_part))

        def skip(total):
            return (total, (zero_part, zero_part))

        return lax.cond(jnp.any(allowed), grad_visit, skip, accumulated)

    query_acc, (key_parts, value_parts) = lax.scan(
        grad_step, jnp.zeros((local_rows, head_count, HEAD), jnp.float32), blocks_in
    )
    key_terms = key_parts.reshape(group_rows, model_width) * score_scale
    value_terms = value_parts.reshape(group_rows, model_width)
    key_sum, value_sum = (
        lax.psum_scatter(
            key_terms.astype(jnp.bfloat16), "ctx", scatter_dimension=0, tiled=True
        ).astype(jnp.float32),
        lax.psum_scatter(
            value_terms.astype(jnp.bfloat16), "ctx", scatter_dimension=0, tiled=True
        ).astype(jnp.float32),
    )
    query_grad = rotate(
        query_acc.reshape(local_rows, model_width) * score_scale, position, -1.0
    ).astype(jnp.bfloat16)
    key_grad = rotate(key_sum, position, -1.0).astype(jnp.bfloat16)
    value_grad = value_sum.astype(jnp.bfloat16)
    normed_grad = (
        back_dot(query_grad, full_query)
        + back_dot(key_grad, full_key)
        + back_dot(value_grad, full_value)
    )
    input_part, grad_norm_one = norm_back(tokens, inverse_one, norm_one, normed_grad)
    input_grad = middle_grad + input_part
    wide_pairs = (
        (normed, query_grad),
        (normed, key_grad),
        (normed, value_grad),
        (attended, branch_grad),
        (ff_input, gate_grad),
        (ff_input, up_grad),
    )

    def wide_term(selector):
        return jnp.concatenate(
            [cross_dot(selector(operand), partner) for operand, partner in wide_pairs], axis=1
        )

    wide_local = lax.psum_scatter(
        wide_term(lambda operand: operand).astype(jnp.bfloat16),
        "fsdp",
        scatter_dimension=0,
        tiled=True,
    )
    ff_local = lax.psum_scatter(
        cross_dot((lambda operand: operand)(hidden), ff_out_grad).astype(jnp.bfloat16),
        "fsdp",
        scatter_dimension=0,
        tiled=True,
    )
    wide_sum, ff_sum = (
        lax.psum(wide_local, "ctx").astype(jnp.float32),
        lax.psum(ff_local, "ctx").astype(jnp.float32),
    )
    gain_sums = lax.psum(
        jnp.stack([grad_norm_one, grad_norm_two, grad_norm_three, grad_norm_four]), ("ctx", "fsdp")
    )
    edge_two = 2 * model_width
    edge_three = 3 * model_width
    edge_four = 4 * model_width
    edge_five = 4 * model_width + ff_width
    return (
        result.astype(jnp.bfloat16)[None],
        input_grad[None],
        wide_sum[:, :model_width],
        wide_sum[:, model_width:edge_two],
        wide_sum[:, edge_two:edge_three],
        wide_sum[:, edge_three:edge_four],
        gain_sums[0],
        gain_sums[1],
        wide_sum[:, edge_four:edge_five],
        wide_sum[:, edge_five:],
        ff_sum,
        gain_sums[2],
        gain_sums[3],
    )


IN_SPECS = (
    (P("fsdp", "ctx", None),) * 2
    + (P("fsdp", None),) * 4
    + (P(), P())
    + (P("fsdp", None),) * 3
    + (P(),) * 6
)
OUT_SPECS = (
    (P("fsdp", "ctx", None),) * 2
    + (P("fsdp", None),) * 4
    + (P(), P())
    + (P("fsdp", None),) * 3
    + (P(), P())
)


MIB = 1 << 20
PLACES = 4


def core_swap(values):
    return lax.ppermute(values, "fsdp", [(i, i ^ 1) for i in range(4)])


def y_swap(values):
    return lax.ppermute(values, "fsdp", [(i, i ^ 2) for i in range(4)])


def ctx_swap(values, bit):
    size = lax.axis_size("ctx")
    return lax.ppermute(values, "ctx", [(i, i ^ bit) for i in range(size)])


def z_shift(values):
    size = lax.axis_size("ctx")
    return lax.ppermute(values, "ctx", [(i, (i + 2) % size) for i in range(size)])


def tie(*values):
    return lax.optimization_barrier(values)


def after(value, *others):
    return lax.optimization_barrier((value, others))[0]


def far_rows(own):
    across = y_swap(own)
    return across, core_swap(across)


def params(limit_mib, *semantics):
    return pltpu.CompilerParams(
        dimension_semantics=semantics or None, vmem_limit_bytes=limit_mib * MIB
    )


def cost(microseconds):
    return pl.CostEstimate(flops=int(microseconds * 1e6), bytes_accessed=0, transcendentals=0)


def whole(shape):
    return pl.BlockSpec(shape, lambda *_: (0,) * len(shape))


SMEM = pl.BlockSpec(memory_space=pltpu.SMEM)


def dot_nn(a, b):
    return lax.dot_general(a, b, (((1,), (0,)), ((), ())), preferred_element_type=f32)


def dot_nt(a, b):
    return lax.dot_general(a, b, (((1,), (1,)), ((), ())), preferred_element_type=f32)


def dot_tn(a, b):
    return lax.dot_general(a, b, (((0,), (0,)), ((), ())), preferred_element_type=f32)


def inverse_rms(values):
    return lax.rsqrt(jnp.mean(values * values, axis=-1, keepdims=True) + eps_norm)


def turn(values, cosine, sine):
    return values * cosine + pltpu.roll(values, HEAD // 2, 1) * sine


def choose(step, refs, target):
    for index, ref in enumerate(refs):

        @pl.when(step == index)
        def _(ref=ref):
            target[...] = ref[...]


def columns_of(me_ref, place, rows):
    return pl.ds(pl.multiple_of((me_ref[0] ^ place) * rows, rows), rows)


def split_qkv_kernel(me_ref, q_ref, k_ref, v_ref, *out_refs):
    part = out_refs[0].shape[1] // 3
    for place, out_ref in enumerate(out_refs):
        for kind, ref in enumerate((q_ref, k_ref, v_ref)):
            out_ref[:, kind * part : (kind + 1) * part] = ref[:, columns_of(me_ref, place, part)]


def pair_columns(half):
    main = half // HEAD * HEAD
    rest = half - main
    return (
        (0, 0, 0, main),
        (1, 0, main, main),
        (0, main, 2 * main, rest),
        (1, main, 2 * main + rest, rest),
    )


def split_ff_kernel(
    me_ref, gate_ref, up_ref, own_ref, own_sent, beside_ref, beside_sent
):
    half = own_ref.shape[-1] // 2
    for me in range(PLACES):

        @pl.when(me_ref[0] == me)
        def _(me=me):
            for place in range(PLACES):
                target = own_ref if place % 2 == 0 else beside_ref
                for kind, start, where, size in pair_columns(half):
                    first = (me ^ place) * half + start
                    target[place // 2, :, where : where + size] = (gate_ref, up_ref)[kind][
                        :, first : first + size
                    ]

    side = me_ref[1] % 2
    own_sent[...] = own_ref[1 - side]
    beside_sent[...] = beside_ref[1 - side]


def project_kernel(
    me_ref, x0, x1, x2, x3, gain_ref, w0, w1, w2, w3, cos_ref, sin_ref, out_ref, x_scr, normed_scr
):
    choose(pl.program_id(0), (x0, x1, x2, x3), x_scr)
    x = x_scr[...].astype(f32)
    normed_scr[...] = (x * inverse_rms(x) * gain_ref[...]).astype(bf16)
    rows = w0.shape[0]
    product = sum(
        dot_nn(normed_scr[:, columns_of(me_ref, place, rows)], w[...])
        for place, w in enumerate((w0, w1, w2, w3))
    )
    heads = out_ref.shape[0]
    for kind in range(3):
        for head in range(heads):
            start = (kind * heads + head) * HEAD
            part = product[:, start : start + HEAD]
            if kind < 2:
                part = turn(part, cos_ref[0], sin_ref[0])
            out_ref[head, kind] = part.astype(bf16)


def block_facts(block, rows, prompt_blocks, cont_blocks, info_ref):
    beyond = jnp.maximum(block - prompt_blocks, 0)
    in_cont = block >= prompt_blocks
    slot = beyond // cont_blocks
    first = jnp.where(in_cont, prompt_blocks + slot * cont_blocks, 0)
    ahead = jnp.where(in_cont, prompt_blocks, 0)
    start = jnp.where(in_cont, beyond % cont_blocks, block) * rows
    limit = jnp.where(in_cont, info_ref[1 + slot], info_ref[0])
    return first, ahead, start, limit


def visit_blocks(visit, block, rows, first, ahead, info_ref, state):
    key_place = lax.broadcasted_iota(jnp.int32, (rows, rows), 0)
    query_place = lax.broadcasted_iota(jnp.int32, (rows, rows), 1)
    key_row = lax.broadcasted_iota(jnp.int32, (rows, 1), 0)

    def prompt_visit(key_block, state):
        bias = jnp.where(key_block * rows + key_row < info_ref[0], 0.0, masked_out)
        return visit(key_block, bias, False, state)

    state = visit(block, jnp.where(key_place <= query_place, 0.0, masked_out), True, state)
    state = lax.fori_loop(0, ahead, prompt_visit, state)
    return lax.fori_loop(
        first, block, lambda key_block, state: visit(key_block, 0.0, False, state), state
    )


def attend_kernel(span, prompt_blocks, cont_blocks, info_ref, qkv_ref, out_ref, exact_ref, lse_ref):
    block = pl.program_id(0)
    small = qkv_ref.shape[2]
    rows = small * span
    scale = LOG2E / math.sqrt(HEAD)

    def take(block, kind):
        return qkv_ref[pl.ds(block * span, span), kind].reshape(rows, HEAD)

    query = take(block, 0)
    first, ahead, start, limit = block_facts(block, rows, prompt_blocks, cont_blocks, info_ref)

    def visit(key_block, bias, _, state):
        top, total, mixed = state
        scores = dot_nt(take(key_block, 1), query) * scale + bias
        new_top = jnp.maximum(top, jnp.max(scores, axis=0, keepdims=True))
        weights = jnp.exp2(scores - new_top)
        shrink = jnp.exp2(top - new_top)
        total = total * shrink + jnp.sum(weights, axis=0, keepdims=True)
        mixed = mixed * shrink + dot_tn(take(key_block, 2), weights.astype(bf16))
        return new_top, total, mixed

    state = (
        jnp.full((1, rows), -1e38, f32),
        jnp.zeros((1, rows), f32),
        jnp.zeros((HEAD, rows), f32),
    )
    top, total, mixed = visit_blocks(visit, block, rows, first, ahead, info_ref, state)
    valid = start + lax.broadcasted_iota(jnp.int32, (1, rows), 1) < limit
    settled = jnp.where(valid, mixed / total, 0.0).T.reshape(span, small, HEAD)
    out_ref[pl.ds(block * span, span)] = settled.astype(bf16)
    exact_ref[pl.ds(block * span, span)] = settled
    lse_ref[block] = top + jnp.log2(total)


def attend_back_kernel(
    span,
    prompt_blocks,
    cont_blocks,
    info_ref,
    qkv_ref,
    grad_ref,
    exact_ref,
    lse_ref,
    cos_ref,
    sin_ref,
    out_ref,
    key_sum,
    value_sum,
):
    block = pl.program_id(0)
    blocks = pl.num_programs(0)
    small = qkv_ref.shape[2]
    rows = small * span
    scale = LOG2E / math.sqrt(HEAD)

    def at(block):
        return pl.ds(block * span, span)

    def flat(values):
        return values.reshape(rows, HEAD)

    def split(values):
        return values.reshape(span, small, HEAD)

    query = flat(qkv_ref[at(block), 0])
    first, ahead, start, limit = block_facts(block, rows, prompt_blocks, cont_blocks, info_ref)
    valid = start + lax.broadcasted_iota(jnp.int32, (rows, 1), 0) < limit
    grad_full = jnp.where(valid, flat(grad_ref[at(block)]).astype(f32), 0.0)
    grad = grad_full.astype(bf16)
    delta = jnp.sum((grad_full * flat(exact_ref[at(block)])).T, axis=0, keepdims=True)
    log_total = lse_ref[block]

    def visit(key_block, bias, fresh, query_sum):
        key = flat(qkv_ref[at(key_block), 1])
        scores = dot_nt(key, query) * scale + bias
        weights = jnp.exp2(scores - log_total)
        weight_grad = dot_nt(flat(qkv_ref[at(key_block), 2]), grad)
        score_grad = (weights * (weight_grad - delta)).astype(bf16)
        value_term = dot_nn(weights.astype(bf16), grad)
        key_term = dot_nn(score_grad, query)
        if fresh:
            value_sum[key_block] = value_term
            key_sum[key_block] = key_term
        else:
            value_sum[key_block] += value_term
            key_sum[key_block] += key_term
        return query_sum + dot_tn(key, score_grad)

    query_sum = visit_blocks(
        visit, block, rows, first, ahead, info_ref, jnp.zeros((HEAD, rows), f32)
    )
    back = 1.0 / math.sqrt(HEAD)

    def unturn(values, block):
        return split(turn(values * back, flat(cos_ref[at(block)]), -flat(sin_ref[at(block)])).astype(bf16))

    out_ref[at(block), 0] = unturn(query_sum.T, block)

    @pl.when(block == blocks - 1)
    def _():
        @pl.loop(0, blocks)
        def _(key_block):
            out_ref[at(key_block), 1] = unturn(key_sum[key_block], key_block)
            out_ref[at(key_block), 2] = split(value_sum[key_block].astype(bf16))


def mix_out_kernel(near_ref, far_ref, w_near_ref, w_far_ref, keep_ref, send_ref):
    heads = near_ref.shape[0] // PLACES
    for step, out_ref in enumerate((keep_ref, send_ref)):
        total = 0.0
        for ref, w_ref in ((near_ref, w_near_ref), (far_ref, w_far_ref)):
            both = jnp.concatenate([ref[step * heads + j] for j in range(heads)], axis=1)
            total = total + dot_nn(both, w_ref[...])
        out_ref[...] = total.astype(out_ref.dtype)


def heads_back_kernel(own_ref, beside_ref, w_near_ref, w_far_ref, near_ref, far_ref):
    heads = near_ref.shape[0] // 2
    for step, ref in enumerate((own_ref, beside_ref)):
        for w_ref, out_ref in ((w_near_ref, near_ref), (w_far_ref, far_ref)):
            both = dot_nt(ref[...], w_ref[...]).astype(bf16)
            for head in range(heads):
                out_ref[step * heads + head] = both[:, head * HEAD : (head + 1) * HEAD]


def project_back_kernel(me_ref, pieces_ref, w0, w1, w2, w3, keep_ref, send_ref):
    step = pl.program_id(0)
    heads = pieces_ref.shape[0]
    pieces = jnp.concatenate(
        [pieces_ref[head, kind] for kind in range(3) for head in range(heads)], axis=1
    )
    rows = w0.shape[0]
    for target, parity in ((keep_ref, 0), (send_ref, 1)):

        @pl.when(step % 2 == parity)
        def _(target=target):
            for place, w in enumerate((w0, w1, w2, w3)):
                target[0, :, columns_of(me_ref, place, rows)] = dot_nt(pieces, w[...]).astype(bf16)


def project_grad_kernel(
    me_ref,
    pieces_ref,
    x0,
    x1,
    x2,
    x3,
    gain_ref,
    w0,
    w1,
    w2,
    w3,
    two_ref,
    three_ref,
    four_ref,
    keep_ref,
    late_ref,
    early_ref,
    x_scr,
    total,
    lanes_scr,
    gains_scr,
):
    step = pl.program_id(0)
    heads = pieces_ref.shape[0]
    choose(step, (x0, x1, x2, x3), x_scr)
    pieces = jnp.concatenate(
        [pieces_ref[head, kind] for kind in range(3) for head in range(heads)], axis=1
    )
    x = x_scr[...].astype(f32)
    normed = (x * inverse_rms(x) * gain_ref[...]).astype(bf16)
    term = dot_tn(normed, pieces)

    @pl.when(step == 0)
    def _():
        total[...] = term

    @pl.when(step > 0)
    def _():
        total[...] += term

    @pl.when(step == pl.num_programs(0) - 1)
    def _():
        rows, columns = w0.shape
        refs = (keep_ref, late_ref, early_ref)
        spread_rows(me_ref, total, refs, slice(0, columns))
        for place, w in enumerate((w0, w1, w2, w3)):
            where = columns_of(me_ref, place, rows)
            product = total[where, :] * w[...].astype(f32)
            lanes_scr[where, :] = sum(
                product[:, first : first + HEAD] for first in range(0, columns, HEAD)
            )
        one = jnp.sum(lanes_scr[...].T, axis=0, keepdims=True) / gain_ref[...]
        gains = jnp.concatenate([one, two_ref[...], three_ref[...], four_ref[...]], axis=0)
        high = gains.astype(bf16).astype(f32)
        gains_scr[...] = jnp.concatenate([high, gains - high], axis=0)
        shards, piece_rows = keep_ref.shape[1:3]
        for ref, owner in piece_views(me_ref, refs):
            part = gains_scr[:, pl.ds(pl.multiple_of(owner * HEAD, HEAD), HEAD)]
            rest = jnp.zeros((piece_rows - part.shape[0], HEAD), f32)
            block = jnp.concatenate([part, rest], axis=0).astype(bf16)
            for shard in range(shards):
                ref[shard, :, columns:] = block


def middle_kernel(keep_ref, received_ref, x_ref, two_ref, three_ref, branch_ref, middle_ref, input_ref):
    branch = keep_ref[...] + received_ref[...].astype(f32)
    middle = x_ref[...].astype(f32) + branch * inverse_rms(branch) * two_ref[...]
    branch_ref[...] = branch
    middle_ref[...] = middle
    input_ref[...] = (middle * inverse_rms(middle) * three_ref[...]).astype(bf16)


def norm_back_parts(values, gain, upstream):
    inverse = inverse_rms(values)
    weighted = upstream * gain
    inner = jnp.mean(values * weighted, axis=-1, keepdims=True)
    value_grad = inverse * weighted - values * (inverse * inverse * inverse * inner)
    return value_grad, jnp.sum(upstream * values * inverse, axis=0, keepdims=True)


def turnaround_kernel(
    keep_ref, received_ref, middle_ref, grad_ref, four_ref, out_ref, back_ref, gain_ref
):
    ff_out = keep_ref[...] + received_ref[...].astype(f32)
    out_ref[...] = (middle_ref[...] + ff_out * inverse_rms(ff_out) * four_ref[...]).astype(bf16)
    value_grad, gain = norm_back_parts(ff_out, four_ref[...], grad_ref[...].astype(f32))
    back_ref[...] = value_grad.astype(bf16)
    gain_ref[...] = gain


def branch_back_kernel(
    keep_ref,
    received_ref,
    middle_ref,
    branch_ref,
    grad_ref,
    two_ref,
    three_ref,
    middle_grad_ref,
    branch_grad_ref,
    gain_two_ref,
    gain_three_ref,
):
    input_grad = keep_ref[...] + received_ref[...].astype(f32)
    middle_part, gain_three_ref[...] = norm_back_parts(middle_ref[...], three_ref[...], input_grad)
    middle_grad = grad_ref[...].astype(f32) + middle_part
    middle_grad_ref[...] = middle_grad
    branch_grad, gain_two_ref[...] = norm_back_parts(branch_ref[...], two_ref[...], middle_grad)
    branch_grad_ref[...] = branch_grad.astype(bf16)


def input_back_kernel(
    keep_ref, received_ref, across_ref, x_ref, middle_grad_ref, one_ref, out_ref
):
    normed_grad = keep_ref[0].astype(f32) + received_ref[0].astype(f32) + across_ref[...].astype(f32)
    part, _ = norm_back_parts(x_ref[...].astype(f32), one_ref[...], normed_grad)
    out_ref[...] = middle_grad_ref[...] + part


class Weights:
    def __init__(self, me_ref, refs, pair_scr, down_scr, sems):
        own, beside, far_y, far_x, corner_y, corner_x, down_near, *down_far = refs
        side = me_ref[1] % 2
        rows = far_y.shape[0]
        half = down_far[0].shape[1]
        moves = []
        for turn_index, far, corner in ((0, far_y, corner_y), (1, far_x, corner_x)):
            block = turn_index ^ side
            for place, source in enumerate((own.at[block], beside.at[block], far, corner)):
                target = pair_scr.at[turn_index, place * rows : (place + 1) * rows]
                moves.append((source, target))
        moves.append((down_near, down_scr.at[0]))
        for index, source in enumerate(down_far):
            moves.append((source, down_scr.at[1, :, index * half : (index + 1) * half]))
        self.copies = [
            pltpu.make_async_copy(source, target, sems.at[index])
            for index, (source, target) in enumerate(moves)
        ]
        self.pair_scr, self.down_scr = pair_scr, down_scr

    COUNT = 11
    DOWN = range(8, 11)

    def start(self, order):
        for index in order:
            self.copies[index].start()

    def wait(self, order):
        for index in order:
            self.copies[index].wait()

    def wait_turn(self, turn_index):
        for index in range(2):

            @pl.when(turn_index == index)
            def _(index=index):
                self.wait(self.turn(index))

    @staticmethod
    def turn(turn_index):
        return range(4 * turn_index, 4 * turn_index + 4)


def put_rows(scr, place_major, me_ref, *refs):
    rows, width = refs[0].shape
    size = width // PLACES
    for index, ref in enumerate(refs):
        where = slice(index * rows, (index + 1) * rows)
        if place_major:
            for place in range(PLACES):
                scr[where, place * size : (place + 1) * size] = ref[:, columns_of(me_ref, place, size)]
        else:
            scr[where, :] = ref[...]


def gate_parts(pair, half):
    def parts(gate, upward):
        sigma = 1.0 / (1.0 + jnp.exp(-gate))
        swish = gate * sigma
        slope = upward * sigma * (1.0 + gate * (1.0 - sigma))
        return swish, slope, (swish * upward).astype(bf16)

    main = half // HEAD * HEAD
    rest = half - main
    body = parts(pair[:, :main], pair[:, main : 2 * main])
    edge = pair[:, 2 * main :]
    edge_swish, edge_slope, edge_hidden = parts(edge, pltpu.roll(edge, rest, 1))
    lane = lax.broadcasted_iota(jnp.int32, edge.shape, 1)
    edge_factor = jnp.where(lane < rest, edge_slope, pltpu.roll(edge_swish, rest, 1))
    return body, edge_factor, edge_hidden


def put_hidden(ref, body, edge, main):
    rows = ref.shape[1]
    for row in range(2):
        where = slice(row * rows, (row + 1) * rows)
        ref[row, :, :main] = body[where]
        ref[row, :, main:] = edge[where]


def ff_kernel(me_ref, own_ref, beside_ref, *refs):
    weight_refs, (keep_ref, send_ref, saved_ref, hidden_ref) = refs[:9], refs[9:13]
    x_scr, hidden_scr, saved_scr, total, pair_w, down_w, sems, saved_sems = refs[13:]
    weights = Weights(me_ref, weight_refs, pair_w, down_w, sems)
    weights.start([*weights.turn(0), *weights.DOWN, *weights.turn(1)])
    put_rows(x_scr, True, me_ref, own_ref, beside_ref)
    half = down_w.shape[1]
    main = half // HEAD * HEAD
    total[...] = jnp.zeros_like(total)

    def save(turn_index):
        return pltpu.make_async_copy(
            saved_scr.at[turn_index], saved_ref.at[turn_index], saved_sems.at[turn_index]
        )

    @pl.loop(0, 2)
    def _(turn_index):
        block = turn_index ^ (me_ref[1] % 2)
        weights.wait_turn(turn_index)
        pair = dot_nn(x_scr[...], pair_w[turn_index])
        (swish, slope, hidden), edge_factor, edge_hidden = gate_parts(pair, half)
        saved_scr[turn_index, :, :main] = slope.astype(bf16)
        saved_scr[turn_index, :, main : 2 * main] = swish.astype(bf16)
        saved_scr[turn_index, :, 2 * main :] = edge_factor.astype(bf16)
        save(turn_index).start()
        hidden_scr[:, :main] = hidden
        hidden_scr[:, main:] = edge_hidden

        @pl.when(block == 0)
        def _():
            put_hidden(hidden_ref, hidden, edge_hidden, main)

        @pl.when(turn_index == 0)
        def _():
            weights.wait(weights.DOWN)

        total[...] += dot_nn(hidden_scr[:, :half], down_w[block])

    rows = keep_ref.shape[0]
    keep_ref[...] = total[:rows]
    send_ref[...] = total[rows:].astype(bf16)
    for turn_index in range(2):
        save(turn_index).wait()


def put_pair_grad(target, hidden_grad, factors, half):
    main = half // HEAD * HEAD
    edge = hidden_grad[:, main:]
    edge = jnp.concatenate([edge, edge], axis=1)
    for values, start in ((hidden_grad[:, :main], 0), (hidden_grad[:, :main], main), (edge, 2 * main)):
        columns = slice(start, start + values.shape[1])
        target[:, columns] = (values * factors[:, columns].astype(f32)).astype(bf16)


def ff_back_kernel(me_ref, own_ref, beside_ref, *refs):
    weight_refs, saved_ref, (keep_ref, send_ref, pair_ref) = refs[:9], refs[9], refs[10:13]
    grad_scr, pair_scr, total, pair_w, down_w, sems = refs[13:]
    weights = Weights(me_ref, weight_refs, pair_w, down_w, sems)
    weights.start([*weights.DOWN, *weights.turn(0), *weights.turn(1)])
    put_rows(grad_scr, False, me_ref, own_ref, beside_ref)
    half, width = down_w.shape[1:]
    rows = keep_ref.shape[0]
    size = width // PLACES
    weights.wait(weights.DOWN)
    total[...] = jnp.zeros_like(total)

    @pl.loop(0, 2)
    def _(turn_index):
        block = turn_index ^ (me_ref[1] % 2)
        hidden_grad = dot_nt(grad_scr[...], down_w[block])
        put_pair_grad(pair_scr, hidden_grad, saved_ref.at[turn_index], half)

        @pl.when(block == 0)
        def _():
            for row in range(2):
                pair_ref[row] = pair_scr[row * rows : (row + 1) * rows]

        weights.wait_turn(turn_index)
        total[...] += dot_nt(pair_scr[...], pair_w[turn_index])

    for place in range(PLACES):
        where = slice(place * size, (place + 1) * size)
        columns = columns_of(me_ref, place, size)
        keep_ref[:, columns] = total[:rows, where]
        send_ref[:, columns] = total[rows:, where].astype(bf16)


def ff_far_kernel(
    me_ref, x2_ref, x3_ref, grad2_ref, grad3_ref, *refs
):
    own, beside, far_y, far_x, corner_y, corner_x, down_near, hidden_ref, pair_ref = refs[:9]
    x_scr, factor_scr, pair_w = refs[9:]
    half = down_near.shape[0]
    main = half // HEAD * HEAD
    rows = x2_ref.shape[0]
    pair_w[:rows] = own[0]
    pair_w[rows : 2 * rows] = beside[0]
    for index, far in enumerate(((far_y, corner_y), (far_x, corner_x))):

        @pl.when(me_ref[1] % 2 == index)
        def _(far=far):
            pair_w[2 * rows : 3 * rows] = far[0][...]
            pair_w[3 * rows :] = far[1][...]

    put_rows(x_scr, True, me_ref, x2_ref, x3_ref)
    (swish, slope, hidden), edge_factor, edge_hidden = gate_parts(dot_nn(x_scr[...], pair_w[...]), half)
    put_hidden(hidden_ref, hidden, edge_hidden, main)
    factor_scr[:, :main] = slope.astype(bf16)
    factor_scr[:, main : 2 * main] = swish.astype(bf16)
    factor_scr[:, 2 * main :] = edge_factor.astype(bf16)
    put_rows(x_scr, False, me_ref, grad2_ref, grad3_ref)
    hidden_grad = dot_nt(x_scr[...], down_near[...])
    for row in range(2):
        where = slice(row * rows, (row + 1) * rows)
        put_pair_grad(pair_ref.at[row], hidden_grad[where], factor_scr.at[where], half)


def piece_height(me_ref, ahead):
    size = 4
    return (me_ref[1] // 2 + ahead) % size


def piece_owner(me_ref, other_x, ahead):
    return (me_ref[1] % 2 ^ other_x) + 2 * piece_height(me_ref, ahead)


def piece_views(me_ref, refs):
    keep, late, early = refs
    for ahead in range(4):
        yield keep.at[ahead], piece_owner(me_ref, 0, ahead)
        yield (late, early)[ahead // 2].at[ahead % 2], piece_owner(me_ref, 1, ahead)


def spread_rows(me_ref, total, refs, columns=slice(None), contiguous=False):
    shards, piece_rows = refs[0].shape[1:3]
    for ref, owner in piece_views(me_ref, refs):
        for shard in range(shards):
            block = owner * shards + shard if contiguous else shard * 8 + owner
            start = pl.multiple_of(block * piece_rows, 8)
            ref[shard, :, columns] = total[pl.ds(start, piece_rows), :].astype(bf16)


def piece_shapes(shape):
    return [(count,) + shape for count in (4, 2, 2)]


def over_x(late, early):
    early = ctx_swap(early, 1)
    late = ctx_swap(after(late, early), 1)
    return [late[0], late[1], early[0], early[1]], early


def weight_grads_kernel(sources, me_ref, *refs):
    operands, refs = refs[: sum(4 + count for count, _ in sources)], refs[len(sources) * 4 + sum(count for count, _ in sources) :]
    outs, scratch, sems = refs[:3], refs[3:-1], refs[-1]
    lefts, rights, totals = scratch[0::3], scratch[1::3], scratch[2::3]
    copies, groups = [], []

    def fetch(source, target):
        copies.append(pltpu.make_async_copy(source, target, sems.at[len(copies)]))

    for (count, _), left, right in zip(sources, lefts, rights, strict=True):
        first = len(copies)
        columns = right.shape[2]
        for place in range(PLACES):
            fetch(operands[place], left.at[place])
            if count == 2:
                fetch(operands[4 + place // 2].at[place % 2], right.at[place])
            else:
                heads = operands[4].shape[0] // PLACES
                for head in range(heads):
                    where = slice(head * HEAD, (head + 1) * HEAD)
                    fetch(operands[4].at[place * heads + head], right.at[place, :, where])
        operands = operands[4 + count :]
        groups.append(range(first, len(copies)))
    for copy in copies:
        copy.start()
    first = 0
    for (_, contiguous), group, left, right, total in zip(
        sources, groups, lefts, rights, totals, strict=True
    ):
        for index in group:
            copies[index].wait()
        columns = total.shape[1]
        total[...] = jnp.zeros_like(total)

        @pl.loop(0, PLACES)
        def _(place, left=left, right=right, total=total, columns=columns):
            total[...] += dot_tn(left[place], right[place, :, :columns])

        spread_rows(me_ref, total, outs, slice(first, first + columns), contiguous)
        first += columns


def weight_grads(me, name, expected, sources):
    rows, width = sources[0][0][0].shape
    operands, kinds, columns, scratch, moves = [me], [], [], [], 0
    for lefts, rights, count, contiguous in sources:
        operands += [*lefts, *rights]
        kinds.append((len(rights), contiguous))
        columns.append(count)
        held = count if len(rights) == 1 else rights[0].shape[2]
        scratch += [
            pltpu.VMEM((PLACES, rows, width), bf16),
            pltpu.VMEM((PLACES, rows, held), bf16),
            pltpu.VMEM((width, count), f32),
        ]
        moves += 2 * PLACES if len(rights) == 2 else PLACES + rights[0].shape[0]
    pieces = piece_shapes((PLACES, width // PLACES // 8, sum(columns)))
    return pl.pallas_call(
        functools.partial(weight_grads_kernel, tuple(kinds)),
        name=name,
        cost_estimate=cost(expected),
        grid=(1,),
        in_specs=[SMEM] + [pl.BlockSpec(memory_space=pl.ANY)] * (len(operands) - 1),
        out_specs=[whole(piece) for piece in pieces],
        out_shape=[shaped(*piece) for piece in pieces],
        scratch_shapes=scratch + [pltpu.SemaphoreType.DMA((moves,))],
        compiler_params=params(32, "arbitrary"),
    )(*operands)


def low_sum(*terms):
    return sum(term.astype(f32) for term in terms).astype(bf16)


def over_z(terms):
    running = low_sum(*terms[3])
    for ahead in (2, 1, 0):
        running = low_sum(*terms[ahead], z_shift(running))
    return running


def spread_piece(piece):
    near, far = [piece], []
    for step in range(3):
        ready = near[-1] if step == 0 else after(near[-1], far[-1])
        far.append(ctx_swap(near[-1], 1))
        near.append(z_shift(ready))
    return near + far + [ctx_swap(after(near[-1], far[-1]), 1)]


def settle_qkv_kernel(me_ref, *refs):
    pieces, outs, gains_ref = refs[:8], refs[8:11], refs[11]
    shards, rows, columns = pieces[0].shape
    part = columns // 3 // HEAD * HEAD
    count = gains_ref.shape[0]
    for index, ref in enumerate(pieces):
        owner = piece_owner(me_ref, index // 4, -(index % 4))
        where = pl.ds(pl.multiple_of(owner * rows, rows), rows)
        gains = 0.0
        for shard in range(shards):
            for kind, out in enumerate(outs):
                out[where, shard * part : (shard + 1) * part] = ref[
                    shard, :, kind * part : (kind + 1) * part
                ].astype(f32)
            gains = gains + ref[shard, :16, 3 * part :].astype(f32)
        stretch = pl.ds(pl.multiple_of(owner * HEAD, HEAD), HEAD)
        gains_ref[:, stretch] = gains[:count] + gains[count : 2 * count]


def settle_pair_kernel(me_ref, *refs):
    pieces, outs = refs[:8], refs[8:]
    shards, rows, columns = pieces[0].shape
    half = columns // 2
    for index, ref in enumerate(pieces):
        owner = piece_owner(me_ref, index // 4, -(index % 4))
        where = pl.ds(pl.multiple_of(owner * rows, rows), rows)
        for kind, start, source, size in pair_columns(half):
            for shard in range(shards):
                first = shard * half + start
                outs[kind][where, first : first + size] = ref[
                    shard, :, source : source + size
                ].astype(f32)


def settle_turned_kernel(me_ref, *refs):
    pieces, (down_ref, out_ref) = refs[:8], refs[8:]
    shards, rows = pieces[0].shape[:2]
    half = down_ref.shape[0]
    for index, ref in enumerate(pieces):
        owner = piece_owner(me_ref, index // 4, -(index % 4))
        stretch = jnp.concatenate([ref[shard].astype(f32) for shard in range(shards)], axis=0)
        columns = pl.ds(pl.multiple_of(owner * shards * rows, shards * rows), shards * rows)
        down_ref[:, columns] = stretch[:, :half].T
        out_ref[:, columns] = stretch[:, half:].T


def settle(kernel, name, me, pieces, outs):
    return pl.pallas_call(
        kernel,
        name=name,
        grid=(1,),
        in_specs=[SMEM] + [whole(pieces[0].shape)] * 8,
        out_specs=[whole(out) for out in outs],
        out_shape=[shaped(*out, kind=f32) for out in outs],
        cost_estimate=cost(4),
        compiler_params=params(40),
    )(me, *pieces)


def shaped(*shape, kind=bf16):
    return jax.ShapeDtypeStruct(shape, kind)


def rope_tables(base, count):
    half = HEAD // 2
    frequencies = rope_base ** (-2.0 * jnp.arange(half, dtype=f32) / HEAD)
    frequencies = jnp.concatenate([frequencies, frequencies])
    sign = jnp.where(jnp.arange(HEAD) < half, -1.0, 1.0)
    blocks = base.shape[0]
    places = jnp.concatenate([base, jnp.arange(count, dtype=base.dtype)])
    angles = places.astype(f32)[:, None] * frequencies
    cosine, sine = jnp.cos(angles), jnp.sin(angles)
    cos_base, sin_base = cosine[:blocks, None], sine[:blocks, None]
    cos_step, sin_step = cosine[None, blocks:], sine[None, blocks:]
    return (
        cos_base * cos_step - sin_base * sin_step,
        (sin_base * cos_step + cos_base * sin_step) * sign,
    )


def pair_shards(
    block_in,
    out_grad,
    w_query,
    w_key,
    w_value,
    w_out,
    norm_one,
    norm_two,
    w_gate,
    w_up,
    w_down,
    norm_three,
    norm_four,
    prompt_len,
    cont_len,
    group_ids,
    cont_ids,
):
    rows, width = block_in.shape[1:]
    ctx_size = lax.axis_size("ctx")
    heads = width // HEAD // PLACES
    part = heads * HEAD
    prompt = P_DEV * ctx_size
    prompt_chunks, cont_chunks = prompt // rows, CONT // rows
    ff_part = w_down.shape[0]
    my_row = lax.axis_index("fsdp")
    my_chunk = lax.axis_index("ctx")
    me = jnp.stack([my_row, my_chunk]).astype(jnp.int32)
    groups, slots = cont_ids.shape
    gain_one, gain_two, gain_three, gain_four = (
        gain[None, :] for gain in (norm_one, norm_two, norm_three, norm_four)
    )
    x_own, grad_own = block_in[0], out_grad[0]
    row_spec, gain_spec = whole((rows, width)), whole((1, width))
    full_row, low_row, gain_row = (
        shaped(rows, width, kind=f32),
        shaped(rows, width),
        shaped(1, width, kind=f32),
    )

    x_across = y_swap(x_own)
    qkv_split = pl.pallas_call(
        split_qkv_kernel,
        name="split_qkv",
        cost_estimate=cost(2),
        grid=(1,),
        in_specs=[SMEM] + [whole((rows, width))] * 3,
        out_specs=[whole((rows, 3 * part))] * 4,
        out_shape=[shaped(rows, 3 * part)] * 4,
        compiler_params=params(16),
    )(me, w_query, w_key, w_value)
    w_qkv = [
        qkv_split[0],
        core_swap(qkv_split[1]),
        y_swap(qkv_split[2]),
        y_swap(core_swap(qkv_split[3])),
    ]
    x_beside = core_swap(x_own)
    x_all = [x_own, x_beside, x_across, core_swap(x_across)]

    row_of = my_row ^ jnp.arange(PLACES, dtype=jnp.int32)
    group_range = jnp.arange(groups, dtype=jnp.int32)
    slot_range = jnp.arange(slots, dtype=jnp.int32)
    pick_row = row_of[:, None] == group_range[None, :]
    group_of = jnp.sum(jnp.where(pick_row, group_ids[None, :], 0), axis=1)
    pick_group = group_of[:, None] == group_range[None, :]
    prompt_of = jnp.sum(jnp.where(pick_group, prompt_len[None, :], 0), axis=1)
    lens_of = jnp.sum(jnp.where(pick_group[:, :, None], cont_len[None], 0), axis=1)
    ids_of = jnp.sum(jnp.where(pick_row[:, :, None], cont_ids[None], 0), axis=1)
    slot_lens = jnp.sum(
        jnp.where(ids_of[:, :, None] == slot_range, lens_of[:, None, :], 0), axis=2
    )
    pick_pair = jnp.arange(PLACES, dtype=jnp.int32) == my_chunk // heads
    pair_prompt = jnp.sum(jnp.where(pick_pair, prompt_of, 0))
    pair_lens = jnp.sum(jnp.where(pick_pair[:, None], slot_lens, 0), axis=0)
    info = jnp.concatenate([pair_prompt[None], pair_lens])

    def first_position(slot, prompt_size):
        return jnp.where(slot >= prompt, prompt_size + (slot - prompt) % CONT, slot)

    starts = jnp.arange(ctx_size, dtype=jnp.int32) * rows
    bases = jnp.concatenate(
        [first_position(my_chunk * rows, prompt_of), first_position(starts, pair_prompt)]
    )
    cos_tables, sin_tables = rope_tables(bases, rows)
    cos_own, sin_own = cos_tables[:PLACES], sin_tables[:PLACES]
    cos_all, sin_all = cos_tables[PLACES:], sin_tables[PLACES:]
    w_qkv = after(w_qkv, cos_own, sin_own, cos_all, sin_all)

    ff_blocks, ff_block = (2, rows, 2 * ff_part), (rows, 2 * ff_part)
    split_shapes = [ff_blocks, ff_block, ff_blocks, ff_block]
    ff_own, ff_own_sent, ff_beside, ff_beside_sent = pl.pallas_call(
        split_ff_kernel,
        name="split_ff",
        cost_estimate=cost(3),
        grid=(1,),
        in_specs=[SMEM] + [whole(w_gate.shape)] * 2,
        out_specs=[whole(shape) for shape in split_shapes],
        out_shape=[shaped(*shape) for shape in split_shapes],
        compiler_params=params(20),
    )(me, w_gate, w_up)
    half = width // 2
    w_qkv, x_all, w_out_sent, ff_beside_sent = tie(w_qkv, x_all, w_out, ff_beside_sent)
    w_ff_beside = core_swap(ff_beside)
    ff_beside_sent = core_swap(ff_beside_sent)
    w_out_far = y_swap(w_out_sent)
    far_y = y_swap(after(ff_own_sent, w_out_far))
    far_x = ctx_swap(far_y, 1)
    corner_y = y_swap(after(ff_beside_sent, far_y))
    corner_x = ctx_swap(corner_y, 1)
    down_left = y_swap(after(w_down, corner_y)[:, :half])
    down_right = y_swap(after(w_down, down_left)[:, half:])

    piece = (heads, 3, rows, HEAD)
    qkv = pl.pallas_call(
        project_kernel,
        name="project",
        cost_estimate=cost(4),
        grid=(PLACES,),
        in_specs=[SMEM]
        + [row_spec] * 4
        + [gain_spec]
        + [whole((rows, 3 * part))] * 4
        + [pl.BlockSpec((1, rows, HEAD), lambda t: (t, 0, 0))] * 2,
        out_specs=pl.BlockSpec(piece, lambda t: (t, 0, 0, 0)),
        out_shape=shaped(PLACES * heads, 3, rows, HEAD),
        scratch_shapes=[pltpu.VMEM((rows, width), bf16)] * 2,
        compiler_params=params(16, "arbitrary"),
    )(me, *x_all, gain_one, *w_qkv, cos_own, sin_own)
    qkv = lax.all_to_all(after(qkv, w_out_far), "ctx", 0, 0, tiled=True)
    qkv = after(qkv, far_x, corner_y)

    qkv_shape, head_shape = (ctx_size, 3, rows, HEAD), (ctx_size, rows, HEAD)
    span = math.gcd(prompt_chunks, cont_chunks)
    blocks = ctx_size // span
    block_shape, lse_shape = (blocks, span * rows, HEAD), (blocks, 1, span * rows)
    block_counts = (span, prompt_chunks // span, cont_chunks // span)
    mixed, exact, log_total = pl.pallas_call(
        functools.partial(attend_kernel, *block_counts),
        name="attend",
        cost_estimate=cost(9),
        grid=(blocks,),
        in_specs=[SMEM, whole(qkv_shape)],
        out_specs=[whole(head_shape), whole(head_shape), whole(lse_shape)],
        out_shape=[
            shaped(*head_shape),
            shaped(*head_shape, kind=f32),
            shaped(*lse_shape, kind=f32),
        ],
        compiler_params=params(16, "arbitrary"),
    )(info, qkv)
    mixed = after(mixed, corner_x, down_left)
    attended = lax.all_to_all(mixed, "ctx", 0, 0, tiled=True)
    attended = after(attended, down_right)
    attended_far = y_swap(attended[2 * heads :])

    two_heads = (2 * heads, rows, HEAD)
    mix_specs = [whole((part, width))] * 2
    keep, send = pl.pallas_call(
        mix_out_kernel,
        name="mix_out",
        cost_estimate=cost(2),
        grid=(1,),
        in_specs=[whole((PLACES * heads, rows, HEAD)), whole(two_heads)] + mix_specs,
        out_specs=[row_spec] * 2,
        out_shape=[full_row, low_row],
        compiler_params=params(10),
    )(attended, attended_far, w_out, w_out_far)

    branch, middle, ff_input = pl.pallas_call(
        middle_kernel,
        name="middle",
        cost_estimate=cost(2),
        grid=(1,),
        in_specs=[row_spec] * 3 + [gain_spec] * 2,
        out_specs=[row_spec] * 3,
        out_shape=[full_row, full_row, low_row],
        compiler_params=params(10),
    )(keep, core_swap(send), x_own, gain_two, gain_three)
    ff_input_beside = core_swap(ff_input)
    ff_input_far = far_rows(ff_input)

    far_pairs = [far_y, far_x, corner_y, corner_x]
    far_weights = far_pairs + [w_down, down_left, down_right]

    both = 2 * rows
    padded = pl.cdiv(ff_part, HEAD) * HEAD
    saved_shape = (2, both, 2 * ff_part)
    hidden_shape, pair_shape = (2, rows, padded), (2, rows, 2 * ff_part)
    anywhere = pl.BlockSpec(memory_space=pl.ANY)

    def ff_call(kernel, name, expected, more_in, outs, scratch, last=()):
        return pl.pallas_call(
            kernel,
            name=name,
            cost_estimate=cost(expected),
            grid=(1,),
            in_specs=[SMEM] + [row_spec] * 2 + [anywhere] * 9 + more_in,
            out_specs=[spec for spec, _ in outs],
            out_shape=[shape for _, shape in outs],
            scratch_shapes=scratch
            + [
                pltpu.VMEM((both, width), f32),
                pltpu.VMEM((2, width, 2 * ff_part), bf16),
                pltpu.VMEM((2, ff_part, width), bf16),
                pltpu.SemaphoreType.DMA((Weights.COUNT,)),
                *last,
            ],
            compiler_params=params(40, "arbitrary"),
        )

    keep, send, ff_saved, hidden = ff_call(
        ff_kernel,
        "ff",
        9,
        [],
        [
            (row_spec, full_row),
            (row_spec, low_row),
            (anywhere, shaped(*saved_shape)),
            (whole(hidden_shape), shaped(*hidden_shape)),
        ],
        [
            pltpu.VMEM((both, width), bf16),
            pltpu.VMEM((both, padded), bf16),
            pltpu.VMEM(saved_shape, bf16),
        ],
        [pltpu.SemaphoreType.DMA((2,))],
    )(me, ff_input, ff_input_beside, ff_own, w_ff_beside, *far_weights)
    send = after(send, ff_input_far[0])
    block_out, ff_grad, part_four = pl.pallas_call(
        turnaround_kernel,
        name="turnaround",
        cost_estimate=cost(2),
        grid=(1,),
        in_specs=[row_spec] * 4 + [gain_spec],
        out_specs=[row_spec, row_spec, gain_spec],
        out_shape=[low_row, low_row, gain_row],
        compiler_params=params(10),
    )(keep, core_swap(send), middle, grad_own, gain_four)

    ff_grad_beside = core_swap(ff_grad)
    ff_grad_far = far_rows(ff_grad)
    keep, send, pair_grad = ff_call(
        ff_back_kernel,
        "ff_back",
        9,
        [whole(saved_shape)],
        [(row_spec, full_row), (row_spec, low_row), (whole(pair_shape), shaped(*pair_shape))],
        [pltpu.VMEM((both, width), bf16), pltpu.VMEM((both, 2 * ff_part), bf16)],
    )(me, ff_grad, ff_grad_beside, ff_own, w_ff_beside, *far_weights, ff_saved)
    send = after(send, ff_grad_far[0])

    middle_grad, branch_grad, part_two, part_three = pl.pallas_call(
        branch_back_kernel,
        name="branch_back",
        cost_estimate=cost(2),
        grid=(1,),
        in_specs=[row_spec] * 5 + [gain_spec] * 2,
        out_specs=[row_spec, row_spec, gain_spec, gain_spec],
        out_shape=[full_row, low_row, gain_row, gain_row],
        compiler_params=params(10),
    )(keep, core_swap(send), middle, branch, grad_own, gain_two, gain_three)
    branch_grad_beside = core_swap(branch_grad)

    heads_near, heads_far = pl.pallas_call(
        heads_back_kernel,
        name="heads_back",
        cost_estimate=cost(2),
        grid=(1,),
        in_specs=[row_spec] * 2 + mix_specs,
        out_specs=[whole(two_heads)] * 2,
        out_shape=[shaped(*two_heads)] * 2,
        compiler_params=params(10),
    )(branch_grad, branch_grad_beside, w_out, w_out_far)
    heads_far = y_swap(heads_far)
    ff_input_far, ff_grad_far = after((ff_input_far, ff_grad_far), heads_near)
    branch_grad_across = y_swap(branch_grad)

    near_share = pl.BlockSpec((1,) + ff_block, lambda *_: (0, 0, 0))
    hidden_far, pair_far = pl.pallas_call(
        ff_far_kernel,
        name="ff_far",
        cost_estimate=cost(6),
        grid=(1,),
        in_specs=[SMEM]
        + [row_spec] * 4
        + [near_share] * 2
        + [whole(ff_block)] * 4
        + [whole((ff_part, width))],
        out_specs=[whole(hidden_shape), whole(pair_shape)],
        out_shape=[shaped(*hidden_shape), shaped(*pair_shape)],
        scratch_shapes=[
            pltpu.VMEM((both, width), bf16),
            pltpu.VMEM((both, 2 * ff_part), bf16),
            pltpu.VMEM((width, 2 * ff_part), bf16),
        ],
        compiler_params=params(26),
    )(me, *ff_input_far, *ff_grad_far, ff_own, w_ff_beside, *far_pairs, w_down)
    pair_far = after(pair_far, heads_far)
    pair_keep, pair_late, pair_early = weight_grads(
        me,
        "pair_grads",
        7,
        [
            (
                [ff_input, ff_input_beside, *ff_input_far],
                [pair_grad, pair_far],
                2 * ff_part,
                False,
            )
        ],
    )
    attended_grad = lax.all_to_all(
        jnp.concatenate([heads_near, heads_far]), "ctx", 0, 0, tiled=True
    )
    branch_grad_far = [branch_grad_across, core_swap(branch_grad_across)]
    pair_over, pair_first = over_x(pair_late, pair_early)
    attended_grad = after(attended_grad, pair_keep)

    pieces = pl.pallas_call(
        functools.partial(attend_back_kernel, *block_counts),
        name="attend_back",
        cost_estimate=cost(11),
        grid=(blocks,),
        in_specs=[
            SMEM,
            whole(qkv_shape),
            whole(head_shape),
            whole(head_shape),
            whole(lse_shape),
            whole(head_shape),
            whole(head_shape),
        ],
        out_specs=whole(qkv_shape),
        out_shape=shaped(*qkv_shape),
        scratch_shapes=[pltpu.VMEM(block_shape, f32)] * 2,
        compiler_params=params(20, "arbitrary"),
    )(info, qkv, attended_grad, exact, log_total, cos_all, sin_all)
    hidden, hidden_far = after((hidden, hidden_far), pieces)
    down_keep, down_late, down_early = weight_grads(
        me,
        "down_grads",
        8,
        [
            ([ff_grad, ff_grad_beside, *ff_grad_far], [hidden, hidden_far], ff_part, True),
            ([branch_grad, branch_grad_beside, *branch_grad_far], [attended], part, True),
        ],
    )
    pieces = lax.all_to_all(after(pieces, pair_first), "ctx", 0, 0, tiled=True)
    pieces = after(pieces, down_keep)

    piece_spec = pl.BlockSpec(piece, lambda t: (t, 0, 0, 0))
    qkv_pieces = piece_shapes((PLACES, rows // 8, 3 * part + HEAD))
    qkv_keep, qkv_late, qkv_early = pl.pallas_call(
        project_grad_kernel,
        name="project_grad",
        cost_estimate=cost(5),
        grid=(PLACES,),
        in_specs=[SMEM, piece_spec]
        + [row_spec] * 4
        + [gain_spec]
        + [whole((rows, 3 * part))] * 4
        + [gain_spec] * 3,
        out_specs=[whole(shape) for shape in qkv_pieces],
        out_shape=[shaped(*shape) for shape in qkv_pieces],
        scratch_shapes=[
            pltpu.VMEM((rows, width), bf16),
            pltpu.VMEM((width, 3 * part), f32),
            pltpu.VMEM((width, HEAD), f32),
            pltpu.VMEM((8, width), f32),
        ],
        compiler_params=params(20, "arbitrary"),
    )(me, pieces, *x_all, gain_one, *w_qkv, part_two, part_three, part_four)
    qkv_over, _ = over_x(qkv_late, qkv_early)
    pieces = after(pieces, qkv_keep)

    pair_rows = pl.BlockSpec((1, rows, width), lambda t: (t // 2, 0, 0))
    keep, send = pl.pallas_call(
        project_back_kernel,
        name="project_back",
        cost_estimate=cost(5),
        grid=(PLACES,),
        in_specs=[SMEM, piece_spec] + [whole((rows, 3 * part))] * 4,
        out_specs=[pair_rows, pair_rows],
        out_shape=[shaped(2, rows, width)] * 2,
        compiler_params=params(12, "arbitrary"),
    )(me, pieces, *w_qkv)

    received = core_swap(send)
    onward = (keep[1].astype(f32) + received[1].astype(f32)).astype(bf16)
    in_grad = pl.pallas_call(
        input_back_kernel,
        name="input_back",
        cost_estimate=cost(2),
        grid=(1,),
        in_specs=[pl.BlockSpec((1, rows, width), lambda *_: (0, 0, 0))] * 2
        + [row_spec] * 3
        + [gain_spec],
        out_specs=row_spec,
        out_shape=full_row,
        compiler_params=params(10),
    )(keep, received, y_swap(onward), x_own, middle_grad, gain_one)

    def shared_rows(piece):
        return lax.all_to_all(piece, "fsdp", 0, 0, tiled=True)

    pair_over = after(pair_over, pieces)
    pair_came = z_shift(low_sum(pair_keep[3], pair_over[3]))
    pair_came = z_shift(low_sum(pair_keep[2], pair_over[2], pair_came))
    pair_came = z_shift(low_sum(pair_keep[1], pair_over[1], pair_came))
    pair_piece = shared_rows(low_sum(pair_keep[0], pair_over[0], pair_came))
    down_over, _ = over_x(down_late, after(down_early, pair_over))
    qkv_piece = shared_rows(
        over_z([[qkv_keep[ahead], qkv_over[ahead]] for ahead in range(4)])
    )
    down_piece = over_z([[down_keep[ahead], down_over[ahead]] for ahead in range(4)])
    query_sum, key_sum, value_sum, gains = settle(
        settle_qkv_kernel, "settle_qkv", me, spread_piece(qkv_piece), [(rows, width)] * 3 + [(4, width)]
    )
    gate_sum, up_sum = settle(
        settle_pair_kernel, "settle_pair", me, spread_piece(pair_piece), [w_gate.shape] * 2
    )
    down_sum, out_sum = settle(
        settle_turned_kernel,
        "settle_turned",
        me,
        spread_piece(down_piece),
        [(ff_part, width), (part, width)],
    )

    return (
        block_out[None],
        in_grad[None],
        query_sum,
        key_sum,
        value_sum,
        out_sum,
        gains[0],
        gains[1],
        gate_sum,
        up_sum,
        down_sum,
        gains[2],
        gains[3],
    )


def solution(mesh):
    fsdp, ctx = mesh.shape["fsdp"], mesh.shape["ctx"]

    def step(*args):
        width, groups = args[0].shape[2], args[0].shape[0]
        heads = width // HEAD
        rows = args[0].shape[1] // ctx
        paired = (
            fsdp == 4
            and groups == fsdp
            and heads == ctx
            and CONT % rows == 0
            and (P_DEV * ctx) % rows == 0
            and width // fsdp == rows
        )
        return jax.shard_map(
            pair_shards if paired else shards,
            mesh=mesh,
            in_specs=IN_SPECS,
            out_specs=OUT_SPECS,
            check_vma=False,
        )(*args)

    return step
```

```python
import functools
import math

import jax
import jax.numpy as jnp
from jax import lax
from jax.experimental import pallas as pl
from jax.experimental.pallas import tpu as pltpu
from jax.sharding import PartitionSpec as P

HEAD = 128
P_DEV = 128
CONT = 512
LOG2E = 1.4426950408889634

eps_norm = 1e-06
rope_base = 50000.0
masked_out = -1e30

bf16 = jnp.bfloat16
f32 = jnp.float32

def rms_norm(values, gain_vec):
    inverse = lax.rsqrt(jnp.mean(values * values, axis=-1, keepdims=True) + eps_norm)
    return (values * inverse * gain_vec, inverse)


def norm_back(values, inverse, gain_vec, upstream):
    weighted = upstream * gain_vec
    inner_mean = jnp.mean(values * weighted, axis=-1, keepdims=True)
    value_grad = inverse * weighted - values * inverse * inverse * inverse * inner_mean
    return (value_grad, jnp.sum(upstream * values * inverse, axis=0))


def rotate(values, position, turn_sign):
    seq_len = values.shape[0]
    half_size = HEAD // 2
    split_heads = values.reshape(seq_len, -1, HEAD)
    frequencies = rope_base ** (-2.0 * jnp.arange(half_size, dtype=jnp.float32) / HEAD)
    angles = position.astype(jnp.float32)[:, None] * frequencies[None, :]
    cosine = jnp.concatenate([jnp.cos(angles), jnp.cos(angles)], axis=-1)[:, None, :]
    sine_part = turn_sign * jnp.concatenate([jnp.sin(angles), jnp.sin(angles)], axis=-1)[:, None, :]
    turned = jnp.concatenate([-split_heads[..., half_size:], split_heads[..., :half_size]], axis=-1)
    return (split_heads * cosine + turned * sine_part).reshape(seq_len, -1)


def token_info(slot_index, prompt, prompt_size, slot_lens):
    in_cont = slot_index >= prompt
    rel_index = jnp.maximum(slot_index - prompt, 0)
    slot_of = jnp.where(in_cont, rel_index // CONT, -1)
    offset = rel_index % CONT
    slot_range = jnp.arange(slot_lens.shape[0], dtype=jnp.int32)
    slot_len = jnp.sum(
        jnp.where(slot_of[:, None] == slot_range[None, :], slot_lens[None, :], 0), axis=1
    )
    token_valid = jnp.where(in_cont, offset < slot_len, slot_index < prompt_size)
    position = jnp.where(in_cont, prompt_size + offset, slot_index)
    return (token_valid, slot_of, position)


def cross_dot(operand, partner):
    return lax.dot_general(
        operand, partner, (((0,), (0,)), ((), ())), preferred_element_type=jnp.float32
    )


def back_dot(operand, partner):
    return lax.dot_general(
        operand, partner, (((1,), (1,)), ((), ())), preferred_element_type=jnp.float32
    )


def keep_same(state):
    return state


def shards(
    block_in,
    out_grad,
    w_query,
    w_key,
    w_value,
    w_out,
    norm_one,
    norm_two,
    w_gate,
    w_up,
    w_down,
    norm_three,
    norm_four,
    prompt_len,
    cont_len,
    group_ids,
    cont_ids,
):
    local_rows = block_in.shape[1]
    model_width = block_in.shape[2]
    ff_width = w_gate.shape[1]
    ctx_size = lax.axis_size("ctx")
    group_rows = local_rows * ctx_size
    prompt = P_DEV * ctx_size
    head_count = model_width // HEAD
    score_scale = 1.0 / math.sqrt(HEAD)
    row_index = lax.axis_index("fsdp")
    groups = group_ids.shape[0]
    slot_count = cont_ids.shape[1]
    group_range = jnp.arange(groups, dtype=jnp.int32)
    own_group = jnp.sum(jnp.where(group_range == row_index, group_ids, 0))
    own_prompt = jnp.sum(jnp.where(group_range == own_group, prompt_len, 0))
    own_lens = jnp.sum(jnp.where((group_range == own_group)[:, None], cont_len, 0), axis=0)
    own_ids = jnp.sum(jnp.where((group_range == row_index)[:, None], cont_ids, 0), axis=0)
    slot_range = jnp.arange(slot_count, dtype=jnp.int32)
    slot_lens = jnp.sum(
        jnp.where(own_ids[:, None] == slot_range[None, :], own_lens[None, :], 0), axis=1
    )
    query_index = lax.axis_index("ctx") * local_rows + jnp.arange(local_rows, dtype=jnp.int32)
    key_index = jnp.arange(group_rows, dtype=jnp.int32)
    query_valid, query_slot, position = token_info(query_index, prompt, own_prompt, slot_lens)
    key_valid, key_slot, unused_pos = token_info(key_index, prompt, own_prompt, slot_lens)
    tokens = block_in[0].astype(jnp.float32)
    full_query, full_key, full_value, full_out = (
        lax.all_gather(w_query, "fsdp", axis=0, tiled=True),
        lax.all_gather(w_key, "fsdp", axis=0, tiled=True),
        lax.all_gather(w_value, "fsdp", axis=0, tiled=True),
        lax.all_gather(w_out, "fsdp", axis=0, tiled=True),
    )
    normed_full, inverse_one = rms_norm(tokens, norm_one)
    normed = normed_full.astype(jnp.bfloat16)
    queries = rotate(
        jnp.dot(normed, full_query, preferred_element_type=jnp.float32), position, 1.0
    ).astype(jnp.bfloat16)
    keys_local = rotate(
        jnp.dot(normed, full_key, preferred_element_type=jnp.float32), position, 1.0
    ).astype(jnp.bfloat16)
    values_local = jnp.dot(normed, full_value, preferred_element_type=jnp.float32).astype(
        jnp.bfloat16
    )
    all_keys, all_values = (
        lax.all_gather(keys_local, "ctx", axis=0, tiled=True),
        lax.all_gather(values_local, "ctx", axis=0, tiled=True),
    )
    key_block = math.gcd(group_rows, 512)
    block_count = group_rows // key_block
    blocks_in = (
        all_keys.reshape(block_count, key_block, head_count, HEAD),
        all_values.reshape(block_count, key_block, head_count, HEAD),
        key_valid.reshape(block_count, key_block),
        key_slot.reshape(block_count, key_block),
        key_index.reshape(block_count, key_block),
    )
    query_heads = queries.reshape(local_rows, head_count, HEAD)

    def mask_of(inputs):
        key_ids = inputs[4]
        return (
            query_valid[:, None]
            & inputs[2][None, :]
            & (key_ids[None, :] <= query_index[:, None])
            & ((key_ids[None, :] < prompt) | (inputs[3][None, :] == query_slot[:, None]))
        )

    def raw_scores(inputs):
        return (
            jnp.einsum("qhd,khd->hqk", query_heads, inputs[0], preferred_element_type=jnp.float32)
            * score_scale
        )

    def running(state_in, inputs):
        allowed = mask_of(inputs)

        def running_visit(state):
            row_top, exp_total = state
            scores = jnp.where(allowed[None], raw_scores(inputs), masked_out)
            new_top = jnp.maximum(row_top, jnp.max(scores, axis=-1, keepdims=True))
            exp_total = exp_total * jnp.exp(row_top - new_top) + jnp.sum(
                jnp.where(allowed[None], jnp.exp(scores - new_top), 0.0), axis=-1, keepdims=True
            )
            return (new_top, exp_total)

        return (lax.cond(jnp.any(allowed), running_visit, keep_same, state_in), None)

    start_top = jnp.full((head_count, local_rows, 1), -jnp.inf, jnp.float32)
    start_total = jnp.zeros((head_count, local_rows, 1), jnp.float32)
    (row_top, exp_total), unused = lax.scan(running, (start_top, start_total), blocks_in)
    has_keys = exp_total > 0.0
    log_total = jnp.where(has_keys, row_top + jnp.log(jnp.where(has_keys, exp_total, 1.0)), 0.0)

    def probs_of(inputs, allowed):
        return jnp.where(allowed[None], jnp.exp(raw_scores(inputs) - log_total), 0.0)

    def mix_step(accumulated, inputs):
        allowed = mask_of(inputs)

        def mix_visit(total):
            attn_probs = probs_of(inputs, allowed).astype(jnp.bfloat16)
            return total + jnp.einsum(
                "hqk,khd->qhd", attn_probs, inputs[1], preferred_element_type=jnp.float32
            )

        return (lax.cond(jnp.any(allowed), mix_visit, keep_same, accumulated), None)

    mixture, unused = lax.scan(
        mix_step, jnp.zeros((local_rows, head_count, HEAD), jnp.float32), blocks_in
    )
    valid_col = query_valid[:, None].astype(jnp.float32)
    attended = (mixture.reshape(local_rows, model_width) * valid_col).astype(jnp.bfloat16)
    branch = jnp.dot(attended, full_out, preferred_element_type=jnp.float32)
    branch_normed, inverse_two = rms_norm(branch, norm_two)
    middle = tokens + branch_normed
    full_gate, full_up, full_down = (
        lax.all_gather(w_gate, "fsdp", axis=0, tiled=True),
        lax.all_gather(w_up, "fsdp", axis=0, tiled=True),
        lax.all_gather(w_down, "fsdp", axis=0, tiled=True),
    )
    ff_normed, inverse_three = rms_norm(middle, norm_three)
    ff_input = ff_normed.astype(jnp.bfloat16)
    gate_pre = jnp.dot(ff_input, full_gate, preferred_element_type=jnp.float32)
    upward = jnp.dot(ff_input, full_up, preferred_element_type=jnp.float32)
    gate_sig = jax.nn.sigmoid(gate_pre)
    swish_out = gate_pre * gate_sig
    hidden = (swish_out * upward).astype(jnp.bfloat16)
    ff_out = jnp.dot(hidden, full_down, preferred_element_type=jnp.float32)
    out_normed, inverse_four = rms_norm(ff_out, norm_four)
    result = middle + out_normed
    upstream = out_grad[0].astype(jnp.float32)
    ff_out_full, grad_norm_four = norm_back(ff_out, inverse_four, norm_four, upstream)
    ff_out_grad = ff_out_full.astype(jnp.bfloat16)
    hidden_grad = back_dot(ff_out_grad, full_down)
    up_grad = (hidden_grad * swish_out).astype(jnp.bfloat16)
    gate_grad = (hidden_grad * upward * gate_sig * (1.0 + gate_pre * (1.0 - gate_sig))).astype(
        jnp.bfloat16
    )
    ff_in_grad = back_dot(gate_grad, full_gate) + back_dot(up_grad, full_up)
    middle_part, grad_norm_three = norm_back(middle, inverse_three, norm_three, ff_in_grad)
    middle_grad = upstream + middle_part
    branch_full, grad_norm_two = norm_back(branch, inverse_two, norm_two, middle_grad)
    branch_grad = branch_full.astype(jnp.bfloat16)
    attended_grad = back_dot(branch_grad, full_out).astype(jnp.bfloat16) * valid_col.astype(
        jnp.bfloat16
    )
    grad_heads = attended_grad.reshape(local_rows, head_count, HEAD)

    def delta_step(accumulated, inputs):
        allowed = mask_of(inputs)

        def delta_visit(total):
            attn_probs = probs_of(inputs, allowed)
            prob_grad = jnp.einsum(
                "qhd,khd->hqk", grad_heads, inputs[1], preferred_element_type=jnp.float32
            )
            return total + jnp.sum(attn_probs * prob_grad, axis=-1, keepdims=True)

        return (lax.cond(jnp.any(allowed), delta_visit, keep_same, accumulated), None)

    row_delta, unused = lax.scan(
        delta_step, jnp.zeros((head_count, local_rows, 1), jnp.float32), blocks_in
    )
    zero_part = jnp.zeros((key_block, head_count, HEAD), jnp.float32)

    def grad_step(accumulated, inputs):
        allowed = mask_of(inputs)

        def grad_visit(total):
            attn_probs = probs_of(inputs, allowed)
            prob_grad = jnp.einsum(
                "qhd,khd->hqk", grad_heads, inputs[1], preferred_element_type=jnp.float32
            )
            score_grad = (attn_probs * (prob_grad - row_delta)).astype(jnp.bfloat16)
            total = total + jnp.einsum(
                "hqk,khd->qhd", score_grad, inputs[0], preferred_element_type=jnp.float32
            )
            key_part = jnp.einsum(
                "hqk,qhd->khd", score_grad, query_heads, preferred_element_type=jnp.float32
            )
            value_part = jnp.einsum(
                "hqk,qhd->khd",
                attn_probs.astype(jnp.bfloat16),
                grad_heads,
                preferred_element_type=jnp.float32,
            )
            return (total, (key_part, value_part))

        def skip(total):
            return (total, (zero_part, zero_part))

        return lax.cond(jnp.any(allowed), grad_visit, skip, accumulated)

    query_acc, (key_parts, value_parts) = lax.scan(
        grad_step, jnp.zeros((local_rows, head_count, HEAD), jnp.float32), blocks_in
    )
    key_terms = key_parts.reshape(group_rows, model_width) * score_scale
    value_terms = value_parts.reshape(group_rows, model_width)
    key_sum, value_sum = (
        lax.psum_scatter(
            key_terms.astype(jnp.bfloat16), "ctx", scatter_dimension=0, tiled=True
        ).astype(jnp.float32),
        lax.psum_scatter(
            value_terms.astype(jnp.bfloat16), "ctx", scatter_dimension=0, tiled=True
        ).astype(jnp.float32),
    )
    query_grad = rotate(
        query_acc.reshape(local_rows, model_width) * score_scale, position, -1.0
    ).astype(jnp.bfloat16)
    key_grad = rotate(key_sum, position, -1.0).astype(jnp.bfloat16)
    value_grad = value_sum.astype(jnp.bfloat16)
    normed_grad = (
        back_dot(query_grad, full_query)
        + back_dot(key_grad, full_key)
        + back_dot(value_grad, full_value)
    )
    input_part, grad_norm_one = norm_back(tokens, inverse_one, norm_one, normed_grad)
    input_grad = middle_grad + input_part
    wide_pairs = (
        (normed, query_grad),
        (normed, key_grad),
        (normed, value_grad),
        (attended, branch_grad),
        (ff_input, gate_grad),
        (ff_input, up_grad),
    )

    def wide_term(selector):
        return jnp.concatenate(
            [cross_dot(selector(operand), partner) for operand, partner in wide_pairs], axis=1
        )

    wide_local = lax.psum_scatter(
        wide_term(lambda operand: operand).astype(jnp.bfloat16),
        "fsdp",
        scatter_dimension=0,
        tiled=True,
    )
    ff_local = lax.psum_scatter(
        cross_dot((lambda operand: operand)(hidden), ff_out_grad).astype(jnp.bfloat16),
        "fsdp",
        scatter_dimension=0,
        tiled=True,
    )
    wide_sum, ff_sum = (
        lax.psum(wide_local, "ctx").astype(jnp.float32),
        lax.psum(ff_local, "ctx").astype(jnp.float32),
    )
    gain_sums = lax.psum(
        jnp.stack([grad_norm_one, grad_norm_two, grad_norm_three, grad_norm_four]), ("ctx", "fsdp")
    )
    edge_two = 2 * model_width
    edge_three = 3 * model_width
    edge_four = 4 * model_width
    edge_five = 4 * model_width + ff_width
    return (
        result.astype(jnp.bfloat16)[None],
        input_grad[None],
        wide_sum[:, :model_width],
        wide_sum[:, model_width:edge_two],
        wide_sum[:, edge_two:edge_three],
        wide_sum[:, edge_three:edge_four],
        gain_sums[0],
        gain_sums[1],
        wide_sum[:, edge_four:edge_five],
        wide_sum[:, edge_five:],
        ff_sum,
        gain_sums[2],
        gain_sums[3],
    )


IN_SPECS = (
    (P("fsdp", "ctx", None),) * 2
    + (P("fsdp", None),) * 4
    + (P(), P())
    + (P("fsdp", None),) * 3
    + (P(),) * 6
)
OUT_SPECS = (
    (P("fsdp", "ctx", None),) * 2
    + (P("fsdp", None),) * 4
    + (P(), P())
    + (P("fsdp", None),) * 3
    + (P(), P())
)


MIB = 1 << 20
PLACES = 4


def core_swap(values):
    return lax.ppermute(values, "fsdp", [(i, i ^ 1) for i in range(4)])


def y_swap(values):
    return lax.ppermute(values, "fsdp", [(i, i ^ 2) for i in range(4)])


def ctx_swap(values, bit):
    size = lax.axis_size("ctx")
    return lax.ppermute(values, "ctx", [(i, i ^ bit) for i in range(size)])


def z_shift(values):
    size = lax.axis_size("ctx")
    return lax.ppermute(values, "ctx", [(i, (i + 2) % size) for i in range(size)])


def tie(*values):
    return lax.optimization_barrier(values)


def after(value, *others):
    return lax.optimization_barrier((value, others))[0]


def far_rows(own):
    across = y_swap(own)
    return across, core_swap(across)


def params(limit_mib, *semantics):
    return pltpu.CompilerParams(
        dimension_semantics=semantics or None, vmem_limit_bytes=limit_mib * MIB
    )


def cost(microseconds):
    return pl.CostEstimate(flops=int(microseconds * 1e6), bytes_accessed=0, transcendentals=0)


def whole(shape):
    return pl.BlockSpec(shape, lambda *_: (0,) * len(shape))


SMEM = pl.BlockSpec(memory_space=pltpu.SMEM)


def dot_nn(a, b):
    return lax.dot_general(a, b, (((1,), (0,)), ((), ())), preferred_element_type=f32)


def dot_nt(a, b):
    return lax.dot_general(a, b, (((1,), (1,)), ((), ())), preferred_element_type=f32)


def dot_tn(a, b):
    return lax.dot_general(a, b, (((0,), (0,)), ((), ())), preferred_element_type=f32)


def inverse_rms(values):
    return lax.rsqrt(jnp.mean(values * values, axis=-1, keepdims=True) + eps_norm)


def turn(values, cosine, sine):
    return values * cosine + pltpu.roll(values, HEAD // 2, 1) * sine


def choose(step, refs, target):
    for index, ref in enumerate(refs):

        @pl.when(step == index)
        def _(ref=ref):
            target[...] = ref[...]


def columns_of(me_ref, place, rows):
    return pl.ds(pl.multiple_of((me_ref[0] ^ place) * rows, rows), rows)


def half_columns(which, ref):
    columns = ref.shape[1]
    return pl.ds(pl.multiple_of(which * columns, HEAD), columns)


def split_qkv_kernel(
    me_ref, q_ref, k_ref, v_ref, mix_ref, own_ref, beside_ref, far_sent, corner_sent, mix_sent, block_scr
):
    part = own_ref.shape[1] // 3
    side = me_ref[1] % 2

    def put(target, place):
        for kind, ref in enumerate((q_ref, k_ref, v_ref)):
            target[:, kind * part : (kind + 1) * part] = ref[:, columns_of(me_ref, place, part)]

    put(own_ref, 0)
    put(beside_ref, 1)
    for place, target in ((2, far_sent), (3, corner_sent)):
        put(block_scr, place)
        target[...] = block_scr[:, half_columns(side, target)]
    mix_sent[...] = mix_ref[:, half_columns(side, mix_sent)]


def pair_columns(half):
    main = half // HEAD * HEAD
    rest = half - main
    return (
        (0, 0, 0, main),
        (1, 0, main, main),
        (0, main, 2 * main, rest),
        (1, main, 2 * main + rest, rest),
    )


def split_ff_kernel(
    me_ref, gate_ref, up_ref, down_ref, own_ref, own_sent, beside_ref, beside_sent, left_ref, right_ref
):
    half = own_ref.shape[-1] // 2
    for me in range(PLACES):

        @pl.when(me_ref[0] == me)
        def _(me=me):
            for place in range(PLACES):
                target = own_ref if place % 2 == 0 else beside_ref
                for kind, start, where, size in pair_columns(half):
                    first = (me ^ place) * half + start
                    target[place // 2, :, where : where + size] = (gate_ref, up_ref)[kind][
                        :, first : first + size
                    ]

    side = me_ref[1] % 2
    middle = left_ref.shape[1]
    left_ref[...] = down_ref[:, :middle]
    right_ref[...] = down_ref[:, middle:]
    own_sent[...] = own_ref[1 - side]
    beside_sent[...] = beside_ref[1 - side]


def project_kernel(
    me_ref,
    x0,
    x1,
    x2,
    x3,
    gain_ref,
    w0,
    w1,
    far_y,
    far_x,
    corner_y,
    corner_x,
    cos_ref,
    sin_ref,
    out_ref,
    w_ref,
    x_scr,
    normed_scr,
):
    step = pl.program_id(0)

    @pl.when(step == 0)
    def _():
        side = me_ref[1] % 2
        w_ref[0] = w0[...]
        w_ref[1] = w1[...]
        for place, first, second in ((2, far_y, far_x), (3, corner_y, corner_x)):
            w_ref[place, :, half_columns(side, first)] = first[...]
            w_ref[place, :, half_columns(1 - side, second)] = second[...]

    choose(step, (x0, x1, x2, x3), x_scr)
    x = x_scr[...].astype(f32)
    normed_scr[...] = (x * inverse_rms(x) * gain_ref[...]).astype(bf16)
    rows = w0.shape[0]
    product = sum(
        dot_nn(normed_scr[:, columns_of(me_ref, place, rows)], w_ref[place])
        for place in range(PLACES)
    )
    heads = out_ref.shape[0]
    for kind in range(3):
        for head in range(heads):
            start = (kind * heads + head) * HEAD
            part = product[:, start : start + HEAD]
            if kind < 2:
                part = turn(part, cos_ref[0], sin_ref[0])
            out_ref[head, kind] = part.astype(bf16)


def block_facts(block, rows, prompt_blocks, cont_blocks, info_ref):
    beyond = jnp.maximum(block - prompt_blocks, 0)
    in_cont = block >= prompt_blocks
    slot = beyond // cont_blocks
    first = jnp.where(in_cont, prompt_blocks + slot * cont_blocks, 0)
    ahead = jnp.where(in_cont, prompt_blocks, 0)
    start = jnp.where(in_cont, beyond % cont_blocks, block) * rows
    limit = jnp.where(in_cont, info_ref[1 + slot], info_ref[0])
    return first, ahead, start, limit


def visit_blocks(visit, block, rows, first, ahead, info_ref, state):
    key_place = lax.broadcasted_iota(jnp.int32, (rows, rows), 0)
    query_place = lax.broadcasted_iota(jnp.int32, (rows, rows), 1)
    key_row = lax.broadcasted_iota(jnp.int32, (rows, 1), 0)

    def prompt_visit(key_block, state):
        bias = jnp.where(key_block * rows + key_row < info_ref[0], 0.0, masked_out)
        return visit(key_block, bias, False, state)

    state = visit(block, jnp.where(key_place <= query_place, 0.0, masked_out), True, state)
    state = lax.fori_loop(0, ahead, prompt_visit, state)
    return lax.fori_loop(
        first, block, lambda key_block, state: visit(key_block, 0.0, False, state), state
    )


def attend_kernel(span, prompt_blocks, cont_blocks, info_ref, qkv_ref, out_ref, exact_ref, lse_ref):
    block = pl.program_id(0)
    small = qkv_ref.shape[2]
    rows = small * span
    scale = LOG2E / math.sqrt(HEAD)

    def take(block, kind):
        return qkv_ref[pl.ds(block * span, span), kind].reshape(rows, HEAD)

    query = take(block, 0)
    first, ahead, start, limit = block_facts(block, rows, prompt_blocks, cont_blocks, info_ref)

    def visit(key_block, bias, _, state):
        top, total, mixed = state
        scores = dot_nt(take(key_block, 1), query) * scale + bias
        new_top = jnp.maximum(top, jnp.max(scores, axis=0, keepdims=True))
        weights = jnp.exp2(scores - new_top)
        shrink = jnp.exp2(top - new_top)
        total = total * shrink + jnp.sum(weights, axis=0, keepdims=True)
        mixed = mixed * shrink + dot_tn(take(key_block, 2), weights.astype(bf16))
        return new_top, total, mixed

    state = (
        jnp.full((1, rows), -1e38, f32),
        jnp.zeros((1, rows), f32),
        jnp.zeros((HEAD, rows), f32),
    )
    top, total, mixed = visit_blocks(visit, block, rows, first, ahead, info_ref, state)
    valid = start + lax.broadcasted_iota(jnp.int32, (1, rows), 1) < limit
    settled = jnp.where(valid, mixed / total, 0.0).T.reshape(span, small, HEAD)
    out_ref[pl.ds(block * span, span)] = settled.astype(bf16)
    exact_ref[pl.ds(block * span, span)] = settled
    lse_ref[block] = top + jnp.log2(total)


def attend_back_kernel(
    span,
    prompt_blocks,
    cont_blocks,
    info_ref,
    qkv_ref,
    grad_ref,
    exact_ref,
    lse_ref,
    cos_ref,
    sin_ref,
    out_ref,
    key_sum,
    value_sum,
):
    block = pl.program_id(0)
    blocks = pl.num_programs(0)
    small = qkv_ref.shape[2]
    rows = small * span
    scale = LOG2E / math.sqrt(HEAD)

    def at(block):
        return pl.ds(block * span, span)

    def flat(values):
        return values.reshape(rows, HEAD)

    def split(values):
        return values.reshape(span, small, HEAD)

    query = flat(qkv_ref[at(block), 0])
    first, ahead, start, limit = block_facts(block, rows, prompt_blocks, cont_blocks, info_ref)
    valid = start + lax.broadcasted_iota(jnp.int32, (rows, 1), 0) < limit
    grad_full = jnp.where(valid, flat(grad_ref[at(block)]).astype(f32), 0.0)
    grad = grad_full.astype(bf16)
    delta = jnp.sum((grad_full * flat(exact_ref[at(block)])).T, axis=0, keepdims=True)
    log_total = lse_ref[block]

    def visit(key_block, bias, fresh, query_sum):
        key = flat(qkv_ref[at(key_block), 1])
        scores = dot_nt(key, query) * scale + bias
        weights = jnp.exp2(scores - log_total)
        weight_grad = dot_nt(flat(qkv_ref[at(key_block), 2]), grad)
        score_grad = (weights * (weight_grad - delta)).astype(bf16)
        value_term = dot_nn(weights.astype(bf16), grad)
        key_term = dot_nn(score_grad, query)
        if fresh:
            value_sum[key_block] = value_term
            key_sum[key_block] = key_term
        else:
            value_sum[key_block] += value_term
            key_sum[key_block] += key_term
        return query_sum + dot_tn(key, score_grad)

    query_sum = visit_blocks(
        visit, block, rows, first, ahead, info_ref, jnp.zeros((HEAD, rows), f32)
    )
    back = 1.0 / math.sqrt(HEAD)

    ahead_tables = cos_ref.shape[0] - qkv_ref.shape[0]

    def unturn(values, block):
        where = pl.ds(ahead_tables + block * span, span)
        return split(turn(values * back, flat(cos_ref[where]), -flat(sin_ref[where])).astype(bf16))

    out_ref[at(block), 0] = unturn(query_sum.T, block)

    @pl.when(block == blocks - 1)
    def _():
        @pl.loop(0, blocks)
        def _(key_block):
            out_ref[at(key_block), 1] = unturn(key_sum[key_block], key_block)
            out_ref[at(key_block), 2] = split(value_sum[key_block].astype(bf16))


def mix_out_kernel(me_ref, near_ref, far_ref, w_near_ref, w_y_ref, w_x_ref, keep_ref, send_ref):
    heads = near_ref.shape[0] // PLACES
    side = me_ref[1] % 2
    for step, out_ref in enumerate((keep_ref, send_ref)):
        near, far = (
            jnp.concatenate([ref[step * heads + j] for j in range(heads)], axis=1)
            for ref in (near_ref, far_ref)
        )
        for which, w_ref in ((side, w_y_ref), (1 - side, w_x_ref)):
            columns = half_columns(which, w_ref)
            term = dot_nn(near, w_near_ref[:, columns]) + dot_nn(far, w_ref[...])
            out_ref[:, columns] = term.astype(out_ref.dtype)


def heads_back_kernel(me_ref, own_ref, beside_ref, w_near_ref, w_y_ref, w_x_ref, near_ref, far_ref):
    heads = near_ref.shape[0] // 2
    side = me_ref[1] % 2
    for step, ref in enumerate((own_ref, beside_ref)):
        near = dot_nt(ref[...], w_near_ref[...])
        far = sum(
            dot_nt(ref[:, half_columns(which, w_ref)], w_ref[...])
            for which, w_ref in ((side, w_y_ref), (1 - side, w_x_ref))
        )
        for value, out_ref in ((near, near_ref), (far, far_ref)):
            low = value.astype(bf16)
            for head in range(heads):
                out_ref[step * heads + head] = low[:, head * HEAD : (head + 1) * HEAD]


def project_back_kernel(me_ref, pieces_ref, w_ref, keep_ref, send_ref):
    step = pl.program_id(0)
    heads = pieces_ref.shape[0]
    pieces = jnp.concatenate(
        [pieces_ref[head, kind] for kind in range(3) for head in range(heads)], axis=1
    )
    rows = w_ref.shape[1]
    for target, parity in ((keep_ref, 0), (send_ref, 1)):

        @pl.when(step % 2 == parity)
        def _(target=target):
            for place in range(PLACES):
                term = dot_nt(pieces, w_ref[place])
                target[0, :, columns_of(me_ref, place, rows)] = term.astype(bf16)


def project_grad_kernel(
    me_ref,
    pieces_ref,
    x0,
    x1,
    x2,
    x3,
    gain_ref,
    w_ref,
    two_ref,
    three_ref,
    four_ref,
    keep_ref,
    late_ref,
    early_ref,
    x_scr,
    total,
    lanes_scr,
    gains_scr,
):
    step = pl.program_id(0)
    heads = pieces_ref.shape[0]
    choose(step, (x0, x1, x2, x3), x_scr)
    pieces = jnp.concatenate(
        [pieces_ref[head, kind] for kind in range(3) for head in range(heads)], axis=1
    )
    x = x_scr[...].astype(f32)
    normed = (x * inverse_rms(x) * gain_ref[...]).astype(bf16)
    term = dot_tn(normed, pieces)

    @pl.when(step == 0)
    def _():
        total[...] = term

    @pl.when(step > 0)
    def _():
        total[...] += term

    @pl.when(step == pl.num_programs(0) - 1)
    def _():
        rows, columns = w_ref.shape[1:]
        refs = (keep_ref, late_ref, early_ref)
        spread_rows(me_ref, total, refs, slice(0, columns))
        for place in range(PLACES):
            where = columns_of(me_ref, place, rows)
            product = total[where, :] * w_ref[place].astype(f32)
            lanes_scr[where, :] = sum(
                product[:, first : first + HEAD] for first in range(0, columns, HEAD)
            )
        one = jnp.sum(lanes_scr[...].T, axis=0, keepdims=True) / gain_ref[...]
        gains = jnp.concatenate([one, two_ref[...], three_ref[...], four_ref[...]], axis=0)
        high = gains.astype(bf16).astype(f32)
        gains_scr[...] = jnp.concatenate([high, gains - high], axis=0)
        shards, piece_rows = keep_ref.shape[1:3]
        for ref, owner in piece_views(me_ref, refs):
            part = gains_scr[:, pl.ds(pl.multiple_of(owner * HEAD, HEAD), HEAD)]
            rest = jnp.zeros((piece_rows - part.shape[0], HEAD), f32)
            block = jnp.concatenate([part, rest], axis=0).astype(bf16)
            for shard in range(shards):
                ref[shard, :, columns:] = block


def middle_kernel(keep_ref, received_ref, x_ref, two_ref, three_ref, branch_ref, middle_ref, input_ref):
    branch = keep_ref[...] + received_ref[...].astype(f32)
    middle = x_ref[...].astype(f32) + branch * inverse_rms(branch) * two_ref[...]
    branch_ref[...] = branch
    middle_ref[...] = middle
    input_ref[...] = (middle * inverse_rms(middle) * three_ref[...]).astype(bf16)


def norm_back_parts(values, gain, upstream):
    inverse = inverse_rms(values)
    weighted = upstream * gain
    inner = jnp.mean(values * weighted, axis=-1, keepdims=True)
    value_grad = inverse * weighted - values * (inverse * inverse * inverse * inner)
    return value_grad, jnp.sum(upstream * values * inverse, axis=0, keepdims=True)


def turnaround_kernel(
    keep_ref, received_ref, middle_ref, grad_ref, four_ref, out_ref, back_ref, gain_ref
):
    ff_out = keep_ref[...] + received_ref[...].astype(f32)
    out_ref[...] = (middle_ref[...] + ff_out * inverse_rms(ff_out) * four_ref[...]).astype(bf16)
    value_grad, gain = norm_back_parts(ff_out, four_ref[...], grad_ref[...].astype(f32))
    back_ref[...] = value_grad.astype(bf16)
    gain_ref[...] = gain


def branch_back_kernel(
    keep_ref,
    received_ref,
    middle_ref,
    branch_ref,
    grad_ref,
    two_ref,
    three_ref,
    middle_grad_ref,
    branch_grad_ref,
    gain_two_ref,
    gain_three_ref,
):
    input_grad = keep_ref[...] + received_ref[...].astype(f32)
    middle_part, gain_three_ref[...] = norm_back_parts(middle_ref[...], three_ref[...], input_grad)
    middle_grad = grad_ref[...].astype(f32) + middle_part
    middle_grad_ref[...] = middle_grad
    branch_grad, gain_two_ref[...] = norm_back_parts(branch_ref[...], two_ref[...], middle_grad)
    branch_grad_ref[...] = branch_grad.astype(bf16)


def input_back_kernel(
    keep_ref, received_ref, across_ref, x_ref, middle_grad_ref, one_ref, out_ref
):
    normed_grad = keep_ref[0].astype(f32) + received_ref[0].astype(f32) + across_ref[...].astype(f32)
    part, _ = norm_back_parts(x_ref[...].astype(f32), one_ref[...], normed_grad)
    out_ref[...] = middle_grad_ref[...] + part


class Weights:
    def __init__(self, me_ref, refs, pair_scr, down_scr, sems):
        own, beside, far_y, far_x, corner_y, corner_x, down_near, *down_far = refs
        side = me_ref[1] % 2
        rows = far_y.shape[0]
        half = down_far[0].shape[1]
        moves = []
        for turn_index, far, corner in ((0, far_y, corner_y), (1, far_x, corner_x)):
            block = turn_index ^ side
            for place, source in enumerate((own.at[block], beside.at[block], far, corner)):
                target = pair_scr.at[turn_index, place * rows : (place + 1) * rows]
                moves.append((source, target))
        moves.append((down_near, down_scr.at[0]))
        for index, source in enumerate(down_far):
            moves.append((source, down_scr.at[1, :, index * half : (index + 1) * half]))
        self.copies = [
            pltpu.make_async_copy(source, target, sems.at[index])
            for index, (source, target) in enumerate(moves)
        ]
        self.pair_scr, self.down_scr = pair_scr, down_scr

    COUNT = 11
    DOWN = range(8, 11)

    def start(self, order):
        for index in order:
            self.copies[index].start()

    def wait(self, order):
        for index in order:
            self.copies[index].wait()

    def wait_turn(self, turn_index):
        for index in range(2):

            @pl.when(turn_index == index)
            def _(index=index):
                self.wait(self.turn(index))

    @staticmethod
    def turn(turn_index):
        return range(4 * turn_index, 4 * turn_index + 4)


def put_rows(scr, place_major, me_ref, *refs):
    rows, width = refs[0].shape
    size = width // PLACES
    for index, ref in enumerate(refs):
        where = slice(index * rows, (index + 1) * rows)
        if place_major:
            for place in range(PLACES):
                scr[where, place * size : (place + 1) * size] = ref[:, columns_of(me_ref, place, size)]
        else:
            scr[where, :] = ref[...]


def gate_parts(pair, half):
    def parts(gate, upward):
        sigma = 1.0 / (1.0 + jnp.exp(-gate))
        swish = gate * sigma
        slope = upward * sigma * (1.0 + gate * (1.0 - sigma))
        return swish, slope, (swish * upward).astype(bf16)

    main = half // HEAD * HEAD
    rest = half - main
    body = parts(pair[:, :main], pair[:, main : 2 * main])
    edge = pair[:, 2 * main :]
    edge_swish, edge_slope, edge_hidden = parts(edge, pltpu.roll(edge, rest, 1))
    lane = lax.broadcasted_iota(jnp.int32, edge.shape, 1)
    edge_factor = jnp.where(lane < rest, edge_slope, pltpu.roll(edge_swish, rest, 1))
    return body, edge_factor, edge_hidden


def put_hidden(ref, body, edge, main):
    rows = ref.shape[1]
    for row in range(2):
        where = slice(row * rows, (row + 1) * rows)
        ref[row, :, :main] = body[where]
        ref[row, :, main:] = edge[where]


def ff_kernel(me_ref, own_ref, beside_ref, *refs):
    weight_refs, (keep_ref, send_ref, saved_ref, hidden_ref) = refs[:9], refs[9:13]
    x_scr, hidden_scr, saved_scr, total, pair_w, down_w, sems, saved_sems = refs[13:]
    weights = Weights(me_ref, weight_refs, pair_w, down_w, sems)
    weights.start([*weights.turn(0), *weights.DOWN, *weights.turn(1)])
    put_rows(x_scr, True, me_ref, own_ref, beside_ref)
    half = down_w.shape[1]
    main = half // HEAD * HEAD
    total[...] = jnp.zeros_like(total)

    def save(turn_index):
        return pltpu.make_async_copy(
            saved_scr.at[turn_index], saved_ref.at[turn_index], saved_sems.at[turn_index]
        )

    @pl.loop(0, 2)
    def _(turn_index):
        block = turn_index ^ (me_ref[1] % 2)
        weights.wait_turn(turn_index)
        pair = dot_nn(x_scr[...], pair_w[turn_index])
        (swish, slope, hidden), edge_factor, edge_hidden = gate_parts(pair, half)
        saved_scr[turn_index, :, :main] = slope.astype(bf16)
        saved_scr[turn_index, :, main : 2 * main] = swish.astype(bf16)
        saved_scr[turn_index, :, 2 * main :] = edge_factor.astype(bf16)
        save(turn_index).start()
        hidden_scr[:, :main] = hidden
        hidden_scr[:, main:] = edge_hidden

        @pl.when(block == 0)
        def _():
            put_hidden(hidden_ref, hidden, edge_hidden, main)

        @pl.when(turn_index == 0)
        def _():
            weights.wait(weights.DOWN)

        total[...] += dot_nn(hidden_scr[:, :half], down_w[block])

    rows = keep_ref.shape[0]
    keep_ref[...] = total[:rows]
    send_ref[...] = total[rows:].astype(bf16)
    for turn_index in range(2):
        save(turn_index).wait()


def put_pair_grad(target, hidden_grad, factors, half):
    main = half // HEAD * HEAD
    edge = hidden_grad[:, main:]
    edge = jnp.concatenate([edge, edge], axis=1)
    for values, start in ((hidden_grad[:, :main], 0), (hidden_grad[:, :main], main), (edge, 2 * main)):
        columns = slice(start, start + values.shape[1])
        target[:, columns] = (values * factors[:, columns].astype(f32)).astype(bf16)


def ff_back_kernel(me_ref, own_ref, beside_ref, *refs):
    weight_refs, saved_ref, (keep_ref, send_ref, pair_ref) = refs[:9], refs[9], refs[10:13]
    grad_scr, pair_scr, total, pair_w, down_w, sems = refs[13:]
    weights = Weights(me_ref, weight_refs, pair_w, down_w, sems)
    weights.start([*weights.DOWN, *weights.turn(0), *weights.turn(1)])
    put_rows(grad_scr, False, me_ref, own_ref, beside_ref)
    half, width = down_w.shape[1:]
    rows = keep_ref.shape[0]
    size = width // PLACES
    weights.wait(weights.DOWN)
    total[...] = jnp.zeros_like(total)

    @pl.loop(0, 2)
    def _(turn_index):
        block = turn_index ^ (me_ref[1] % 2)
        hidden_grad = dot_nt(grad_scr[...], down_w[block])
        put_pair_grad(pair_scr, hidden_grad, saved_ref.at[turn_index], half)

        @pl.when(block == 0)
        def _():
            for row in range(2):
                pair_ref[row] = pair_scr[row * rows : (row + 1) * rows]

        weights.wait_turn(turn_index)
        total[...] += dot_nt(pair_scr[...], pair_w[turn_index])

    for place in range(PLACES):
        where = slice(place * size, (place + 1) * size)
        columns = columns_of(me_ref, place, size)
        keep_ref[:, columns] = total[:rows, where]
        send_ref[:, columns] = total[rows:, where].astype(bf16)


def ff_far_kernel(
    me_ref, x2_ref, x3_ref, grad2_ref, grad3_ref, *refs
):
    own, beside, far_y, far_x, corner_y, corner_x, down_near, hidden_ref, pair_ref = refs[:9]
    x_scr, factor_scr, pair_w = refs[9:]
    half = down_near.shape[0]
    main = half // HEAD * HEAD
    rows = x2_ref.shape[0]
    pair_w[:rows] = own[0]
    pair_w[rows : 2 * rows] = beside[0]
    for index, far in enumerate(((far_y, corner_y), (far_x, corner_x))):

        @pl.when(me_ref[1] % 2 == index)
        def _(far=far):
            pair_w[2 * rows : 3 * rows] = far[0][...]
            pair_w[3 * rows :] = far[1][...]

    put_rows(x_scr, True, me_ref, x2_ref, x3_ref)
    (swish, slope, hidden), edge_factor, edge_hidden = gate_parts(dot_nn(x_scr[...], pair_w[...]), half)
    put_hidden(hidden_ref, hidden, edge_hidden, main)
    factor_scr[:, :main] = slope.astype(bf16)
    factor_scr[:, main : 2 * main] = swish.astype(bf16)
    factor_scr[:, 2 * main :] = edge_factor.astype(bf16)
    put_rows(x_scr, False, me_ref, grad2_ref, grad3_ref)
    hidden_grad = dot_nt(x_scr[...], down_near[...])
    for row in range(2):
        where = slice(row * rows, (row + 1) * rows)
        put_pair_grad(pair_ref.at[row], hidden_grad[where], factor_scr.at[where], half)


def piece_height(me_ref, ahead):
    size = 4
    return (me_ref[1] // 2 + ahead) % size


def piece_owner(me_ref, other_x, ahead):
    return (me_ref[1] % 2 ^ other_x) + 2 * piece_height(me_ref, ahead)


def piece_views(me_ref, refs):
    keep, late, early = refs
    for ahead in range(4):
        yield keep.at[ahead], piece_owner(me_ref, 0, ahead)
        yield (late, early)[ahead // 2].at[ahead % 2], piece_owner(me_ref, 1, ahead)


def spread_rows(me_ref, total, refs, columns=slice(None), contiguous=False):
    shards, piece_rows = refs[0].shape[1:3]
    for ref, owner in piece_views(me_ref, refs):
        for shard in range(shards):
            block = owner * shards + shard if contiguous else shard * 8 + owner
            start = pl.multiple_of(block * piece_rows, 8)
            ref[shard, :, columns] = total[pl.ds(start, piece_rows), :].astype(bf16)


def piece_shapes(shape):
    return [(count,) + shape for count in (4, 2, 2)]


def over_x(late, early):
    early = ctx_swap(early, 1)
    late = ctx_swap(after(late, early), 1)
    return [late[0], late[1], early[0], early[1]], early


def weight_grads_kernel(sources, me_ref, *refs):
    operands, refs = refs[: sum(4 + count for count, _ in sources)], refs[len(sources) * 4 + sum(count for count, _ in sources) :]
    outs, scratch, sems = refs[:3], refs[3:-1], refs[-1]
    lefts, rights, totals = scratch[0::3], scratch[1::3], scratch[2::3]
    copies, groups = [], []

    def fetch(source, target):
        copies.append(pltpu.make_async_copy(source, target, sems.at[len(copies)]))

    for (count, _), left, right in zip(sources, lefts, rights, strict=True):
        first = len(copies)
        columns = right.shape[2]
        for place in range(PLACES):
            fetch(operands[place], left.at[place])
            if count == 2:
                fetch(operands[4 + place // 2].at[place % 2], right.at[place])
            else:
                heads = operands[4].shape[0] // PLACES
                for head in range(heads):
                    where = slice(head * HEAD, (head + 1) * HEAD)
                    fetch(operands[4].at[place * heads + head], right.at[place, :, where])
        operands = operands[4 + count :]
        groups.append(range(first, len(copies)))
    for copy in copies:
        copy.start()
    first = 0
    for (_, contiguous), group, left, right, total in zip(
        sources, groups, lefts, rights, totals, strict=True
    ):
        for index in group:
            copies[index].wait()
        columns = total.shape[1]
        total[...] = jnp.zeros_like(total)

        @pl.loop(0, PLACES)
        def _(place, left=left, right=right, total=total, columns=columns):
            total[...] += dot_tn(left[place], right[place, :, :columns])

        spread_rows(me_ref, total, outs, slice(first, first + columns), contiguous)
        first += columns


def weight_grads(me, name, expected, sources):
    rows, width = sources[0][0][0].shape
    operands, kinds, columns, scratch, moves = [me], [], [], [], 0
    for lefts, rights, count, contiguous in sources:
        operands += [*lefts, *rights]
        kinds.append((len(rights), contiguous))
        columns.append(count)
        held = count if len(rights) == 1 else rights[0].shape[2]
        scratch += [
            pltpu.VMEM((PLACES, rows, width), bf16),
            pltpu.VMEM((PLACES, rows, held), bf16),
            pltpu.VMEM((width, count), f32),
        ]
        moves += 2 * PLACES if len(rights) == 2 else PLACES + rights[0].shape[0]
    pieces = piece_shapes((PLACES, width // PLACES // 8, sum(columns)))
    return pl.pallas_call(
        functools.partial(weight_grads_kernel, tuple(kinds)),
        name=name,
        cost_estimate=cost(expected),
        grid=(1,),
        in_specs=[SMEM] + [pl.BlockSpec(memory_space=pl.ANY)] * (len(operands) - 1),
        out_specs=[whole(piece) for piece in pieces],
        out_shape=[shaped(*piece) for piece in pieces],
        scratch_shapes=scratch + [pltpu.SemaphoreType.DMA((moves,))],
        compiler_params=params(32, "arbitrary"),
    )(*operands)


def low_sum(*terms):
    return sum(term.astype(f32) for term in terms).astype(bf16)


def over_z(terms):
    running = low_sum(*terms[3])
    for ahead in (2, 1, 0):
        running = low_sum(*terms[ahead], z_shift(running))
    return running


def spread_piece(piece):
    near, far = [piece], []
    for step in range(3):
        ready = near[-1] if step == 0 else after(near[-1], far[-1])
        far.append(ctx_swap(near[-1], 1))
        near.append(z_shift(ready))
    return near + far + [ctx_swap(after(near[-1], far[-1]), 1)]


def settle_qkv_kernel(me_ref, *refs):
    pieces, outs, gains_ref = refs[:8], refs[8:11], refs[11]
    shards, rows, columns = pieces[0].shape
    part = columns // 3 // HEAD * HEAD
    count = gains_ref.shape[0]
    for index, ref in enumerate(pieces):
        owner = piece_owner(me_ref, index // 4, -(index % 4))
        where = pl.ds(pl.multiple_of(owner * rows, rows), rows)
        gains = 0.0
        for shard in range(shards):
            for kind, out in enumerate(outs):
                out[where, shard * part : (shard + 1) * part] = ref[
                    shard, :, kind * part : (kind + 1) * part
                ].astype(f32)
            gains = gains + ref[shard, :16, 3 * part :].astype(f32)
        stretch = pl.ds(pl.multiple_of(owner * HEAD, HEAD), HEAD)
        gains_ref[:, stretch] = gains[:count] + gains[count : 2 * count]


def settle_pair_kernel(me_ref, *refs):
    pieces, outs = refs[:8], refs[8:]
    shards, rows, columns = pieces[0].shape
    half = columns // 2
    for index, ref in enumerate(pieces):
        owner = piece_owner(me_ref, index // 4, -(index % 4))
        where = pl.ds(pl.multiple_of(owner * rows, rows), rows)
        for kind, start, source, size in pair_columns(half):
            for shard in range(shards):
                first = shard * half + start
                outs[kind][where, first : first + size] = ref[
                    shard, :, source : source + size
                ].astype(f32)


def settle_turned_kernel(me_ref, *refs):
    pieces, (down_ref, out_ref) = refs[:8], refs[8:]
    shards, rows = pieces[0].shape[:2]
    half = down_ref.shape[0]
    for index, ref in enumerate(pieces):
        owner = piece_owner(me_ref, index // 4, -(index % 4))
        stretch = jnp.concatenate([ref[shard].astype(f32) for shard in range(shards)], axis=0)
        columns = pl.ds(pl.multiple_of(owner * shards * rows, shards * rows), shards * rows)
        down_ref[:, columns] = stretch[:, :half].T
        out_ref[:, columns] = stretch[:, half:].T


def settle(kernel, name, me, pieces, outs):
    return pl.pallas_call(
        kernel,
        name=name,
        grid=(1,),
        in_specs=[SMEM] + [whole(pieces[0].shape)] * 8,
        out_specs=[whole(out) for out in outs],
        out_shape=[shaped(*out, kind=f32) for out in outs],
        cost_estimate=cost(4),
        compiler_params=params(40),
    )(me, *pieces)


def shaped(*shape, kind=bf16):
    return jax.ShapeDtypeStruct(shape, kind)


def rope_tables(base, count):
    half = HEAD // 2
    frequencies = rope_base ** (-2.0 * jnp.arange(half, dtype=f32) / HEAD)
    frequencies = jnp.concatenate([frequencies, frequencies])
    sign = jnp.where(jnp.arange(HEAD) < half, -1.0, 1.0)
    blocks = base.shape[0]
    places = jnp.concatenate([base, jnp.arange(count, dtype=base.dtype)])
    angles = places.astype(f32)[:, None] * frequencies
    cosine, sine = jnp.cos(angles), jnp.sin(angles)
    cos_base, sin_base = cosine[:blocks, None], sine[:blocks, None]
    cos_step, sin_step = cosine[None, blocks:], sine[None, blocks:]
    return (
        cos_base * cos_step - sin_base * sin_step,
        (sin_base * cos_step + cos_base * sin_step) * sign,
    )


def pair_shards(
    block_in,
    out_grad,
    w_query,
    w_key,
    w_value,
    w_out,
    norm_one,
    norm_two,
    w_gate,
    w_up,
    w_down,
    norm_three,
    norm_four,
    prompt_len,
    cont_len,
    group_ids,
    cont_ids,
):
    rows, width = block_in.shape[1:]
    ctx_size = lax.axis_size("ctx")
    heads = width // HEAD // PLACES
    part = heads * HEAD
    prompt = P_DEV * ctx_size
    prompt_chunks, cont_chunks = prompt // rows, CONT // rows
    ff_part = w_down.shape[0]
    my_row = lax.axis_index("fsdp")
    my_chunk = lax.axis_index("ctx")
    me = jnp.stack([my_row, my_chunk]).astype(jnp.int32)
    groups, slots = cont_ids.shape
    gain_one, gain_two, gain_three, gain_four = (
        gain[None, :] for gain in (norm_one, norm_two, norm_three, norm_four)
    )
    x_own, grad_own = block_in[0], out_grad[0]
    row_spec, gain_spec = whole((rows, width)), whole((1, width))
    full_row, low_row, gain_row = (
        shaped(rows, width, kind=f32),
        shaped(rows, width),
        shaped(1, width, kind=f32),
    )

    x_across = y_swap(x_own)
    qkv_block, qkv_half, mix_half = (rows, 3 * part), (rows, 3 * part // 2), (part, width // 2)
    split_shapes = [qkv_block, qkv_block, qkv_half, qkv_half, mix_half]
    qkv_own, qkv_beside, qkv_far, qkv_corner, w_out_sent = pl.pallas_call(
        split_qkv_kernel,
        name="split_qkv",
        cost_estimate=cost(2),
        grid=(1,),
        in_specs=[SMEM] + [whole((rows, width))] * 3 + [whole((part, width))],
        out_specs=[whole(shape) for shape in split_shapes],
        out_shape=[shaped(*shape) for shape in split_shapes],
        scratch_shapes=[pltpu.VMEM(qkv_block, bf16)],
        compiler_params=params(58),
    )(me, w_query, w_key, w_value, w_out)
    qkv_far = y_swap(qkv_far)
    qkv_corner = lax.ppermute(qkv_corner, "fsdp", [(i, i ^ 3) for i in range(4)])
    w_qkv = [
        qkv_own,
        core_swap(qkv_beside),
        qkv_far,
        ctx_swap(qkv_far, 1),
        qkv_corner,
        ctx_swap(qkv_corner, 1),
    ]
    x_beside = core_swap(x_own)
    x_all = [x_own, x_beside, x_across, core_swap(x_across)]

    row_of = my_row ^ jnp.arange(PLACES, dtype=jnp.int32)
    group_range = jnp.arange(groups, dtype=jnp.int32)
    slot_range = jnp.arange(slots, dtype=jnp.int32)
    pick_row = row_of[:, None] == group_range[None, :]
    group_of = jnp.sum(jnp.where(pick_row, group_ids[None, :], 0), axis=1)
    pick_group = group_of[:, None] == group_range[None, :]
    prompt_of = jnp.sum(jnp.where(pick_group, prompt_len[None, :], 0), axis=1)
    lens_of = jnp.sum(jnp.where(pick_group[:, :, None], cont_len[None], 0), axis=1)
    ids_of = jnp.sum(jnp.where(pick_row[:, :, None], cont_ids[None], 0), axis=1)
    slot_lens = jnp.sum(
        jnp.where(ids_of[:, :, None] == slot_range, lens_of[:, None, :], 0), axis=2
    )
    pick_pair = jnp.arange(PLACES, dtype=jnp.int32) == my_chunk // heads
    pair_prompt = jnp.sum(jnp.where(pick_pair, prompt_of, 0))
    pair_lens = jnp.sum(jnp.where(pick_pair[:, None], slot_lens, 0), axis=0)
    info = jnp.concatenate([pair_prompt[None], pair_lens])

    def first_position(slot, prompt_size):
        return jnp.where(slot >= prompt, prompt_size + (slot - prompt) % CONT, slot)

    starts = jnp.arange(ctx_size, dtype=jnp.int32) * rows
    bases = jnp.concatenate(
        [first_position(my_chunk * rows, prompt_of), first_position(starts, pair_prompt)]
    )
    cos_tables, sin_tables = rope_tables(bases, rows)
    w_qkv = after(w_qkv, cos_tables, sin_tables, info)

    ff_blocks, ff_block = (2, rows, 2 * ff_part), (rows, 2 * ff_part)
    split_shapes = [ff_blocks, ff_block, ff_blocks, ff_block] + [(ff_part, width // 2)] * 2
    ff_own, ff_own_sent, ff_beside, ff_beside_sent, left_sent, right_sent = pl.pallas_call(
        split_ff_kernel,
        name="split_ff",
        cost_estimate=cost(3),
        grid=(1,),
        in_specs=[SMEM] + [whole(w_gate.shape)] * 2 + [whole(w_down.shape)],
        out_specs=[whole(shape) for shape in split_shapes],
        out_shape=[shaped(*shape) for shape in split_shapes],
        compiler_params=params(58),
    )(me, w_gate, w_up, w_down)
    w_qkv, x_all, w_out_sent, ff_beside_sent = tie(w_qkv, x_all, w_out_sent, ff_beside_sent)
    w_ff_beside = core_swap(ff_beside)
    ff_beside_sent = core_swap(ff_beside_sent)
    w_out_y = y_swap(w_out_sent)
    w_out_x = ctx_swap(w_out_y, 1)
    far_y = y_swap(after(ff_own_sent, w_out_y))
    far_x = ctx_swap(far_y, 1)
    corner_y = y_swap(after(ff_beside_sent, far_y))
    corner_x = ctx_swap(corner_y, 1)
    down_left = y_swap(after(left_sent, corner_y))
    down_right = y_swap(after(right_sent, down_left))

    piece = (heads, 3, rows, HEAD)
    qkv, w_qkv = pl.pallas_call(
        project_kernel,
        name="project",
        cost_estimate=cost(4),
        grid=(PLACES,),
        in_specs=[SMEM]
        + [row_spec] * 4
        + [gain_spec]
        + [whole(qkv_block)] * 2
        + [whole(qkv_half)] * 4
        + [pl.BlockSpec((1, rows, HEAD), lambda t: (t, 0, 0))] * 2,
        out_specs=[pl.BlockSpec(piece, lambda t: (t, 0, 0, 0)), whole((PLACES,) + qkv_block)],
        out_shape=[shaped(PLACES * heads, 3, rows, HEAD), shaped(PLACES, *qkv_block)],
        scratch_shapes=[pltpu.VMEM((rows, width), bf16)] * 2,
        compiler_params=params(58, "arbitrary"),
    )(me, *x_all, gain_one, *w_qkv, cos_tables, sin_tables)
    qkv = lax.all_to_all(after(qkv, w_out_y), "ctx", 0, 0, tiled=True)
    qkv = after(qkv, far_x, corner_y)

    qkv_shape, head_shape = (ctx_size, 3, rows, HEAD), (ctx_size, rows, HEAD)
    span = math.gcd(prompt_chunks, cont_chunks)
    blocks = ctx_size // span
    block_shape, lse_shape = (blocks, span * rows, HEAD), (blocks, 1, span * rows)
    block_counts = (span, prompt_chunks // span, cont_chunks // span)
    mixed, exact, log_total = pl.pallas_call(
        functools.partial(attend_kernel, *block_counts),
        name="attend",
        cost_estimate=cost(9),
        grid=(blocks,),
        in_specs=[SMEM, whole(qkv_shape)],
        out_specs=[whole(head_shape), whole(head_shape), whole(lse_shape)],
        out_shape=[
            shaped(*head_shape),
            shaped(*head_shape, kind=f32),
            shaped(*lse_shape, kind=f32),
        ],
        compiler_params=params(58, "arbitrary"),
    )(info, qkv)
    mixed = after(mixed, corner_x, down_left)
    attended = lax.all_to_all(mixed, "ctx", 0, 0, tiled=True)
    attended = after(attended, down_right, w_out_x)
    attended_far = y_swap(attended[2 * heads :])

    two_heads = (2 * heads, rows, HEAD)
    mix_specs = [whole((part, width))] + [whole(mix_half)] * 2
    keep, send = pl.pallas_call(
        mix_out_kernel,
        name="mix_out",
        cost_estimate=cost(2),
        grid=(1,),
        in_specs=[SMEM, whole((PLACES * heads, rows, HEAD)), whole(two_heads)] + mix_specs,
        out_specs=[row_spec] * 2,
        out_shape=[full_row, low_row],
        compiler_params=params(10),
    )(me, attended, attended_far, w_out, w_out_y, w_out_x)

    branch, middle, ff_input = pl.pallas_call(
        middle_kernel,
        name="middle",
        cost_estimate=cost(2),
        grid=(1,),
        in_specs=[row_spec] * 3 + [gain_spec] * 2,
        out_specs=[row_spec] * 3,
        out_shape=[full_row, full_row, low_row],
        compiler_params=params(10),
    )(keep, core_swap(send), x_own, gain_two, gain_three)
    ff_input_beside = core_swap(ff_input)
    ff_input_far = far_rows(ff_input)

    far_pairs = [far_y, far_x, corner_y, corner_x]
    far_weights = far_pairs + [w_down, down_left, down_right]

    both = 2 * rows
    padded = pl.cdiv(ff_part, HEAD) * HEAD
    saved_shape = (2, both, 2 * ff_part)
    hidden_shape, pair_shape = (2, rows, padded), (2, rows, 2 * ff_part)
    anywhere = pl.BlockSpec(memory_space=pl.ANY)

    def ff_call(kernel, name, expected, more_in, outs, scratch, last=()):
        return pl.pallas_call(
            kernel,
            name=name,
            cost_estimate=cost(expected),
            grid=(1,),
            in_specs=[SMEM] + [row_spec] * 2 + [anywhere] * 9 + more_in,
            out_specs=[spec for spec, _ in outs],
            out_shape=[shape for _, shape in outs],
            scratch_shapes=scratch
            + [
                pltpu.VMEM((both, width), f32),
                pltpu.VMEM((2, width, 2 * ff_part), bf16),
                pltpu.VMEM((2, ff_part, width), bf16),
                pltpu.SemaphoreType.DMA((Weights.COUNT,)),
                *last,
            ],
            compiler_params=params(40, "arbitrary"),
        )

    keep, send, ff_saved, hidden = ff_call(
        ff_kernel,
        "ff",
        9,
        [],
        [
            (row_spec, full_row),
            (row_spec, low_row),
            (anywhere, shaped(*saved_shape)),
            (whole(hidden_shape), shaped(*hidden_shape)),
        ],
        [
            pltpu.VMEM((both, width), bf16),
            pltpu.VMEM((both, padded), bf16),
            pltpu.VMEM(saved_shape, bf16),
        ],
        [pltpu.SemaphoreType.DMA((2,))],
    )(me, ff_input, ff_input_beside, ff_own, w_ff_beside, *far_weights)
    send = after(send, ff_input_far[0])
    block_out, ff_grad, part_four = pl.pallas_call(
        turnaround_kernel,
        name="turnaround",
        cost_estimate=cost(2),
        grid=(1,),
        in_specs=[row_spec] * 4 + [gain_spec],
        out_specs=[row_spec, row_spec, gain_spec],
        out_shape=[low_row, low_row, gain_row],
        compiler_params=params(10),
    )(keep, core_swap(send), middle, grad_own, gain_four)

    ff_grad_beside = core_swap(ff_grad)
    ff_grad_far = far_rows(ff_grad)
    keep, send, pair_grad = ff_call(
        ff_back_kernel,
        "ff_back",
        9,
        [whole(saved_shape)],
        [(row_spec, full_row), (row_spec, low_row), (whole(pair_shape), shaped(*pair_shape))],
        [pltpu.VMEM((both, width), bf16), pltpu.VMEM((both, 2 * ff_part), bf16)],
    )(me, ff_grad, ff_grad_beside, ff_own, w_ff_beside, *far_weights, ff_saved)
    send = after(send, ff_grad_far[0])

    middle_grad, branch_grad, part_two, part_three = pl.pallas_call(
        branch_back_kernel,
        name="branch_back",
        cost_estimate=cost(2),
        grid=(1,),
        in_specs=[row_spec] * 5 + [gain_spec] * 2,
        out_specs=[row_spec, row_spec, gain_spec, gain_spec],
        out_shape=[full_row, low_row, gain_row, gain_row],
        compiler_params=params(10),
    )(keep, core_swap(send), middle, branch, grad_own, gain_two, gain_three)
    branch_grad_beside = core_swap(branch_grad)

    heads_near, heads_far = pl.pallas_call(
        heads_back_kernel,
        name="heads_back",
        cost_estimate=cost(2),
        grid=(1,),
        in_specs=[SMEM] + [row_spec] * 2 + mix_specs,
        out_specs=[whole(two_heads)] * 2,
        out_shape=[shaped(*two_heads)] * 2,
        compiler_params=params(10),
    )(me, branch_grad, branch_grad_beside, w_out, w_out_y, w_out_x)
    heads_far = y_swap(heads_far)
    ff_input_far, ff_grad_far = after((ff_input_far, ff_grad_far), heads_near)
    branch_grad_across = y_swap(branch_grad)

    near_share = pl.BlockSpec((1,) + ff_block, lambda *_: (0, 0, 0))
    hidden_far, pair_far = pl.pallas_call(
        ff_far_kernel,
        name="ff_far",
        cost_estimate=cost(6),
        grid=(1,),
        in_specs=[SMEM]
        + [row_spec] * 4
        + [near_share] * 2
        + [whole(ff_block)] * 4
        + [whole((ff_part, width))],
        out_specs=[whole(hidden_shape), whole(pair_shape)],
        out_shape=[shaped(*hidden_shape), shaped(*pair_shape)],
        scratch_shapes=[
            pltpu.VMEM((both, width), bf16),
            pltpu.VMEM((both, 2 * ff_part), bf16),
            pltpu.VMEM((width, 2 * ff_part), bf16),
        ],
        compiler_params=params(26),
    )(me, *ff_input_far, *ff_grad_far, ff_own, w_ff_beside, *far_pairs, w_down)
    pair_far = after(pair_far, heads_far)
    pair_keep, pair_late, pair_early = weight_grads(
        me,
        "pair_grads",
        7,
        [
            (
                [ff_input, ff_input_beside, *ff_input_far],
                [pair_grad, pair_far],
                2 * ff_part,
                False,
            )
        ],
    )
    heads_far = after(heads_far, pair_keep)
    attended_grad = lax.all_to_all(
        jnp.concatenate([heads_near, heads_far]), "ctx", 0, 0, tiled=True
    )
    branch_grad_far = [branch_grad_across, core_swap(branch_grad_across)]
    pair_over, pair_first = over_x(pair_late, pair_early)
    pair_run = low_sum(pair_keep[3], pair_over[3])
    pair_came = z_shift(pair_run)
    attended_grad = after(attended_grad, pair_run)

    pieces = pl.pallas_call(
        functools.partial(attend_back_kernel, *block_counts),
        name="attend_back",
        cost_estimate=cost(11),
        grid=(blocks,),
        in_specs=[
            SMEM,
            whole(qkv_shape),
            whole(head_shape),
            whole(head_shape),
            whole(lse_shape),
            whole(cos_tables.shape),
            whole(sin_tables.shape),
        ],
        out_specs=whole(qkv_shape),
        out_shape=shaped(*qkv_shape),
        scratch_shapes=[pltpu.VMEM(block_shape, f32)] * 2,
        compiler_params=params(58, "arbitrary"),
    )(info, qkv, attended_grad, exact, log_total, cos_tables, sin_tables)
    hidden, hidden_far = after((hidden, hidden_far), pieces)
    down_keep, down_late, down_early = weight_grads(
        me,
        "down_grads",
        8,
        [
            ([ff_grad, ff_grad_beside, *ff_grad_far], [hidden, hidden_far], ff_part, True),
            ([branch_grad, branch_grad_beside, *branch_grad_far], [attended], part, True),
        ],
    )
    pieces = lax.all_to_all(after(pieces, pair_came), "ctx", 0, 0, tiled=True)
    pieces = after(pieces, down_keep)

    piece_spec = pl.BlockSpec(piece, lambda t: (t, 0, 0, 0))
    qkv_pieces = piece_shapes((PLACES, rows // 8, 3 * part + HEAD))
    qkv_keep, qkv_late, qkv_early = pl.pallas_call(
        project_grad_kernel,
        name="project_grad",
        cost_estimate=cost(5),
        grid=(PLACES,),
        in_specs=[SMEM, piece_spec]
        + [row_spec] * 4
        + [gain_spec, whole((PLACES,) + qkv_block)]
        + [gain_spec] * 3,
        out_specs=[whole(shape) for shape in qkv_pieces],
        out_shape=[shaped(*shape) for shape in qkv_pieces],
        scratch_shapes=[
            pltpu.VMEM((rows, width), bf16),
            pltpu.VMEM((width, 3 * part), f32),
            pltpu.VMEM((width, HEAD), f32),
            pltpu.VMEM((8, width), f32),
        ],
        compiler_params=params(20, "arbitrary"),
    )(me, pieces, *x_all, gain_one, w_qkv, part_two, part_three, part_four)
    qkv_over, _ = over_x(qkv_late, qkv_early)
    pieces = after(pieces, qkv_keep)

    pair_rows = pl.BlockSpec((1, rows, width), lambda t: (t // 2, 0, 0))
    keep, send = pl.pallas_call(
        project_back_kernel,
        name="project_back",
        cost_estimate=cost(5),
        grid=(PLACES,),
        in_specs=[SMEM, piece_spec, whole((PLACES,) + qkv_block)],
        out_specs=[pair_rows, pair_rows],
        out_shape=[shaped(2, rows, width)] * 2,
        compiler_params=params(12, "arbitrary"),
    )(me, pieces, w_qkv)

    received = core_swap(send)
    onward = (keep[1].astype(f32) + received[1].astype(f32)).astype(bf16)
    in_grad = pl.pallas_call(
        input_back_kernel,
        name="input_back",
        cost_estimate=cost(2),
        grid=(1,),
        in_specs=[pl.BlockSpec((1, rows, width), lambda *_: (0, 0, 0))] * 2
        + [row_spec] * 3
        + [gain_spec],
        out_specs=row_spec,
        out_shape=full_row,
        compiler_params=params(10),
    )(keep, received, y_swap(onward), x_own, middle_grad, gain_one)

    def shared_rows(piece):
        return lax.all_to_all(piece, "fsdp", 0, 0, tiled=True)

    pair_came = after(pair_came, pieces)
    pair_came = z_shift(low_sum(pair_keep[2], pair_over[2], pair_came))
    pair_over = after(pair_over, pieces)
    pair_came = z_shift(low_sum(pair_keep[1], pair_over[1], pair_came))
    pair_piece = shared_rows(low_sum(pair_keep[0], pair_over[0], pair_came))
    down_over, _ = over_x(down_late, after(down_early, pair_over))
    qkv_piece = shared_rows(
        over_z([[qkv_keep[ahead], qkv_over[ahead]] for ahead in range(4)])
    )
    down_piece = over_z([[down_keep[ahead], down_over[ahead]] for ahead in range(4)])
    query_sum, key_sum, value_sum, gains = settle(
        settle_qkv_kernel, "settle_qkv", me, spread_piece(qkv_piece), [(rows, width)] * 3 + [(4, width)]
    )
    gate_sum, up_sum = settle(
        settle_pair_kernel, "settle_pair", me, spread_piece(pair_piece), [w_gate.shape] * 2
    )
    down_sum, out_sum = settle(
        settle_turned_kernel,
        "settle_turned",
        me,
        spread_piece(down_piece),
        [(ff_part, width), (part, width)],
    )

    return (
        block_out[None],
        in_grad[None],
        query_sum,
        key_sum,
        value_sum,
        out_sum,
        gains[0],
        gains[1],
        gate_sum,
        up_sum,
        down_sum,
        gains[2],
        gains[3],
    )


def solution(mesh):
    fsdp, ctx = mesh.shape["fsdp"], mesh.shape["ctx"]

    def step(*args):
        width, groups = args[0].shape[2], args[0].shape[0]
        heads = width // HEAD
        rows = args[0].shape[1] // ctx
        paired = (
            fsdp == 4
            and groups == fsdp
            and heads == ctx
            and CONT % rows == 0
            and (P_DEV * ctx) % rows == 0
            and width // fsdp == rows
        )
        return jax.shard_map(
            pair_shards if paired else shards,
            mesh=mesh,
            in_specs=IN_SPECS,
            out_specs=OUT_SPECS,
            check_vma=False,
        )(*args)

    return step
```
